32 devices in a mesh: groups: 2 (over y), tile: 4 (over z), pair: 2 (over x), sub: 2 (over core).
Axes of the slice: x: 2, y: 2, z: 4, core: 2. Of those that a mesh axis runs over, the one named last changes fastest.
Arguments:
- ref_chips: bfloat16 [4, 256, 4096], P(('groups', 'pair'), ('tile', 'sub')), parts along dimension 0, may hold values from -300 to 700
- search_windows: bfloat16 [4, 512, 16384], P(('groups', 'pair'), ('tile', 'sub')), parts along dimension 0, may hold values from -300 to 700
- dest_block: int32 [4, 512, 1], P(('groups', 'pair'), ('tile', 'sub')), parts along dimension 0, may hold values from 0 to 7; in each aligned block of 64 rows (0 to 63, 64 to 127, ..., all dimensions but the last counted through in order) at most 16 rows name the same one
- dest_slot: int32 [4, 512], P(('groups', 'pair'), ('tile', 'sub')), parts along dimension 0, may hold values from 0 to 31
Outputs:
- smoothed_scores: float32 [4, 256, 4096], P(('groups', 'pair'), ('tile', 'sub')), parts along dimension 0
The draws below stay inside these ranges and needn't reach their ends.
There are 2 independent parts, one for each index of `groups`. The reference program is written for one: setup_inputs(seed, part) draws one part's arguments, and reference() takes and returns one part's arrays. A program takes and returns all parts, laid end to end along the dimension named above; each array names one. Nothing has to cross between parts.
Inputs may be any that keep to these rules, and one draw needn't show every extreme that they name: `dest_block`: in the rows of one device (aligned blocks of 64 windows), no block index is named by more than 16 windows.
All inputs are finite; a program needn't handle non-finite values.
Results may differ from the reference program's by a relative error of at most 0.0003.
Values may be sent and summed in bfloat16 or wider, within the bound.
No kernel may reach another device: no remote copies, remote signals or barrier semaphores. Data moves between devices by JAX's collectives and lax.ppermute only.
A program may use at most 64 MiB of HBM per device.

```python
import math
import jax
import jax.numpy as jnp
import numpy as np
from jax import lax

CHIP = 64
WIN = 128
OFF = 64
GC = 8
W_DEV = 64
CAP = 16
CHIP_DEV = 32
NCHIP = 256
ROWS = 32
NWIN = 512
PAIRS = 2
N_TILE = 4
N_SUB = 2


def textured(key, leading, side_length):
    parts_keys = jax.random.split(key, 3)
    noise = jax.random.truncated_normal(parts_keys[0], -4.0, 4.0, leading + (side_length, side_length), jnp.float32)
    spread = math.log(10.0)
    row_scale = jnp.exp(spread * jax.random.uniform(parts_keys[1], leading + (side_length, 1), jnp.float32))
    column_scale = jnp.exp(spread * jax.random.uniform(parts_keys[2], leading + (1, side_length), jnp.float32))
    values = row_scale * column_scale * (1.0 + noise)
    return values.reshape(leading + (side_length * side_length,))


def draw_ref_chips(key, part):
    return textured(jax.random.fold_in(key, 101), (PAIRS, NCHIP), CHIP).astype(jnp.bfloat16)


def draw_search_windows(key, part):
    return textured(jax.random.fold_in(key, 202), (PAIRS, NWIN), WIN).astype(jnp.bfloat16)


def plant(values, rng, smallest, largest):
    shape = values.shape
    place = [jax.random.randint(jax.random.fold_in(rng, axis), (), 0, shape[axis]) for axis in range(len(shape))]
    values = values.at[tuple(place)].set(smallest)
    longest = shape.index(max(shape))
    place[longest] = (place[longest] + 1) % shape[longest]
    return values.at[tuple(place)].set(largest)


def deal_out(rng, own, number, rows, number_of, top, most, lean):
    order = jax.random.permutation(rng, number_of)
    crowded, usual = load_shares(number_of, rows * top, most, lean, True), load_shares(number_of, rows * top, most, lean, False)
    places = jnp.arange(number_of)

    def named(lengths, offset_by):
        used = int((lengths > 0).sum())
        fixed = max(1, used // 4)
        moved = fixed + (places - fixed + offset_by * (used - fixed)) % max(1, number_of - fixed)
        return jnp.zeros((number_of,), jnp.int32).at[order[jnp.where(places < fixed, places, moved)]].set(jnp.asarray(lengths, jnp.int32))

    lengths = jnp.where(number % 4 == 0, named(crowded, number // 4), named(usual, number - number // 4 - 1))
    mixed = jax.random.permutation(jax.random.fold_in(own, 3), number_of)
    donor, taker = mixed[0:number_of // 2 * 2:2], mixed[1:number_of // 2 * 2:2]
    slack = jnp.minimum(lengths[donor] - 1, most - lengths[taker]) // 2
    slack = jnp.where((donor == order[0]) | (taker == order[0]) | (lengths[taker] == 0), 0, jnp.maximum(slack, 0))
    moved = jax.random.randint(jax.random.fold_in(own, 4), (number_of // 2,), 0, 1 << 20) % (slack + 1)
    lengths = lengths.at[donor].add(-moved).at[taker].add(moved)
    items = jnp.searchsorted(jnp.cumsum(lengths), jnp.arange(rows * top), side="right").astype(jnp.int32)
    listing = items.reshape(top, rows).T
    listing = listing[jax.random.permutation(jax.random.fold_in(own, 1), rows)]
    offset_by = jax.random.randint(jax.random.fold_in(own, 2), (rows, 1), 0, top)
    return jnp.take_along_axis(listing, (jnp.arange(top)[None, :] + offset_by) % top, axis=1)


def load_shares(count, total, most, lean, full):
    loads = [(1 << 20) // math.isqrt(grade ** lean) + 1 for grade in range(1, count + 1)]
    largest = most if full else min(most, max(-(-total // count), total * loads[0] // sum(loads)))
    least = 1 if total - largest >= count - 1 else 0
    given, spare = [largest] + [least] * (count - 1), total - largest - least * (count - 1)
    while spare > 0:
        free = [i for i in range(1, count) if given[i] < largest] or [i for i in range(1, count) if given[i] < most]
        whole, left = sum([loads[i] for i in free]), spare
        for i in free:
            extra = min(most - given[i], max(1, left * loads[i] // whole), spare)
            given[i] = given[i] + extra
            spare = spare - extra
    return np.array(given)


def setup_inputs(seed: int = 0, part: int = 0) -> dict:
    streams_of = jax.random.split(jax.random.key(seed), 5)
    own_keys = jax.random.split(jax.random.fold_in(streams_of[4], part), 5)
    ref_chips = draw_ref_chips(jax.random.fold_in(jax.random.fold_in(streams_of[4], part), 71), part)
    search_windows = draw_search_windows(jax.random.fold_in(jax.random.fold_in(streams_of[4], part), 71), part)
    dest_block_keys = jax.random.split(jax.random.fold_in(own_keys[2], 1), PAIRS * NWIN // W_DEV)
    dest_block_turns = jax.random.permutation(jax.random.fold_in(own_keys[2], 3), PAIRS * NWIN // W_DEV)
    dest_block = jax.vmap(lambda own, number: deal_out(jax.random.fold_in(own_keys[2], 2), own, number, W_DEV, N_TILE * N_SUB, 1, CAP, 2))(dest_block_keys, dest_block_turns).reshape((PAIRS, NWIN, 1))
    dest_slot = plant(jax.random.randint(own_keys[3], (PAIRS, NWIN), 0, CHIP_DEV), jax.random.fold_in(own_keys[3], 1), 0, CHIP_DEV - 1).astype(jnp.int32)
    return dict(ref_chips=ref_chips, search_windows=search_windows, dest_block=dest_block, dest_slot=dest_slot)


def reference(ref_chips, search_windows, dest_block, dest_slot):

    def one_pair(operands):
        chips_raw, windows_raw, blocks, slots = operands
        chip_float = chips_raw.astype(jnp.float32).reshape(NCHIP, CHIP, CHIP)
        centred = chip_float - lax.optimization_barrier(jnp.mean(chip_float, axis=(1, 2), keepdims=True))
        chip_std = jnp.sqrt(lax.optimization_barrier(jnp.mean(centred * centred, axis=(1, 2))) + 1e-06)
        targets = (blocks[:, 0] * CHIP_DEV + slots).astype(jnp.int32)
        window_float = windows_raw.astype(jnp.float32).reshape(NWIN, WIN, WIN)
        padded = jnp.pad(centred[targets], ((0, 0), (0, WIN - CHIP), (0, WIN - CHIP)))
        cross = jnp.fft.irfft2(jnp.conj(jnp.fft.rfft2(padded)) * jnp.fft.rfft2(window_float), s=(WIN, WIN))
        numerator = cross[:, :OFF, :OFF]
        starts = jnp.arange(OFF, dtype=jnp.int32)[:, None]
        pixels = jnp.arange(WIN, dtype=jnp.int32)[None, :]
        window_band = ((pixels >= starts) & (pixels < starts + CHIP)).astype(jnp.float32)
        first_sum = jnp.einsum('ax,wxy,ey->wae', window_band, window_float, window_band, precision=lax.Precision.HIGHEST)
        second_sum = jnp.einsum('ax,wxy,ey->wae', window_band, window_float * window_float, window_band, precision=lax.Precision.HIGHEST)
        patch_mean = first_sum / (CHIP * CHIP)
        patch_var = second_sum / (CHIP * CHIP) - patch_mean * patch_mean
        score = numerator / (CHIP * chip_std[targets][:, None, None] * jnp.sqrt(patch_var + 1e-06))
        total = jax.ops.segment_sum(score.reshape(NWIN, OFF * OFF), targets, num_segments=NCHIP)
        looks = jax.ops.segment_sum(jnp.ones((NWIN,), jnp.float32), targets, num_segments=NCHIP)
        average = total / jnp.maximum(looks, 1.0)[:, None]
        grid = average.reshape(ROWS, GC, OFF * OFF)
        edges = jnp.pad(grid, ((1, 1), (1, 1), (0, 0)))
        smoothed = (4.0 * grid + edges[:-2, 1:-1] + edges[2:, 1:-1] + edges[1:-1, :-2] + edges[1:-1, 2:]) / 8.0
        return smoothed.reshape(NCHIP, OFF * OFF)
    return lax.map(one_pair, (ref_chips, search_windows, dest_block, dest_slot))
```

```python
import functools

import jax
import jax.numpy as jnp
import ml_dtypes
import numpy as np
from jax import lax
from jax.experimental import pallas as pl
from jax.experimental.pallas import tpu as pltpu
from jax.sharding import PartitionSpec as P

CHIP = 64
WIN = 128
GC = 8
OFF = WIN - CHIP
PERIOD = WIN - 1
HALF = WIN // 2
ROWS = OFF * OFF // WIN
GROUP = 8
CODE = 32767.0
epsilon = 1e-06
f32 = jnp.float32
bf16 = jnp.bfloat16


def split_table(table):
    high = table.astype(ml_dtypes.bfloat16)
    low = (table - high.astype(np.float64)).astype(ml_dtypes.bfloat16)
    return (high, low)


def basis():
    freqs = np.arange(HALF)[:, None]
    places = np.arange(WIN)[None, :]
    angle = (freqs * places % PERIOD) * (2.0 * np.pi / PERIOD)
    used = (places < PERIOD).astype(np.float64)
    return (np.cos(angle) * used, np.sin(angle) * used)


def interleaved(table):
    return np.concatenate([table[0::2], table[1::2]], axis=0)


def twice(block):
    zero = np.zeros_like(block)
    return np.block([[block, zero], [zero, block]])


def tables():
    cosine, sine = basis()
    forward = np.concatenate([cosine, sine], axis=0)
    high, low = split_table(forward)
    starts = np.arange(OFF)[:, None]
    places = np.arange(WIN)[None, :]
    band = ((places >= starts) & (places < starts + CHIP)).astype(ml_dtypes.bfloat16)
    rows_band = interleaved(band)
    window_rows = np.concatenate([high, low, rows_band], axis=0)
    square_rows = np.concatenate([rows_band, rows_band], axis=1)
    window_lanes = np.concatenate([high.T, low.T], axis=1)
    window_lanes = np.concatenate([window_lanes, window_lanes], axis=0)
    band_lanes = twice(band.T)

    def chip_rows_of(part):
        joined = np.concatenate([part[:, 0:CHIP:2], part[:, 1:CHIP:2]], axis=1)
        return np.concatenate([joined, joined], axis=1)

    chip_rows = np.concatenate([chip_rows_of(high), chip_rows_of(low)], axis=0)
    same = np.concatenate([cosine, cosine], axis=0)[:, :CHIP].T
    cross = np.concatenate([sine, -sine], axis=0)[:, :CHIP].T
    same_high, same_low = split_table(same)
    cross_high, cross_low = split_table(cross)
    chip_lanes = np.concatenate([same_high, cross_high, same_low, cross_low], axis=1)
    chip_lanes = np.concatenate([chip_lanes] * 4, axis=0)
    weight = np.full((2 * HALF, 1), 2.0 / PERIOD)
    weight[0] = 1.0 / PERIOD
    inverse = (forward * weight)[:, :OFF].T
    inv_high, inv_low = split_table(inverse)
    rows_high, rows_low = interleaved(inv_high), interleaved(inv_low)
    inverse_rows = np.block([[rows_high, rows_high], [rows_low, rows_low]])
    inverse_lanes = np.concatenate([twice(inv_high.T), twice(inv_low.T)], axis=1)
    inverse_lanes = np.concatenate([inverse_lanes, inverse_lanes], axis=0)
    return dict(
        window_rows=window_rows, square_rows=square_rows, window_lanes=window_lanes,
        band_lanes=band_lanes, chip_rows=chip_rows, chip_lanes=chip_lanes,
        inverse_rows=inverse_rows, inverse_lanes=inverse_lanes,
    )


def dot(left, right):
    return jnp.dot(left, right, preferred_element_type=f32)


def halves(value):
    high = value.astype(bf16)
    low = (value - high.astype(f32)).astype(bf16)
    return (high, low)


def thirds(value):
    high = value.astype(bf16)
    rest = value - high.astype(f32)
    middle = rest.astype(bf16)
    low = (rest - middle.astype(f32)).astype(bf16)
    return (high, middle, low)


def window_kernel(windows, window_rows, square_rows, window_lanes, band_lanes, spectra, scale):
    group = windows.shape[0]
    for first in range(0, group, 2):
        image = jnp.concatenate([windows[first], windows[first + 1]], axis=1)
        rows = dot(window_rows[...], image)
        spec_rows = rows[:WIN] + rows[WIN:2 * WIN]
        sums = rows[2 * WIN:]
        wide = image.astype(f32)
        square_high, square_low = halves(wide * wide)
        squares = dot(square_rows[...], jnp.concatenate([square_high, square_low], axis=0))
        for part in range(2):
            lanes = slice(part * WIN, (part + 1) * WIN)
            high, low = halves(spec_rows[:, lanes])
            both = dot(jnp.concatenate([high, low], axis=1), window_lanes[...])
            spectra[first + part] = both[:, :WIN] + both[:, WIN:]
            pieces = []
            for source in (sums, squares):
                own = source[:, lanes]
                packed = jnp.concatenate([own[:ROWS], own[ROWS:]], axis=1)
                pieces.extend(thirds(packed))
            boxed = dot(jnp.concatenate(pieces, axis=0), band_lanes[...])
            boxes = [boxed[i * ROWS:(i + 1) * ROWS] for i in range(6)]
            mean = (boxes[0] + boxes[1] + boxes[2]) * (1.0 / (CHIP * CHIP))
            second = (boxes[3] + boxes[4] + boxes[5]) * (1.0 / (CHIP * CHIP))
            variance = second - mean * mean
            scale[first + part] = lax.rsqrt(variance + epsilon)


def full_sum(value):
    return jnp.sum(jnp.sum(value, axis=0, keepdims=True), axis=1, keepdims=True)


def score_kernel(
    capacity, chip_amount, choice, place, target, ranks, slots, position,
    spectra, scale, chip_rows, chip_lanes, inverse_rows, inverse_lanes, *rest,
):
    *sources, out, marks = rest
    step = pl.program_id(0)
    group = spectra.shape[0]
    body = capacity * ROWS
    lane = lax.broadcasted_iota(jnp.int32, (8, WIN), 1)
    line = lax.broadcasted_iota(jnp.int32, (8, WIN), 0)

    @pl.when(step == 0)
    def _():
        out[...] = jnp.zeros_like(out)
        marks[...] = jnp.zeros_like(marks)

    even = lax.broadcasted_iota(jnp.int32, (ROWS, WIN), 1) < CHIP
    zero = jnp.zeros((ROWS, WIN), f32)
    for first in range(0, group, 2):
        images = []
        gains = []
        for part in range(2):
            window = step * group + first + part
            raw = sources[0][place[window]].astype(f32)
            for index in range(1, len(sources)):
                other = sources[index][place[window]].astype(f32)
                raw = jnp.where(choice[window] == index, other, raw)
            centred = raw - full_sum(raw) * (1.0 / (CHIP * CHIP))
            power = full_sum(centred * centred) * (1.0 / (CHIP * CHIP))
            gains.append(lax.rsqrt(power + epsilon) * (1.0 / CHIP))
            high = centred.astype(bf16).astype(f32)
            low = centred - high
            images.append(jnp.concatenate([
                jnp.where(even, high, zero).astype(bf16), jnp.where(even, zero, high).astype(bf16),
                jnp.where(even, low, zero).astype(bf16), jnp.where(even, zero, low).astype(bf16),
            ], axis=0))
        rows = dot(chip_rows[...], jnp.concatenate(images, axis=1))
        rows = rows[:WIN] + rows[WIN:]
        products = []
        for part in range(2):
            high, low = halves(rows[:, part * WIN:(part + 1) * WIN])
            both = dot(jnp.concatenate([high, low], axis=1), chip_lanes[...])
            both = both[:, :2 * WIN] + both[:, 2 * WIN:]
            same, cross = both[:, :WIN], both[:, WIN:]
            own = spectra[first + part]
            turned = pltpu.roll(own, HALF, 1)
            same_c, same_s = same[:HALF], same[HALF:]
            cross_c, cross_s = cross[:HALF], cross[HALF:]
            own_c, own_s = own[:HALF], own[HALF:]
            turned_c, turned_s = turned[:HALF], turned[HALF:]
            out_c = same_c * own_c + cross_c * turned_c + same_s * own_s + cross_s * turned_s
            out_s = same_c * own_s + cross_c * turned_s - same_s * own_c - cross_s * turned_c
            product = jnp.concatenate([out_c, out_s], axis=0)
            products.append(jnp.concatenate(halves(product), axis=0))
        back = dot(inverse_rows[...], jnp.concatenate(products, axis=1))
        back = back[:OFF] + back[OFF:]
        for part in range(2):
            window = step * group + first + part
            mine = back[:, part * WIN:(part + 1) * WIN]
            packed = jnp.concatenate([mine[:ROWS], mine[ROWS:]], axis=1)
            both = dot(jnp.concatenate(halves(packed), axis=1), inverse_lanes[...])
            numerator = both[:, :WIN] + both[:, WIN:]
            score = numerator * (scale[first + part] * gains[part])
            size = jnp.abs(score)
            largest = jnp.max(jnp.max(size, axis=0, keepdims=True), axis=1, keepdims=True)
            power = jnp.ceil(jnp.log2(jnp.maximum(largest, 1e-30)))
            root = jnp.sqrt(size * jnp.exp2(-power).astype(bf16).astype(f32))
            code = jnp.minimum(jnp.round(root * CODE), CODE)
            code = jnp.where(score < 0, -code, code).astype(jnp.int32).astype(jnp.int16)
            to = target[window]
            out[to, pl.ds(pl.multiple_of(ranks[window] * ROWS, ROWS), ROWS), :] = code
            here = lane == position[0] * capacity + ranks[window]
            named = (slots[window] + 1).astype(f32)
            mark = jnp.where(line == 0, named, jnp.where(line == 1, power, 0.0))
            marks[to] = marks[to] + jnp.where(here, mark, 0.0)

    @pl.when(step == pl.num_programs(0) - 1)
    def _():
        for to in range(out.shape[0]):
            notes = marks[to]
            notes = jnp.concatenate([notes, jnp.zeros_like(notes)], axis=0)
            out[to, body:, :] = notes.astype(jnp.int32).astype(jnp.int16)


def average_kernel(capacity, chip_amount, codes, smooth, first, last, values):
    devices = codes.shape[0]
    body = capacity * ROWS
    slots = devices * capacity
    notes = codes[0, body:, :].astype(jnp.int32).astype(f32)
    for source in range(1, devices):
        notes = notes + codes[source, body:, :].astype(jnp.int32).astype(f32)
    for source in range(devices):
        wide = codes[source, :body, :].astype(jnp.int32).astype(f32)
        values[source * body:(source + 1) * body, :] = wide * jnp.abs(wide)
    chip = lax.broadcasted_iota(jnp.int32, (chip_amount, WIN), 0)
    hit = (notes[0:1] - 1.0).astype(jnp.int32) == chip
    looks = jnp.sum(hit.astype(f32), axis=1, keepdims=True)
    weight = jnp.where(hit, jnp.exp2(notes[1:2]), 0.0).astype(bf16)[:, :slots]
    weight = jnp.concatenate([weight, weight], axis=1)
    factor = 1.0 / (jnp.maximum(looks, 1.0) * (CODE * CODE))
    factor = jnp.broadcast_to(factor, (chip_amount, WIN))
    column = chip % GC
    zero = jnp.zeros((GC, WIN), f32)
    for row in range(ROWS):
        high, low = halves(values[pl.ds(row, slots, stride=ROWS), :])
        average = dot(weight, jnp.concatenate([high, low], axis=0)) * factor
        lanes = slice(row * WIN, (row + 1) * WIN)
        first[:, lanes] = average[:GC]
        last[:, lanes] = average[chip_amount - GC:]
        below = jnp.concatenate([average[GC:], zero], axis=0)
        above = jnp.concatenate([zero, average[:-GC]], axis=0)
        left = jnp.where(column == 0, 0.0, pltpu.roll(average, 1, 0))
        right = jnp.where(column == GC - 1, 0.0, pltpu.roll(average, chip_amount - 1, 0))
        smooth[:, lanes] = (4.0 * average + above + below + left + right) * 0.125


def whole(array):
    return pl.BlockSpec(array.shape, lambda *_: (0,) * array.ndim)


def prepare_windows(windows, table):
    amount = windows.shape[0]
    group = min(GROUP, amount)
    images = windows.reshape(amount, WIN, WIN)
    constants = [jnp.asarray(table[k]) for k in ("window_rows", "square_rows", "window_lanes", "band_lanes")]
    return pl.pallas_call(
        window_kernel,
        grid=(amount // group,),
        in_specs=[pl.BlockSpec((group, WIN, WIN), lambda i: (i, 0, 0))] + [whole(c) for c in constants],
        out_specs=[
            pl.BlockSpec((group, WIN, WIN), lambda i: (i, 0, 0)),
            pl.BlockSpec((group, ROWS, WIN), lambda i: (i, 0, 0)),
        ],
        out_shape=[
            jax.ShapeDtypeStruct((amount, WIN, WIN), f32),
            jax.ShapeDtypeStruct((amount, ROWS, WIN), f32),
        ],
        name="window_spectra",
    )(images, *constants)


def score_windows(spectra, scale, sources, scalars, table, devices, capacity, chip_amount):
    amount = spectra.shape[0]
    group = min(GROUP, amount)
    constants = [jnp.asarray(table[k]) for k in ("chip_rows", "chip_lanes", "inverse_rows", "inverse_lanes")]
    shape = (devices, capacity * ROWS + 16, WIN)
    return pl.pallas_call(
        functools.partial(score_kernel, capacity, chip_amount),
        grid_spec=pltpu.PrefetchScalarGridSpec(
            num_scalar_prefetch=len(scalars),
            grid=(amount // group,),
            in_specs=[
                pl.BlockSpec((group, WIN, WIN), lambda i, *_: (i, 0, 0)),
                pl.BlockSpec((group, ROWS, WIN), lambda i, *_: (i, 0, 0)),
            ] + [whole(c) for c in constants] + [whole(s) for s in sources],
            out_specs=pl.BlockSpec(shape, lambda i, *_: (0, 0, 0)),
            scratch_shapes=[pltpu.VMEM((devices, 8, WIN), f32)],
        ),
        out_shape=jax.ShapeDtypeStruct(shape, jnp.int16),
        name="scores",
    )(*scalars, spectra, scale, *constants, *sources)


def average_scores(codes, capacity, chip_amount):
    devices = codes.shape[0]
    return pl.pallas_call(
        functools.partial(average_kernel, capacity, chip_amount),
        out_shape=[
            jax.ShapeDtypeStruct((chip_amount, OFF * OFF), f32),
            jax.ShapeDtypeStruct((GC, OFF * OFF), f32),
            jax.ShapeDtypeStruct((GC, OFF * OFF), f32),
        ],
        scratch_shapes=[pltpu.VMEM((devices * capacity * ROWS, WIN), f32)],
        name="average",
    )(codes)


def on_device(ref_chips, search_windows, dest_block, dest_slot):
    table = tables()
    chips = ref_chips[0]
    windows = search_windows[0]
    targets = dest_block[0, :, 0]
    slots = dest_slot[0]
    window_amount = windows.shape[0]
    chip_amount = chips.shape[0]
    tiles = lax.axis_size("tile")
    subs = lax.axis_size("sub")
    devices = tiles * subs
    capacity = max(2, 2 * window_amount // devices)

    images = chips.reshape(chip_amount, ROWS, WIN)
    sent = jnp.broadcast_to(images[None], (tiles,) + images.shape)
    gathered = lax.all_to_all(sent, "tile", split_axis=0, concat_axis=0, tiled=True)
    gathered = gathered.reshape(tiles * chip_amount, ROWS, WIN)
    sources = [gathered]
    for shift in range(1, subs):
        ring = [(i, (i - shift) % subs) for i in range(subs)]
        sources.append(lax.ppermute(gathered, "sub", ring))

    spectra, scale = prepare_windows(windows, table)

    order = jnp.arange(window_amount, dtype=jnp.int32)
    matches = targets[:, None] == targets[None, :]
    earlier = order[:, None] > order[None, :]
    ranks = jnp.sum((matches & earlier).astype(jnp.int32), axis=1)
    choice = (targets % subs - lax.axis_index("sub")) % subs
    place = (targets // subs) * chip_amount + slots
    position = jnp.full((1,), lax.axis_index(("tile", "sub")), jnp.int32)
    scalars = (choice, place, targets, ranks, slots, position)
    codes = score_windows(spectra, scale, sources, scalars, table, devices, capacity, chip_amount)

    received = lax.all_to_all(codes, ("tile", "sub"), split_axis=0, concat_axis=0, tiled=True)
    smooth, first, last = average_scores(received, capacity, chip_amount)
    forward = [(i, i + 1) for i in range(devices - 1)]
    backward = [(i + 1, i) for i in range(devices - 1)]
    above = lax.ppermute(last, ("tile", "sub"), forward)
    below = lax.ppermute(first, ("tile", "sub"), backward)
    top = smooth[:GC] + above * 0.125
    bottom = smooth[chip_amount - GC:] + below * 0.125
    result = jnp.concatenate([top, smooth[GC:chip_amount - GC], bottom], axis=0)
    return result[None]


def solution(mesh):
    return jax.shard_map(
        on_device,
        mesh=mesh,
        in_specs=(
            P(("groups", "pair"), ("tile", "sub"), None),
            P(("groups", "pair"), ("tile", "sub"), None),
            P(("groups", "pair"), ("tile", "sub"), None),
            P(("groups", "pair"), ("tile", "sub")),
        ),
        out_specs=P(("groups", "pair"), ("tile", "sub"), None),
        check_vma=False,
    )
```

```python
import functools

import jax
import jax.numpy as jnp
import ml_dtypes
import numpy as np
from jax import lax
from jax.experimental import pallas as pl
from jax.experimental.pallas import tpu as pltpu
from jax.sharding import PartitionSpec as P

CHIP = 64
WIN = 128
GC = 8
OFF = WIN - CHIP
PERIOD = WIN - 1
HALF = WIN // 2
ROWS = OFF * OFF // WIN
GROUP = 8
SCORE_GROUP = 16
CODE = 32767.0
epsilon = 1e-06
f32 = jnp.float32
bf16 = jnp.bfloat16


def split_table(table):
    high = table.astype(ml_dtypes.bfloat16)
    low = (table - high.astype(np.float64)).astype(ml_dtypes.bfloat16)
    return (high, low)


def basis():
    freqs = np.arange(HALF)[:, None]
    places = np.arange(WIN)[None, :]
    angle = (freqs * places % PERIOD) * (2.0 * np.pi / PERIOD)
    used = (places < PERIOD).astype(np.float64)
    return (np.cos(angle) * used, np.sin(angle) * used)


def interleaved(table):
    return np.concatenate([table[0::2], table[1::2]], axis=0)


def twice(block):
    zero = np.zeros_like(block)
    return np.block([[block, zero], [zero, block]])


def tables():
    cosine, sine = basis()
    forward = np.concatenate([cosine, sine], axis=0)
    high, low = split_table(forward)
    starts = np.arange(OFF)[:, None]
    places = np.arange(WIN)[None, :]
    band = ((places >= starts) & (places < starts + CHIP)).astype(ml_dtypes.bfloat16)
    rows_band = interleaved(band)
    window_rows = np.concatenate([high, low, rows_band], axis=0)
    square_rows = np.concatenate([rows_band, rows_band], axis=1)
    window_lanes = np.concatenate([high.T, low.T], axis=1)
    window_lanes = np.concatenate([window_lanes, window_lanes], axis=0)
    band_lanes = twice(band.T)

    def pair_of(part):
        return np.concatenate([part[:, 0:CHIP:2], part[:, 1:CHIP:2]], axis=1)

    chip_rows = np.concatenate([pair_of(high), pair_of(high), pair_of(low)], axis=1)
    same = np.concatenate([cosine, cosine], axis=0)[:, :CHIP].T
    cross = np.concatenate([sine, -sine], axis=0)[:, :CHIP].T
    lane_high, lane_low = split_table(twice(np.concatenate([same, cross], axis=1)))
    chip_lanes = np.concatenate([lane_high, lane_high, lane_low], axis=0)
    weight = np.full((2 * HALF, 1), 2.0 / PERIOD)
    weight[0] = 1.0 / PERIOD
    inverse = (forward * weight)[:, :OFF].T
    inv_high, inv_low = split_table(inverse)
    rows_high, rows_low = interleaved(inv_high), interleaved(inv_low)
    inverse_rows = np.block([[rows_high, rows_high], [rows_low, rows_low]])
    inverse_lanes = np.concatenate([twice(inv_high.T), twice(inv_low.T)], axis=1)
    inverse_lanes = np.concatenate([inverse_lanes, inverse_lanes], axis=0)
    return dict(
        window_rows=window_rows, square_rows=square_rows, window_lanes=window_lanes,
        band_lanes=band_lanes, chip_rows=chip_rows, chip_lanes=chip_lanes,
        inverse_rows=inverse_rows, inverse_lanes=inverse_lanes,
    )


def dot(left, right):
    return jnp.dot(left, right, preferred_element_type=f32)


def halves(value):
    high = value.astype(bf16)
    low = (value - high.astype(f32)).astype(bf16)
    return (high, low)


def thirds(value):
    high = value.astype(bf16)
    rest = value - high.astype(f32)
    middle = rest.astype(bf16)
    low = (rest - middle.astype(f32)).astype(bf16)
    return (high, middle, low)


def window_kernel(windows, window_rows, square_rows, window_lanes, band_lanes, spectra, scale):
    group = windows.shape[0]
    for first in range(0, group, 2):
        image = jnp.concatenate([windows[first], windows[first + 1]], axis=1)
        rows = dot(window_rows[...], image)
        spec_rows = rows[:WIN] + rows[WIN:2 * WIN]
        sums = rows[2 * WIN:]
        wide = image.astype(f32)
        square_high, square_low = halves(wide * wide)
        squares = dot(square_rows[...], jnp.concatenate([square_high, square_low], axis=0))
        for part in range(2):
            lanes = slice(part * WIN, (part + 1) * WIN)
            high, low = halves(spec_rows[:, lanes])
            both = dot(jnp.concatenate([high, low], axis=1), window_lanes[...])
            spectra[first + part] = both[:, :WIN] + both[:, WIN:]
            pieces = []
            for source in (sums, squares):
                own = source[:, lanes]
                packed = jnp.concatenate([own[:ROWS], own[ROWS:]], axis=1)
                pieces.extend(thirds(packed))
            boxed = dot(jnp.concatenate(pieces, axis=0), band_lanes[...])
            boxes = [boxed[i * ROWS:(i + 1) * ROWS] for i in range(6)]
            mean = (boxes[0] + boxes[1] + boxes[2]) * (1.0 / (CHIP * CHIP))
            second = (boxes[3] + boxes[4] + boxes[5]) * (1.0 / (CHIP * CHIP))
            variance = second - mean * mean
            scale[first + part] = lax.rsqrt(variance + epsilon)


def score_kernel(
    capacity, choice, place, target, ranks, slots, position,
    spectra, scale, chip_lanes, chip_rows, inverse_rows, inverse_lanes, *rest,
):
    *sources, out, marks, lefts, lines, packs, pairs, products, backs = rest
    step = pl.program_id(0)
    group = spectra.shape[0]
    body = capacity * ROWS
    lane = lax.broadcasted_iota(jnp.int32, (8, WIN), 1)
    line = lax.broadcasted_iota(jnp.int32, (8, WIN), 0)

    @pl.when(step == 0)
    def _():
        out[...] = jnp.zeros_like(out)
        marks[...] = jnp.zeros_like(marks)

    raws = []
    for part in range(group):
        window = step * group + part
        raw = sources[0][place[window]]
        for index in range(1, len(sources)):
            raw = jnp.where(choice[window] == index, sources[index][place[window]], raw)
        raws.append(raw.astype(f32))
    total = jnp.concatenate([jnp.sum(raw, axis=0, keepdims=True) for raw in raws], axis=0)
    mean = jnp.sum(total, axis=1, keepdims=True) * (1.0 / (CHIP * CHIP))
    raws = [raws[part] - mean[part:part + 1] for part in range(group)]
    total = jnp.concatenate([jnp.sum(raw * raw, axis=0, keepdims=True) for raw in raws], axis=0)
    power = jnp.sum(total, axis=1, keepdims=True) * (1.0 / (CHIP * CHIP))
    gain = lax.rsqrt(power + epsilon) * (1.0 / CHIP)
    for part in range(group):
        own = slice(part * ROWS, (part + 1) * ROWS)
        high, low = halves(raws[part])
        lefts[own, :WIN] = high
        lefts[own, WIN:2 * WIN] = low
        lefts[own, 2 * WIN:] = high
    lines[...] = dot(lefts[...], chip_lanes[...])

    def chip_spectrum(part):
        high, low = halves(lines[part * ROWS:(part + 1) * ROWS, :])
        pieces = [high[:, :2 * WIN], high[:, 2 * WIN:], low[:, :2 * WIN], low[:, 2 * WIN:]]
        pairs[part] = dot(chip_rows[...], jnp.concatenate(pieces + pieces[:2], axis=0))

    def multiply(part):
        lanes = slice(part % 2 * WIN, (part % 2 + 1) * WIN)
        for row in range(0, HALF, 32):
            upper, lower = slice(row, row + 32), slice(HALF + row, HALF + row + 32)
            own_c, own_s = spectra[part, upper], spectra[part, lower]
            turned_c, turned_s = pltpu.roll(own_c, HALF, 1), pltpu.roll(own_s, HALF, 1)
            same_c, same_s = pairs[part, upper, :WIN], pairs[part, lower, :WIN]
            cross_c, cross_s = pairs[part, upper, WIN:], pairs[part, lower, WIN:]
            out_c = same_c * own_c + cross_c * turned_c + same_s * own_s + cross_s * turned_s
            out_s = same_c * own_s + cross_c * turned_s - same_s * own_c - cross_s * turned_c
            for value, place_to in ((out_c, row), (out_s, HALF + row)):
                high, low = halves(value)
                products[part // 2, place_to:place_to + 32, lanes] = high
                products[part // 2, WIN + place_to:WIN + place_to + 32, lanes] = low

    def invert(pair):
        back = dot(inverse_rows[...], products[pair])
        backs[pair] = back[:OFF] + back[OFF:]

    def pack(pair):
        for part in (2 * pair, 2 * pair + 1):
            lanes = slice(part % 2 * WIN, (part % 2 + 1) * WIN)
            own = slice(part * ROWS, (part + 1) * ROWS)
            high, low = halves(backs[pair, :, lanes])
            packs[own, :WIN] = high[:ROWS]
            packs[own, WIN:2 * WIN] = high[ROWS:]
            packs[own, 2 * WIN:3 * WIN] = low[:ROWS]
            packs[own, 3 * WIN:] = low[ROWS:]

    for part in range(group + 4):
        if part < group:
            chip_spectrum(part)
        if 2 <= part < group + 2:
            multiply(part - 2)
            if part % 2 == 1:
                invert((part - 2) // 2)
        if part >= 4 and part % 2 == 1:
            pack((part - 4) // 2)
    both = dot(packs[...], inverse_lanes[...])
    scores = []
    for part in range(group):
        own = slice(part * ROWS, (part + 1) * ROWS)
        numerator = both[own, :WIN] + both[own, WIN:]
        scores.append(numerator * (scale[part] * gain[part:part + 1]))
    largest = jnp.concatenate([jnp.max(jnp.abs(score), axis=0, keepdims=True) for score in scores], axis=0)
    largest = jnp.max(largest, axis=1, keepdims=True)
    power = jnp.ceil(jnp.log2(jnp.maximum(largest, 1e-30)))
    shrink = jnp.exp2(-power).astype(bf16).astype(f32)
    for part in range(group):
        window = step * group + part
        score = scores[part]
        size = jnp.maximum(jnp.abs(score) * shrink[part:part + 1], 1e-30)
        root = size * lax.rsqrt(size) * CODE
        root = jnp.minimum(root, CODE)
        code = jnp.round(jnp.where(score < 0, -root, root)).astype(jnp.int32).astype(jnp.int16)
        to = target[window]
        out[to, pl.ds(pl.multiple_of(ranks[window] * ROWS, ROWS), ROWS), :] = code
        here = lane == position[0] * capacity + ranks[window]
        named = (slots[window] + 1).astype(f32)
        mark = jnp.where(line == 0, named, jnp.where(line == 1, power[part:part + 1], 0.0))
        marks[to] = marks[to] + jnp.where(here, mark, 0.0)

    @pl.when(step == pl.num_programs(0) - 1)
    def _():
        for to in range(out.shape[0]):
            notes = marks[to]
            notes = jnp.concatenate([notes, jnp.zeros_like(notes)], axis=0)
            out[to, body:, :] = notes.astype(jnp.int32).astype(jnp.int16)


def average_kernel(capacity, chip_amount, codes, smooth, first, last, values):
    devices = codes.shape[0]
    body = capacity * ROWS
    slots = devices * capacity
    notes = codes[0, body:, :].astype(jnp.int32).astype(f32)
    for source in range(1, devices):
        notes = notes + codes[source, body:, :].astype(jnp.int32).astype(f32)
    for source in range(devices):
        wide = codes[source, :body, :].astype(jnp.int32).astype(f32)
        values[source * body:(source + 1) * body, :] = wide * jnp.abs(wide)
    chip = lax.broadcasted_iota(jnp.int32, (chip_amount, WIN), 0)
    hit = (notes[0:1] - 1.0).astype(jnp.int32) == chip
    looks = jnp.sum(hit.astype(f32), axis=1, keepdims=True)
    weight = jnp.where(hit, jnp.exp2(notes[1:2]), 0.0).astype(bf16)[:, :slots]
    weight = jnp.concatenate([weight, weight], axis=1)
    factor = 1.0 / (jnp.maximum(looks, 1.0) * (CODE * CODE))
    factor = jnp.broadcast_to(factor, (chip_amount, WIN))
    column = chip % GC
    zero = jnp.zeros((GC, WIN), f32)
    for row in range(ROWS):
        high, low = halves(values[pl.ds(row, slots, stride=ROWS), :])
        average = dot(weight, jnp.concatenate([high, low], axis=0)) * factor
        lanes = slice(row * WIN, (row + 1) * WIN)
        first[:, lanes] = average[:GC]
        last[:, lanes] = average[chip_amount - GC:]
        below = jnp.concatenate([average[GC:], zero], axis=0)
        above = jnp.concatenate([zero, average[:-GC]], axis=0)
        left = jnp.where(column == 0, 0.0, pltpu.roll(average, 1, 0))
        right = jnp.where(column == GC - 1, 0.0, pltpu.roll(average, chip_amount - 1, 0))
        smooth[:, lanes] = (4.0 * average + above + below + left + right) * 0.125


def whole(array):
    return pl.BlockSpec(array.shape, lambda *_: (0,) * array.ndim)


def window_parts(amount, parts):
    groups = amount // min(GROUP, amount)
    parts = max(1, min(parts, groups))
    sizes = [groups // parts + (1 if i < groups % parts else 0) for i in range(parts)]
    return [(sum(sizes[:i]), sizes[i]) for i in range(parts)]


def continue_kernel(*refs):
    window_kernel(*refs[:5], *refs[7:])


def prepare_windows(images, table, start, count, previous):
    amount = images.shape[0]
    group = min(GROUP, amount)
    constants = [jnp.asarray(table[k]) for k in ("window_rows", "square_rows", "window_lanes", "band_lanes")]
    kept = [] if previous is None else list(previous)
    done = count * group
    return pl.pallas_call(
        window_kernel if previous is None else continue_kernel,
        grid=(count,),
        in_specs=[pl.BlockSpec((group, WIN, WIN), lambda i: (i + start, 0, 0))]
        + [whole(c) for c in constants]
        + [pl.BlockSpec(memory_space=pl.ANY) for _ in kept],
        out_specs=[
            pl.BlockSpec((group, WIN, WIN), lambda i: (i + start, 0, 0)),
            pl.BlockSpec((group, ROWS, WIN), lambda i: (i + start, 0, 0)),
        ],
        out_shape=[
            jax.ShapeDtypeStruct((amount, WIN, WIN), f32),
            jax.ShapeDtypeStruct((amount, ROWS, WIN), f32),
        ],
        input_output_aliases={5: 0, 6: 1} if kept else {},
        cost_estimate=pl.CostEstimate(
            flops=done * 2 * 900 * 65536, transcendentals=done * ROWS * WIN, bytes_accessed=done * 120000
        ),
        name="window_spectra",
    )(images, *constants, *kept)


def score_windows(spectra, scale, sources, scalars, table, devices, capacity):
    amount = spectra.shape[0]
    group = min(SCORE_GROUP, amount)
    constants = [jnp.asarray(table[k]) for k in ("chip_lanes", "chip_rows", "inverse_rows", "inverse_lanes")]
    shape = (devices, capacity * ROWS + 16, WIN)
    return pl.pallas_call(
        functools.partial(score_kernel, capacity),
        grid_spec=pltpu.PrefetchScalarGridSpec(
            num_scalar_prefetch=len(scalars),
            grid=(amount // group,),
            in_specs=[
                pl.BlockSpec((group, WIN, WIN), lambda i, *_: (i, 0, 0)),
                pl.BlockSpec((group, ROWS, WIN), lambda i, *_: (i, 0, 0)),
            ] + [whole(c) for c in constants] + [whole(s) for s in sources],
            out_specs=pl.BlockSpec(shape, lambda i, *_: (0, 0, 0)),
            scratch_shapes=[
                pltpu.VMEM((devices, 8, WIN), f32),
                pltpu.VMEM((group * ROWS, 3 * WIN), bf16),
                pltpu.VMEM((group * ROWS, 4 * WIN), f32),
                pltpu.VMEM((group * ROWS, 4 * WIN), bf16),
                pltpu.VMEM((group, WIN, 2 * WIN), f32),
                pltpu.VMEM((group // 2, 2 * WIN, 2 * WIN), bf16),
                pltpu.VMEM((group // 2, OFF, 2 * WIN), f32),
            ],
        ),
        out_shape=jax.ShapeDtypeStruct(shape, jnp.int16),
        name="scores",
    )(*scalars, spectra, scale, *constants, *sources)


def average_scores(codes, capacity, chip_amount):
    devices = codes.shape[0]
    return pl.pallas_call(
        functools.partial(average_kernel, capacity, chip_amount),
        out_shape=[
            jax.ShapeDtypeStruct((chip_amount, OFF * OFF), f32),
            jax.ShapeDtypeStruct((GC, OFF * OFF), f32),
            jax.ShapeDtypeStruct((GC, OFF * OFF), f32),
        ],
        scratch_shapes=[pltpu.VMEM((devices * capacity * ROWS, WIN), f32)],
        name="average",
    )(codes)


def on_device(ref_chips, search_windows, dest_block, dest_slot):
    table = tables()
    chips = ref_chips[0]
    windows = search_windows[0]
    targets = dest_block[0, :, 0]
    slots = dest_slot[0]
    window_amount = windows.shape[0]
    chip_amount = chips.shape[0]
    tiles = lax.axis_size("tile")
    subs = lax.axis_size("sub")
    devices = tiles * subs
    capacity = max(2, 2 * window_amount // devices)

    block = chips.reshape(chip_amount, ROWS, WIN)
    images = windows.reshape(window_amount, WIN, WIN)
    tile, sub = lax.axis_index("tile"), lax.axis_index("sub")
    parts = window_parts(window_amount, tiles - 1)
    prepared = None
    others = [[] for _ in range(1, subs)]
    own = []

    def share(pieces):
        own.extend(pieces)
        joined = pieces[0] if len(pieces) == 1 else jnp.concatenate(pieces, axis=0)
        for shift in range(1, subs):
            ring = [(i, (i - shift) % subs) for i in range(subs)]
            others[shift - 1].append(lax.ppermute(joined, "sub", ring))

    right = left = block
    fresh = [block]
    for hop in range(1, tiles):
        ahead = [(i, i + 1) for i in range(hop - 1, tiles - 1)]
        behind = [(i + 1, i) for i in range(tiles - hop)]
        if 2 * (hop - 1) >= tiles:
            right = left = lax.ppermute(right, "tile", ahead + behind)
            arrived = [right]
        else:
            right = lax.ppermute(right, "tile", ahead)
            left = lax.ppermute(left, "tile", behind)
            arrived = [right, left]
            if 2 * hop >= tiles:
                right = left = jnp.where(tile >= hop, right, left)
                arrived = [right]
        share(fresh)
        if hop <= len(parts):
            prepared = prepare_windows(images, table, *parts[hop - 1], prepared)
        fresh = arrived
    share(fresh)
    if prepared is None:
        prepared = prepare_windows(images, table, *parts[0], None)
    spectra, scale = prepared
    sources = [jnp.concatenate(own, axis=0)]
    sources.extend(jnp.concatenate(pieces, axis=0) for pieces in others)

    order = jnp.arange(window_amount, dtype=jnp.int32)
    matches = targets[:, None] == targets[None, :]
    earlier = order[:, None] > order[None, :]
    ranks = jnp.sum((matches & earlier).astype(jnp.int32), axis=1)
    choice = (targets % subs - sub) % subs
    apart = targets // subs - tile
    far = jnp.abs(apart)
    single = (tiles + 1) // 2
    arrival = jnp.where(far < single, 2 * far - (apart < 0), far + single - 1)
    place = jnp.maximum(arrival, 0) * chip_amount + slots
    position = jnp.full((1,), lax.axis_index(("tile", "sub")), jnp.int32)
    scalars = (choice, place, targets, ranks, slots, position)
    codes = score_windows(spectra, scale, sources, scalars, table, devices, capacity)

    received = lax.all_to_all(codes, ("tile", "sub"), split_axis=0, concat_axis=0, tiled=True)
    smooth, first, last = average_scores(received, capacity, chip_amount)
    forward = [(i, i + 1) for i in range(devices - 1)]
    backward = [(i + 1, i) for i in range(devices - 1)]
    above = lax.ppermute(last, ("tile", "sub"), forward)
    below = lax.ppermute(first, ("tile", "sub"), backward)
    top = smooth[:GC] + above * 0.125
    bottom = smooth[chip_amount - GC:] + below * 0.125
    result = jnp.concatenate([top, smooth[GC:chip_amount - GC], bottom], axis=0)
    return result[None]


def solution(mesh):
    return jax.shard_map(
        on_device,
        mesh=mesh,
        in_specs=(
            P(("groups", "pair"), ("tile", "sub"), None),
            P(("groups", "pair"), ("tile", "sub"), None),
            P(("groups", "pair"), ("tile", "sub"), None),
            P(("groups", "pair"), ("tile", "sub")),
        ),
        out_specs=P(("groups", "pair"), ("tile", "sub"), None),
        check_vma=False,
    )
```

```python
import functools

import jax
import jax.numpy as jnp
import ml_dtypes
import numpy as np
from jax import lax
from jax.experimental import pallas as pl
from jax.experimental.pallas import tpu as pltpu
from jax.sharding import PartitionSpec as P

CHIP = 64
WIN = 128
GC = 8
OFF = WIN - CHIP
PERIOD = WIN - 1
HALF = WIN // 2
ROWS = OFF * OFF // WIN
GROUP = 8
SCORE_GROUP = 16
VMEM_GRANT = 24 * 1024 * 1024
CODE = 32767.0
epsilon = 1e-06
f32 = jnp.float32
bf16 = jnp.bfloat16


def split_table(table):
    high = table.astype(ml_dtypes.bfloat16)
    low = (table - high.astype(np.float64)).astype(ml_dtypes.bfloat16)
    return (high, low)


def basis():
    freqs = np.arange(HALF)[:, None]
    places = np.arange(WIN)[None, :]
    angle = (freqs * places % PERIOD) * (2.0 * np.pi / PERIOD)
    used = (places < PERIOD).astype(np.float64)
    return (np.cos(angle) * used, np.sin(angle) * used)


def interleaved(table):
    return np.concatenate([table[0::2], table[1::2]], axis=0)


def twice(block):
    zero = np.zeros_like(block)
    return np.block([[block, zero], [zero, block]])


def tables():
    cosine, sine = basis()
    forward = np.concatenate([cosine, sine], axis=0)
    high, low = split_table(forward)
    starts = np.arange(OFF)[:, None]
    places = np.arange(WIN)[None, :]
    band = ((places >= starts) & (places < starts + CHIP)).astype(ml_dtypes.bfloat16)
    rows_band = interleaved(band)
    window_rows = np.concatenate([high, low, rows_band], axis=0)
    square_rows = np.concatenate([rows_band, rows_band], axis=1)
    window_lanes = np.concatenate([high.T, low.T], axis=1)
    window_lanes = np.concatenate([window_lanes, window_lanes], axis=0)
    band_lanes = twice(band.T)

    def pair_of(part):
        return np.concatenate([part[:, 0:CHIP:2], part[:, 1:CHIP:2]], axis=1)

    chip_rows = np.concatenate([pair_of(high), pair_of(high), pair_of(low)], axis=1)
    same = np.concatenate([cosine, cosine], axis=0)[:, :CHIP].T
    cross = np.concatenate([sine, -sine], axis=0)[:, :CHIP].T
    lane_high, lane_low = split_table(twice(np.concatenate([same, cross], axis=1)))
    chip_lanes = np.concatenate([lane_high, lane_high, lane_low], axis=0)
    weight = np.full((2 * HALF, 1), 2.0 / PERIOD)
    weight[0] = 1.0 / PERIOD
    inverse = (forward * weight)[:, :OFF].T
    inv_high, inv_low = split_table(inverse)
    rows_high, rows_low = interleaved(inv_high), interleaved(inv_low)
    inverse_rows = np.block([[rows_high, rows_high], [rows_low, rows_low]])
    inverse_lanes = np.concatenate([twice(inv_high.T), twice(inv_low.T)], axis=1)
    inverse_lanes = np.concatenate([inverse_lanes, inverse_lanes], axis=0)
    return dict(
        window_rows=window_rows, square_rows=square_rows, window_lanes=window_lanes,
        band_lanes=band_lanes, chip_rows=chip_rows, chip_lanes=chip_lanes,
        inverse_rows=inverse_rows, inverse_lanes=inverse_lanes,
    )


def dot(left, right):
    return jnp.dot(left, right, preferred_element_type=f32)


def halves(value):
    high = value.astype(bf16)
    low = (value - high.astype(f32)).astype(bf16)
    return (high, low)


def thirds(value):
    high = value.astype(bf16)
    rest = value - high.astype(f32)
    middle = rest.astype(bf16)
    low = (rest - middle.astype(f32)).astype(bf16)
    return (high, middle, low)


def window_kernel(windows, window_rows, square_rows, window_lanes, band_lanes, spectra, scale):
    group = windows.shape[0]
    base = pl.program_id(0) * group
    for first in range(0, group, 2):
        image = jnp.concatenate([windows[first], windows[first + 1]], axis=1)
        rows = dot(window_rows[...], image)
        spec_rows = rows[:WIN] + rows[WIN:2 * WIN]
        sums = rows[2 * WIN:]
        wide = image.astype(f32)
        square_high, square_low = halves(wide * wide)
        squares = dot(square_rows[...], jnp.concatenate([square_high, square_low], axis=0))
        for part in range(2):
            lanes = slice(part * WIN, (part + 1) * WIN)
            high, low = halves(spec_rows[:, lanes])
            both = dot(jnp.concatenate([high, low], axis=1), window_lanes[...])
            spectra[base + first + part] = both[:, :WIN] + both[:, WIN:]
            pieces = []
            for source in (sums, squares):
                own = source[:, lanes]
                packed = jnp.concatenate([own[:ROWS], own[ROWS:]], axis=1)
                pieces.extend(thirds(packed))
            boxed = dot(jnp.concatenate(pieces, axis=0), band_lanes[...])
            boxes = [boxed[i * ROWS:(i + 1) * ROWS] for i in range(6)]
            mean = (boxes[0] + boxes[1] + boxes[2]) * (1.0 / (CHIP * CHIP))
            second = (boxes[3] + boxes[4] + boxes[5]) * (1.0 / (CHIP * CHIP))
            variance = second - mean * mean
            scale[base + first + part] = lax.rsqrt(variance + epsilon)


def score_kernel(
    capacity, choice, place, target, ranks, slots, position,
    spectra, scale, chip_lanes, chip_rows, inverse_rows, inverse_lanes, *rest,
):
    *sources, out, marks, lefts, lines, packs, pairs, products, backs = rest
    step = pl.program_id(0)
    group = lefts.shape[0] // ROWS
    base = step * group
    body = capacity * ROWS
    lane = lax.broadcasted_iota(jnp.int32, (8, WIN), 1)
    line = lax.broadcasted_iota(jnp.int32, (8, WIN), 0)

    @pl.when(step == 0)
    def _():
        out[...] = jnp.zeros_like(out)
        marks[...] = jnp.zeros_like(marks)

    raws = []
    for part in range(group):
        window = base + part
        raw = sources[0][place[window]]
        for index in range(1, len(sources)):
            raw = jnp.where(choice[window] == index, sources[index][place[window]], raw)
        raws.append(raw.astype(f32))
    total = jnp.concatenate([jnp.sum(raw, axis=0, keepdims=True) for raw in raws], axis=0)
    mean = jnp.sum(total, axis=1, keepdims=True) * (1.0 / (CHIP * CHIP))
    raws = [raws[part] - mean[part:part + 1] for part in range(group)]
    total = jnp.concatenate([jnp.sum(raw * raw, axis=0, keepdims=True) for raw in raws], axis=0)
    power = jnp.sum(total, axis=1, keepdims=True) * (1.0 / (CHIP * CHIP))
    gain = lax.rsqrt(power + epsilon) * (1.0 / CHIP)
    for part in range(group):
        own = slice(part * ROWS, (part + 1) * ROWS)
        high, low = halves(raws[part])
        lefts[own, :WIN] = high
        lefts[own, WIN:2 * WIN] = low
        lefts[own, 2 * WIN:] = high
    lines[...] = dot(lefts[...], chip_lanes[...])

    def chip_spectrum(part):
        high, low = halves(lines[part * ROWS:(part + 1) * ROWS, :])
        pieces = [high[:, :2 * WIN], high[:, 2 * WIN:], low[:, :2 * WIN], low[:, 2 * WIN:]]
        pairs[part] = dot(chip_rows[...], jnp.concatenate(pieces + pieces[:2], axis=0))

    def multiply(part):
        lanes = slice(part % 2 * WIN, (part % 2 + 1) * WIN)
        for row in range(0, HALF, 32):
            upper, lower = slice(row, row + 32), slice(HALF + row, HALF + row + 32)
            own_c, own_s = spectra[base + part, upper], spectra[base + part, lower]
            turned_c, turned_s = pltpu.roll(own_c, HALF, 1), pltpu.roll(own_s, HALF, 1)
            same_c, same_s = pairs[part, upper, :WIN], pairs[part, lower, :WIN]
            cross_c, cross_s = pairs[part, upper, WIN:], pairs[part, lower, WIN:]
            out_c = same_c * own_c + cross_c * turned_c + same_s * own_s + cross_s * turned_s
            out_s = same_c * own_s + cross_c * turned_s - same_s * own_c - cross_s * turned_c
            for value, place_to in ((out_c, row), (out_s, HALF + row)):
                high, low = halves(value)
                products[part // 2, place_to:place_to + 32, lanes] = high
                products[part // 2, WIN + place_to:WIN + place_to + 32, lanes] = low

    def invert(pair):
        back = dot(inverse_rows[...], products[pair])
        backs[pair] = back[:OFF] + back[OFF:]

    def pack(pair):
        for part in (2 * pair, 2 * pair + 1):
            lanes = slice(part % 2 * WIN, (part % 2 + 1) * WIN)
            own = slice(part * ROWS, (part + 1) * ROWS)
            high, low = halves(backs[pair, :, lanes])
            packs[own, :WIN] = high[:ROWS]
            packs[own, WIN:2 * WIN] = high[ROWS:]
            packs[own, 2 * WIN:3 * WIN] = low[:ROWS]
            packs[own, 3 * WIN:] = low[ROWS:]

    for part in range(group + 4):
        if part < group:
            chip_spectrum(part)
        if 2 <= part < group + 2:
            multiply(part - 2)
            if part % 2 == 1:
                invert((part - 2) // 2)
        if part >= 4 and part % 2 == 1:
            pack((part - 4) // 2)
    both = dot(packs[...], inverse_lanes[...])
    scores = []
    for part in range(group):
        own = slice(part * ROWS, (part + 1) * ROWS)
        numerator = both[own, :WIN] + both[own, WIN:]
        scores.append(numerator * (scale[base + part] * gain[part:part + 1]))
    largest = jnp.concatenate([jnp.max(jnp.abs(score), axis=0, keepdims=True) for score in scores], axis=0)
    largest = jnp.max(largest, axis=1, keepdims=True)
    power = jnp.ceil(jnp.log2(jnp.maximum(largest, 1e-30)))
    shrink = jnp.exp2(-power).astype(bf16).astype(f32)
    for part in range(group):
        window = base + part
        score = scores[part]
        size = jnp.maximum(jnp.abs(score) * shrink[part:part + 1], 1e-30)
        root = size * lax.rsqrt(size) * CODE
        root = jnp.minimum(root, CODE)
        code = jnp.round(jnp.where(score < 0, -root, root)).astype(jnp.int32).astype(jnp.int16)
        to = target[window]
        out[to, pl.ds(pl.multiple_of(ranks[window] * ROWS, ROWS), ROWS), :] = code
        here = lane == position[0] * capacity + ranks[window]
        named = (slots[window] + 1).astype(f32)
        mark = jnp.where(line == 0, named, jnp.where(line == 1, power[part:part + 1], 0.0))
        marks[to] = marks[to] + jnp.where(here, mark, 0.0)

    @pl.when(step == pl.num_programs(0) - 1)
    def _():
        for to in range(out.shape[0]):
            notes = marks[to]
            notes = jnp.concatenate([notes, jnp.zeros_like(notes)], axis=0)
            out[to, body:, :] = notes.astype(jnp.int32).astype(jnp.int16)


def average_kernel(capacity, chip_amount, codes, smooth, first, last, values):
    devices = codes.shape[0]
    body = capacity * ROWS
    slots = devices * capacity
    notes = codes[0, body:, :].astype(jnp.int32).astype(f32)
    for source in range(1, devices):
        notes = notes + codes[source, body:, :].astype(jnp.int32).astype(f32)
    for source in range(devices):
        wide = codes[source, :body, :].astype(jnp.int32).astype(f32)
        turned = jnp.swapaxes((wide * jnp.abs(wide)).reshape(capacity, ROWS, WIN), 0, 1)
        values[:, source * capacity:(source + 1) * capacity, :] = turned
    chip = lax.broadcasted_iota(jnp.int32, (chip_amount, WIN), 0)
    hit = (notes[0:1] - 1.0).astype(jnp.int32) == chip
    looks = jnp.sum(hit.astype(f32), axis=1, keepdims=True)
    weight = jnp.where(hit, jnp.exp2(notes[1:2]), 0.0).astype(bf16)[:, :slots]
    weight = jnp.concatenate([weight, weight], axis=1)
    factor = 1.0 / (jnp.maximum(looks, 1.0) * (CODE * CODE))
    factor = jnp.broadcast_to(factor, (chip_amount, WIN))
    column = chip % GC
    zero = jnp.zeros((GC, WIN), f32)
    for row in range(ROWS):
        high, low = halves(values[row])
        average = dot(weight, jnp.concatenate([high, low], axis=0)) * factor
        lanes = slice(row * WIN, (row + 1) * WIN)
        first[:, lanes] = average[:GC]
        last[:, lanes] = average[chip_amount - GC:]
        below = jnp.concatenate([average[GC:], zero], axis=0)
        above = jnp.concatenate([zero, average[:-GC]], axis=0)
        left = jnp.where(column == 0, 0.0, pltpu.roll(average, 1, 0))
        right = jnp.where(column == GC - 1, 0.0, pltpu.roll(average, chip_amount - 1, 0))
        smooth[:, lanes] = (4.0 * average + above + below + left + right) * 0.125


def resident():
    return pl.BlockSpec(memory_space=pltpu.VMEM)


def near(array):
    return pltpu.with_memory_space_constraint(array, pltpu.VMEM)


def prepare_windows(images, table):
    amount = images.shape[0]
    group = min(GROUP, amount)
    constants = [jnp.asarray(table[k]) for k in ("window_rows", "square_rows", "window_lanes", "band_lanes")]
    return pl.pallas_call(
        window_kernel,
        grid=(amount // group,),
        in_specs=[pl.BlockSpec((group, WIN, WIN), lambda i: (i, 0, 0))] + [resident() for _ in constants],
        out_specs=[resident(), resident()],
        out_shape=[
            pltpu.VMEM((amount, WIN, WIN), f32),
            pltpu.VMEM((amount, ROWS, WIN), f32),
        ],
        cost_estimate=pl.CostEstimate(
            flops=amount * 2 * 900 * 65536, transcendentals=amount * ROWS * WIN, bytes_accessed=amount * 120000
        ),
        compiler_params=pltpu.CompilerParams(vmem_limit_bytes=VMEM_GRANT),
        name="window_spectra",
    )(images, *constants)


def score_windows(spectra, scale, sources, scalars, table, devices, capacity):
    amount = spectra.shape[0]
    group = min(SCORE_GROUP, amount)
    constants = [jnp.asarray(table[k]) for k in ("chip_lanes", "chip_rows", "inverse_rows", "inverse_lanes")]
    shape = (devices, capacity * ROWS + 16, WIN)
    return pl.pallas_call(
        functools.partial(score_kernel, capacity),
        grid_spec=pltpu.PrefetchScalarGridSpec(
            num_scalar_prefetch=len(scalars),
            grid=(amount // group,),
            in_specs=[
                resident(), resident(),
            ] + [resident() for _ in constants] + [resident() for _ in sources],
            out_specs=resident(),
            scratch_shapes=[
                pltpu.VMEM((devices, 8, WIN), f32),
                pltpu.VMEM((group * ROWS, 3 * WIN), bf16),
                pltpu.VMEM((group * ROWS, 4 * WIN), f32),
                pltpu.VMEM((group * ROWS, 4 * WIN), bf16),
                pltpu.VMEM((group, WIN, 2 * WIN), f32),
                pltpu.VMEM((group // 2, 2 * WIN, 2 * WIN), bf16),
                pltpu.VMEM((group // 2, OFF, 2 * WIN), f32),
            ],
        ),
        out_shape=pltpu.VMEM(shape, jnp.int16),
        compiler_params=pltpu.CompilerParams(vmem_limit_bytes=VMEM_GRANT),
        name="scores",
    )(*scalars, near(spectra), near(scale), *constants, *[near(source) for source in sources])


def average_scores(codes, capacity, chip_amount):
    devices = codes.shape[0]
    return pl.pallas_call(
        functools.partial(average_kernel, capacity, chip_amount),
        in_specs=[resident()],
        out_specs=[resident(), resident(), resident()],
        out_shape=[
            pltpu.VMEM((chip_amount, OFF * OFF), f32),
            pltpu.VMEM((GC, OFF * OFF), f32),
            pltpu.VMEM((GC, OFF * OFF), f32),
        ],
        scratch_shapes=[pltpu.VMEM((ROWS, devices * capacity, WIN), f32)],
        compiler_params=pltpu.CompilerParams(vmem_limit_bytes=VMEM_GRANT),
        name="average",
    )(near(codes))


def finish_kernel(turn, smooth, inner, outer, result):
    edge = smooth.shape[0] - GC
    result[...] = smooth[...]
    for row in range(ROWS):
        lanes = slice(row * WIN, (row + 1) * WIN)
        near, far = inner[:, lanes], outer[:, lanes]
        swap = turn[0] == 1
        result[:GC, lanes] = smooth[:GC, lanes] + jnp.where(swap, near, far) * 0.125
        result[edge:, lanes] = smooth[edge:, lanes] + jnp.where(swap, far, near) * 0.125


def finish(smooth, inner, outer, turn):
    return pl.pallas_call(
        finish_kernel,
        in_specs=[pl.BlockSpec(memory_space=pltpu.SMEM), resident(), resident(), resident()],
        out_shape=jax.ShapeDtypeStruct(smooth.shape, f32),
        compiler_params=pltpu.CompilerParams(vmem_limit_bytes=VMEM_GRANT),
        name="finish",
    )(jnp.full((1,), turn, jnp.int32), smooth, near(inner), near(outer))


def on_device(ref_chips, search_windows, dest_block, dest_slot):
    table = tables()
    chips = ref_chips[0]
    windows = search_windows[0]
    targets = dest_block[0, :, 0]
    slots = dest_slot[0]
    window_amount = windows.shape[0]
    chip_amount = chips.shape[0]
    tiles = lax.axis_size("tile")
    subs = lax.axis_size("sub")
    devices = tiles * subs
    capacity = max(2, 2 * window_amount // devices)

    block = chips.reshape(chip_amount, ROWS, WIN)
    images = windows.reshape(window_amount, WIN, WIN)
    sub = lax.axis_index("sub")
    sent = jnp.broadcast_to(block.reshape(1, chip_amount * ROWS, WIN), (tiles, chip_amount * ROWS, WIN))
    gathered = lax.all_to_all(sent, "tile", split_axis=0, concat_axis=0, tiled=True)
    gathered = gathered.reshape(tiles * chip_amount, ROWS, WIN)
    spectra, scale = prepare_windows(images, table)
    sources = [gathered]
    for shift in range(1, subs):
        ring = [(i, (i - shift) % subs) for i in range(subs)]
        sources.append(lax.ppermute(gathered, "sub", ring))

    order = jnp.arange(window_amount, dtype=jnp.int32)
    matches = targets[:, None] == targets[None, :]
    earlier = order[:, None] > order[None, :]
    ranks = jnp.sum((matches & earlier).astype(jnp.int32), axis=1)
    choice = (targets % subs - sub) % subs
    place = (targets // subs) * chip_amount + slots
    position = jnp.full((1,), lax.axis_index(("tile", "sub")), jnp.int32)
    scalars = (choice, place, targets, ranks, slots, position)
    codes = score_windows(spectra, scale, sources, scalars, table, devices, capacity)

    received = lax.all_to_all(codes, ("tile", "sub"), split_axis=0, concat_axis=0, tiled=True)
    smooth, first, last = average_scores(received, capacity, chip_amount)
    if subs == 2:
        inner = lax.ppermute(jnp.where(sub == 0, last, first), "sub", [(0, 1), (1, 0)])
        ups = [(2 * i + 1, 2 * i + 2) for i in range(tiles - 1)]
        downs = [(2 * i + 2, 2 * i + 1) for i in range(tiles - 1)]
        outer = lax.ppermute(jnp.where(sub == 0, first, last), ("tile", "sub"), ups + downs)
        turn = sub
    else:
        inner = lax.ppermute(first, ("tile", "sub"), [(i + 1, i) for i in range(devices - 1)])
        outer = lax.ppermute(last, ("tile", "sub"), [(i, i + 1) for i in range(devices - 1)])
        turn = 0
    return finish(smooth, inner, outer, turn)[None]


def solution(mesh):
    return jax.shard_map(
        on_device,
        mesh=mesh,
        in_specs=(
            P(("groups", "pair"), ("tile", "sub"), None),
            P(("groups", "pair"), ("tile", "sub"), None),
            P(("groups", "pair"), ("tile", "sub"), None),
            P(("groups", "pair"), ("tile", "sub")),
        ),
        out_specs=P(("groups", "pair"), ("tile", "sub"), None),
        check_vma=False,
    )
```

```python
import functools

import jax
import jax.numpy as jnp
import ml_dtypes
import numpy as np
from jax import lax
from jax.experimental import pallas as pl
from jax.experimental.pallas import tpu as pltpu
from jax.sharding import PartitionSpec as P

CHIP = 64
WIN = 128
GC = 8
OFF = WIN - CHIP
PERIOD = WIN - 1
HALF = WIN // 2
ROWS = OFF * OFF // WIN
GROUP = 8
SCORE_GROUP = 16
VMEM_GRANT = 24 * 1024 * 1024
CODE = 32767.0
epsilon = 1e-06
f32 = jnp.float32
bf16 = jnp.bfloat16


def split_table(table):
    high = table.astype(ml_dtypes.bfloat16)
    low = (table - high.astype(np.float64)).astype(ml_dtypes.bfloat16)
    return (high, low)


def basis():
    freqs = np.arange(HALF)[:, None]
    places = np.arange(WIN)[None, :]
    angle = (freqs * places % PERIOD) * (2.0 * np.pi / PERIOD)
    used = (places < PERIOD).astype(np.float64)
    return (np.cos(angle) * used, np.sin(angle) * used)


def interleaved(table):
    return np.concatenate([table[0::2], table[1::2]], axis=0)


def twice(block):
    zero = np.zeros_like(block)
    return np.block([[block, zero], [zero, block]])


def tables():
    cosine, sine = basis()
    forward = np.concatenate([cosine, sine], axis=0)
    high, low = split_table(forward)
    starts = np.arange(OFF)[:, None]
    places = np.arange(WIN)[None, :]
    band = ((places >= starts) & (places < starts + CHIP)).astype(ml_dtypes.bfloat16)
    rows_band = interleaved(band)
    window_rows = np.concatenate([high, low, rows_band], axis=0)
    square_rows = np.concatenate([rows_band, rows_band], axis=1)
    window_lanes = np.concatenate([high.T, low.T], axis=1)
    window_lanes = np.concatenate([window_lanes, window_lanes], axis=0)
    band_lanes = twice(band.T)

    def pair_of(part):
        return np.concatenate([part[:, 0:CHIP:2], part[:, 1:CHIP:2]], axis=1)

    chip_rows = np.concatenate([pair_of(high), pair_of(high), pair_of(low)], axis=1)
    same = np.concatenate([cosine, cosine], axis=0)[:, :CHIP].T
    cross = np.concatenate([sine, -sine], axis=0)[:, :CHIP].T
    lane_high, lane_low = split_table(twice(np.concatenate([same, cross], axis=1)))
    chip_lanes = np.concatenate([lane_high, lane_high, lane_low], axis=0)
    weight = np.full((2 * HALF, 1), 2.0 / PERIOD)
    weight[0] = 1.0 / PERIOD
    inverse = (forward * weight)[:, :OFF].T
    inv_high, inv_low = split_table(inverse)
    rows_high, rows_low = interleaved(inv_high), interleaved(inv_low)
    inverse_rows = np.block([[rows_high, rows_high], [rows_low, rows_low]])
    inverse_lanes = np.concatenate([twice(inv_high.T), twice(inv_low.T)], axis=1)
    inverse_lanes = np.concatenate([inverse_lanes, inverse_lanes], axis=0)
    return dict(
        window_rows=window_rows, square_rows=square_rows, window_lanes=window_lanes,
        band_lanes=band_lanes, chip_rows=chip_rows, chip_lanes=chip_lanes,
        inverse_rows=inverse_rows, inverse_lanes=inverse_lanes,
    )


def dot(left, right):
    return jnp.dot(left, right, preferred_element_type=f32)


def halves(value):
    high = value.astype(bf16)
    low = (value - high.astype(f32)).astype(bf16)
    return (high, low)


def thirds(value):
    high = value.astype(bf16)
    rest = value - high.astype(f32)
    middle = rest.astype(bf16)
    low = (rest - middle.astype(f32)).astype(bf16)
    return (high, middle, low)


def window_kernel(windows, window_rows, square_rows, window_lanes, band_lanes, spectra, scale):
    group = windows.shape[0]
    for first in range(0, group, 2):
        image = jnp.concatenate([windows[first], windows[first + 1]], axis=1)
        rows = dot(window_rows[...], image)
        spec_rows = rows[:WIN] + rows[WIN:2 * WIN]
        sums = rows[2 * WIN:]
        wide = image.astype(f32)
        square_high, square_low = halves(wide * wide)
        squares = dot(square_rows[...], jnp.concatenate([square_high, square_low], axis=0))
        for part in range(2):
            lanes = slice(part * WIN, (part + 1) * WIN)
            high, low = halves(spec_rows[:, lanes])
            both = dot(jnp.concatenate([high, low], axis=1), window_lanes[...])
            spectra[first + part] = both[:, :WIN] + both[:, WIN:]
            pieces = []
            for source in (sums, squares):
                own = source[:, lanes]
                packed = jnp.concatenate([own[:ROWS], own[ROWS:]], axis=1)
                pieces.extend(thirds(packed))
            boxed = dot(jnp.concatenate(pieces, axis=0), band_lanes[...])
            boxes = [boxed[i * ROWS:(i + 1) * ROWS] for i in range(6)]
            mean = (boxes[0] + boxes[1] + boxes[2]) * (1.0 / (CHIP * CHIP))
            second = (boxes[3] + boxes[4] + boxes[5]) * (1.0 / (CHIP * CHIP))
            variance = second - mean * mean
            scale[first + part] = lax.rsqrt(variance + epsilon)


def score_kernel(
    capacity, choice, place, target, ranks, slots, position,
    spectra, scale, chip_lanes, chip_rows, inverse_rows, inverse_lanes, *rest,
):
    *sources, out, marks, lefts, lines, packs, pairs, products, backs = rest
    step = pl.program_id(0)
    group = lefts.shape[0] // ROWS
    base = step * group
    body = capacity * ROWS
    lane = lax.broadcasted_iota(jnp.int32, (8, WIN), 1)
    line = lax.broadcasted_iota(jnp.int32, (8, WIN), 0)

    @pl.when(step == 0)
    def _():
        out[...] = jnp.zeros_like(out)
        marks[...] = jnp.zeros_like(marks)

    raws = []
    for part in range(group):
        window = base + part
        raw = sources[0][place[window]]
        for index in range(1, len(sources)):
            raw = jnp.where(choice[window] == index, sources[index][place[window]], raw)
        raws.append(raw.astype(f32))
    total = jnp.concatenate([jnp.sum(raw, axis=0, keepdims=True) for raw in raws], axis=0)
    mean = jnp.sum(total, axis=1, keepdims=True) * (1.0 / (CHIP * CHIP))
    raws = [raws[part] - mean[part:part + 1] for part in range(group)]
    total = jnp.concatenate([jnp.sum(raw * raw, axis=0, keepdims=True) for raw in raws], axis=0)
    power = jnp.sum(total, axis=1, keepdims=True) * (1.0 / (CHIP * CHIP))
    gain = lax.rsqrt(power + epsilon) * (1.0 / CHIP)
    for part in range(group):
        own = slice(part * ROWS, (part + 1) * ROWS)
        high, low = halves(raws[part])
        lefts[own, :WIN] = high
        lefts[own, WIN:2 * WIN] = low
        lefts[own, 2 * WIN:] = high
    lines[...] = dot(lefts[...], chip_lanes[...])

    def chip_spectrum(part):
        high, low = halves(lines[part * ROWS:(part + 1) * ROWS, :])
        pieces = [high[:, :2 * WIN], high[:, 2 * WIN:], low[:, :2 * WIN], low[:, 2 * WIN:]]
        pairs[part] = dot(chip_rows[...], jnp.concatenate(pieces + pieces[:2], axis=0))

    def multiply(part):
        lanes = slice(part % 2 * WIN, (part % 2 + 1) * WIN)
        for row in range(0, HALF, 32):
            upper, lower = slice(row, row + 32), slice(HALF + row, HALF + row + 32)
            own_c, own_s = spectra[part, upper], spectra[part, lower]
            turned_c, turned_s = pltpu.roll(own_c, HALF, 1), pltpu.roll(own_s, HALF, 1)
            same_c, same_s = pairs[part, upper, :WIN], pairs[part, lower, :WIN]
            cross_c, cross_s = pairs[part, upper, WIN:], pairs[part, lower, WIN:]
            out_c = same_c * own_c + cross_c * turned_c + same_s * own_s + cross_s * turned_s
            out_s = same_c * own_s + cross_c * turned_s - same_s * own_c - cross_s * turned_c
            for value, place_to in ((out_c, row), (out_s, HALF + row)):
                high, low = halves(value)
                products[part // 2, place_to:place_to + 32, lanes] = high
                products[part // 2, WIN + place_to:WIN + place_to + 32, lanes] = low

    def invert(pair):
        back = dot(inverse_rows[...], products[pair])
        backs[pair] = back[:OFF] + back[OFF:]

    def pack(pair):
        for part in (2 * pair, 2 * pair + 1):
            lanes = slice(part % 2 * WIN, (part % 2 + 1) * WIN)
            own = slice(part * ROWS, (part + 1) * ROWS)
            high, low = halves(backs[pair, :, lanes])
            packs[own, :WIN] = high[:ROWS]
            packs[own, WIN:2 * WIN] = high[ROWS:]
            packs[own, 2 * WIN:3 * WIN] = low[:ROWS]
            packs[own, 3 * WIN:] = low[ROWS:]

    for part in range(group + 4):
        if part < group:
            chip_spectrum(part)
        if 2 <= part < group + 2:
            multiply(part - 2)
            if part % 2 == 1:
                invert((part - 2) // 2)
        if part >= 4 and part % 2 == 1:
            pack((part - 4) // 2)
    both = dot(packs[...], inverse_lanes[...])
    scores = []
    for part in range(group):
        own = slice(part * ROWS, (part + 1) * ROWS)
        numerator = both[own, :WIN] + both[own, WIN:]
        scores.append(numerator * (scale[part] * gain[part:part + 1]))
    largest = jnp.concatenate([jnp.max(jnp.abs(score), axis=0, keepdims=True) for score in scores], axis=0)
    largest = jnp.max(largest, axis=1, keepdims=True)
    power = jnp.ceil(jnp.log2(jnp.maximum(largest, 1e-30)))
    shrink = jnp.exp2(-power).astype(bf16).astype(f32)
    for part in range(group):
        window = base + part
        score = scores[part]
        size = jnp.maximum(jnp.abs(score) * shrink[part:part + 1], 1e-30)
        root = size * lax.rsqrt(size) * CODE
        root = jnp.minimum(root, CODE)
        code = jnp.round(jnp.where(score < 0, -root, root)).astype(jnp.int32).astype(jnp.int16)
        to = target[window]
        out[to, pl.ds(pl.multiple_of(ranks[window] * ROWS, ROWS), ROWS), :] = code
        here = lane == position[0] * capacity + ranks[window]
        named = (slots[window] + 1).astype(f32)
        mark = jnp.where(line == 0, named, jnp.where(line == 1, power[part:part + 1], 0.0))
        marks[to] = marks[to] + jnp.where(here, mark, 0.0)

    @pl.when(step == pl.num_programs(0) - 1)
    def _():
        for to in range(out.shape[0]):
            notes = marks[to]
            notes = jnp.concatenate([notes, jnp.zeros_like(notes)], axis=0)
            out[to, body:, :] = notes.astype(jnp.int32).astype(jnp.int16)


def average_kernel(capacity, chip_amount, codes, smooth, first, last, values):
    devices = codes.shape[0]
    body = capacity * ROWS
    slots = devices * capacity
    notes = codes[0, body:, :].astype(jnp.int32).astype(f32)
    for source in range(1, devices):
        notes = notes + codes[source, body:, :].astype(jnp.int32).astype(f32)
    for source in range(devices):
        wide = codes[source, :body, :].astype(jnp.int32).astype(f32)
        turned = jnp.swapaxes((wide * jnp.abs(wide)).reshape(capacity, ROWS, WIN), 0, 1)
        values[:, source * capacity:(source + 1) * capacity, :] = turned
    chip = lax.broadcasted_iota(jnp.int32, (chip_amount, WIN), 0)
    hit = (notes[0:1] - 1.0).astype(jnp.int32) == chip
    looks = jnp.sum(hit.astype(f32), axis=1, keepdims=True)
    weight = jnp.where(hit, jnp.exp2(notes[1:2]), 0.0).astype(bf16)[:, :slots]
    weight = jnp.concatenate([weight, weight], axis=1)
    factor = 1.0 / (jnp.maximum(looks, 1.0) * (CODE * CODE))
    factor = jnp.broadcast_to(factor, (chip_amount, WIN))
    column = chip % GC
    zero = jnp.zeros((GC, WIN), f32)
    for row in range(ROWS):
        high, low = halves(values[row])
        average = dot(weight, jnp.concatenate([high, low], axis=0)) * factor
        lanes = slice(row * WIN, (row + 1) * WIN)
        first[:, lanes] = average[:GC]
        last[:, lanes] = average[chip_amount - GC:]
        below = jnp.concatenate([average[GC:], zero], axis=0)
        above = jnp.concatenate([zero, average[:-GC]], axis=0)
        left = jnp.where(column == 0, 0.0, pltpu.roll(average, 1, 0))
        right = jnp.where(column == GC - 1, 0.0, pltpu.roll(average, chip_amount - 1, 0))
        smooth[:, lanes] = (4.0 * average + above + below + left + right) * 0.125


def resident():
    return pl.BlockSpec(memory_space=pltpu.VMEM)


def away(array):
    return pltpu.with_memory_space_constraint(array, pltpu.HBM)


def near(array):
    return pltpu.with_memory_space_constraint(array, pltpu.VMEM)


def spread_kernel(chips, sent):
    chip_amount = chips.shape[0]
    for first in range(0, chip_amount, 8):
        for row in range(0, ROWS, 8):
            lanes = [chips[first:first + 8, (row + i) * WIN:(row + i + 1) * WIN].astype(f32) for i in range(8)]
            turned = jnp.swapaxes(jnp.stack(lanes, axis=0), 0, 1).astype(bf16)
            for to in range(sent.shape[0]):
                sent[to, first:first + 8, row:row + 8, :] = turned


def spread(chips, tiles):
    return pl.pallas_call(
        spread_kernel,
        in_specs=[resident()],
        out_specs=resident(),
        out_shape=pltpu.VMEM((tiles, chips.shape[0], ROWS, WIN), bf16),
        compiler_params=pltpu.CompilerParams(vmem_limit_bytes=VMEM_GRANT),
        name="spread",
    )(chips)


def prepare_windows(images, table):
    amount = images.shape[0]
    group = min(GROUP, amount)
    constants = [jnp.asarray(table[k]) for k in ("window_rows", "square_rows", "window_lanes", "band_lanes")]
    return pl.pallas_call(
        window_kernel,
        grid=(amount // group,),
        in_specs=[pl.BlockSpec((group, WIN, WIN), lambda i: (i, 0, 0))] + [resident() for _ in constants],
        out_specs=[
            pl.BlockSpec((group, WIN, WIN), lambda i: (i, 0, 0)),
            pl.BlockSpec((group, ROWS, WIN), lambda i: (i, 0, 0)),
        ],
        out_shape=[
            pltpu.HBM((amount, WIN, WIN), f32),
            pltpu.HBM((amount, ROWS, WIN), f32),
        ],
        cost_estimate=pl.CostEstimate(
            flops=amount * 2 * 900 * 65536, transcendentals=amount * ROWS * WIN, bytes_accessed=amount * 120000
        ),
        compiler_params=pltpu.CompilerParams(vmem_limit_bytes=VMEM_GRANT),
        name="window_spectra",
    )(images, *constants)


def score_windows(spectra, scale, sources, scalars, table, devices, capacity):
    amount = spectra.shape[0]
    group = min(SCORE_GROUP, amount)
    constants = [jnp.asarray(table[k]) for k in ("chip_lanes", "chip_rows", "inverse_rows", "inverse_lanes")]
    shape = (devices, capacity * ROWS + 16, WIN)
    return pl.pallas_call(
        functools.partial(score_kernel, capacity),
        grid_spec=pltpu.PrefetchScalarGridSpec(
            num_scalar_prefetch=len(scalars),
            grid=(amount // group,),
            in_specs=[
                pl.BlockSpec((group, WIN, WIN), lambda i, *_: (i, 0, 0)),
                pl.BlockSpec((group, ROWS, WIN), lambda i, *_: (i, 0, 0)),
            ] + [resident() for _ in constants] + [resident() for _ in sources],
            out_specs=resident(),
            scratch_shapes=[
                pltpu.VMEM((devices, 8, WIN), f32),
                pltpu.VMEM((group * ROWS, 3 * WIN), bf16),
                pltpu.VMEM((group * ROWS, 4 * WIN), f32),
                pltpu.VMEM((group * ROWS, 4 * WIN), bf16),
                pltpu.VMEM((group, WIN, 2 * WIN), f32),
                pltpu.VMEM((group // 2, 2 * WIN, 2 * WIN), bf16),
                pltpu.VMEM((group // 2, OFF, 2 * WIN), f32),
            ],
        ),
        out_shape=pltpu.VMEM(shape, jnp.int16),
        compiler_params=pltpu.CompilerParams(vmem_limit_bytes=VMEM_GRANT),
        name="scores",
    )(*scalars, away(spectra), away(scale), *[away(c) for c in constants], *[near(source) for source in sources])


def average_scores(codes, capacity, chip_amount):
    devices = codes.shape[0]
    return pl.pallas_call(
        functools.partial(average_kernel, capacity, chip_amount),
        in_specs=[resident()],
        out_specs=[resident(), resident(), resident()],
        out_shape=[
            pltpu.VMEM((chip_amount, OFF * OFF), f32),
            pltpu.VMEM((GC, OFF * OFF), f32),
            pltpu.VMEM((GC, OFF * OFF), f32),
        ],
        scratch_shapes=[pltpu.VMEM((ROWS, devices * capacity, WIN), f32)],
        compiler_params=pltpu.CompilerParams(vmem_limit_bytes=VMEM_GRANT),
        name="average",
    )(near(codes))


def finish_kernel(turn, smooth, inner, outer, result):
    edge = smooth.shape[0] - GC
    result[...] = smooth[...]
    for row in range(ROWS):
        lanes = slice(row * WIN, (row + 1) * WIN)
        near, far = inner[:, lanes], outer[:, lanes]
        swap = turn[0] == 1
        result[:GC, lanes] = smooth[:GC, lanes] + jnp.where(swap, near, far) * 0.125
        result[edge:, lanes] = smooth[edge:, lanes] + jnp.where(swap, far, near) * 0.125


def finish(smooth, inner, outer, turn):
    return pl.pallas_call(
        finish_kernel,
        in_specs=[pl.BlockSpec(memory_space=pltpu.SMEM), resident(), resident(), resident()],
        out_shape=jax.ShapeDtypeStruct(smooth.shape, f32),
        compiler_params=pltpu.CompilerParams(vmem_limit_bytes=VMEM_GRANT),
        name="finish",
    )(jnp.full((1,), turn, jnp.int32), smooth, near(inner), near(outer))


def on_device(ref_chips, search_windows, dest_block, dest_slot):
    table = tables()
    chips = ref_chips[0]
    windows = search_windows[0]
    targets = dest_block[0, :, 0]
    slots = dest_slot[0]
    window_amount = windows.shape[0]
    chip_amount = chips.shape[0]
    tiles = lax.axis_size("tile")
    subs = lax.axis_size("sub")
    devices = tiles * subs
    capacity = max(2, 2 * window_amount // devices)

    images = windows.reshape(window_amount, WIN, WIN)
    sub = lax.axis_index("sub")
    sent = spread(chips, tiles).reshape(tiles, chip_amount * ROWS, WIN)
    gathered = lax.all_to_all(sent, "tile", split_axis=0, concat_axis=0, tiled=True)
    gathered = gathered.reshape(tiles * chip_amount, ROWS, WIN)
    spectra, scale = prepare_windows(images, table)
    sources = [gathered]
    for shift in range(1, subs):
        ring = [(i, (i - shift) % subs) for i in range(subs)]
        sources.append(lax.ppermute(gathered, "sub", ring))

    order = jnp.arange(window_amount, dtype=jnp.int32)
    matches = targets[:, None] == targets[None, :]
    earlier = order[:, None] > order[None, :]
    ranks = jnp.sum((matches & earlier).astype(jnp.int32), axis=1)
    choice = (targets % subs - sub) % subs
    place = (targets // subs) * chip_amount + slots
    position = jnp.full((1,), lax.axis_index(("tile", "sub")), jnp.int32)
    scalars = (choice, place, targets, ranks, slots, position)
    codes = score_windows(spectra, scale, sources, scalars, table, devices, capacity)

    received = lax.all_to_all(codes, ("tile", "sub"), split_axis=0, concat_axis=0, tiled=True)
    smooth, first, last = average_scores(received, capacity, chip_amount)
    if subs == 2:
        inner = lax.ppermute(jnp.where(sub == 0, last, first), "sub", [(0, 1), (1, 0)])
        ups = [(2 * i + 1, 2 * i + 2) for i in range(tiles - 1)]
        downs = [(2 * i + 2, 2 * i + 1) for i in range(tiles - 1)]
        outer = lax.ppermute(jnp.where(sub == 0, first, last), ("tile", "sub"), ups + downs)
        turn = sub
    else:
        inner = lax.ppermute(first, ("tile", "sub"), [(i + 1, i) for i in range(devices - 1)])
        outer = lax.ppermute(last, ("tile", "sub"), [(i, i + 1) for i in range(devices - 1)])
        turn = 0
    return finish(smooth, inner, outer, turn)[None]


def solution(mesh):
    return jax.shard_map(
        on_device,
        mesh=mesh,
        in_specs=(
            P(("groups", "pair"), ("tile", "sub"), None),
            P(("groups", "pair"), ("tile", "sub"), None),
            P(("groups", "pair"), ("tile", "sub"), None),
            P(("groups", "pair"), ("tile", "sub")),
        ),
        out_specs=P(("groups", "pair"), ("tile", "sub"), None),
        check_vma=False,
    )
```

```python
import functools

import jax
import jax.numpy as jnp
import ml_dtypes
import numpy as np
from jax import lax
from jax.experimental import pallas as pl
from jax.experimental.pallas import tpu as pltpu
from jax.sharding import PartitionSpec as P

CHIP = 64
WIN = 128
GC = 8
OFF = WIN - CHIP
PERIOD = WIN - 1
HALF = WIN // 2
ROWS = OFF * OFF // WIN
GROUP = 8
SCORE_GROUP = 16
VMEM_GRANT = 24 * 1024 * 1024
CODE = 32767.0
epsilon = 1e-06
f32 = jnp.float32
bf16 = jnp.bfloat16


def split_table(table):
    high = table.astype(ml_dtypes.bfloat16)
    low = (table - high.astype(np.float64)).astype(ml_dtypes.bfloat16)
    return (high, low)


def basis():
    freqs = np.arange(HALF)[:, None]
    places = np.arange(WIN)[None, :]
    angle = (freqs * places % PERIOD) * (2.0 * np.pi / PERIOD)
    used = (places < PERIOD).astype(np.float64)
    return (np.cos(angle) * used, np.sin(angle) * used)


def interleaved(table):
    return np.concatenate([table[0::2], table[1::2]], axis=0)


def twice(block):
    zero = np.zeros_like(block)
    return np.block([[block, zero], [zero, block]])


def tables():
    cosine, sine = basis()
    forward = np.concatenate([cosine, sine], axis=0)
    high, low = split_table(forward)
    starts = np.arange(OFF)[:, None]
    places = np.arange(WIN)[None, :]
    band = ((places >= starts) & (places < starts + CHIP)).astype(ml_dtypes.bfloat16)
    rows_band = interleaved(band)
    window_rows = np.concatenate([high, low, rows_band], axis=0)
    square_rows = np.concatenate([rows_band, rows_band], axis=1)
    window_lanes = np.concatenate([high.T, low.T], axis=1)
    window_lanes = np.concatenate([window_lanes, window_lanes], axis=0)
    band_lanes = twice(band.T)

    def pair_of(part):
        return np.concatenate([part[:, 0:CHIP:2], part[:, 1:CHIP:2]], axis=1)

    chip_rows = np.concatenate([pair_of(high), pair_of(high), pair_of(low)], axis=1)
    same = np.concatenate([cosine, cosine], axis=0)[:, :CHIP].T
    cross = np.concatenate([sine, -sine], axis=0)[:, :CHIP].T
    lane_high, lane_low = split_table(twice(np.concatenate([same, cross], axis=1)))
    chip_lanes = np.concatenate([lane_high, lane_high, lane_low], axis=0)
    weight = np.full((2 * HALF, 1), 2.0 / PERIOD)
    weight[0] = 1.0 / PERIOD
    inverse = (forward * weight)[:, :OFF].T
    inv_high, inv_low = split_table(inverse)
    rows_high, rows_low = interleaved(inv_high), interleaved(inv_low)
    inverse_rows = np.block([[rows_high, rows_high], [rows_low, rows_low]])
    inverse_lanes = np.concatenate([twice(inv_high.T), twice(inv_low.T)], axis=1)
    inverse_lanes = np.concatenate([inverse_lanes, inverse_lanes], axis=0)
    return dict(
        window_rows=window_rows, square_rows=square_rows, window_lanes=window_lanes,
        band_lanes=band_lanes, chip_rows=chip_rows, chip_lanes=chip_lanes,
        inverse_rows=inverse_rows, inverse_lanes=inverse_lanes,
    )


def dot(left, right):
    return jnp.dot(left, right, preferred_element_type=f32)


def halves(value):
    high = value.astype(bf16)
    low = (value - high.astype(f32)).astype(bf16)
    return (high, low)


def thirds(value):
    high = value.astype(bf16)
    rest = value - high.astype(f32)
    middle = rest.astype(bf16)
    low = (rest - middle.astype(f32)).astype(bf16)
    return (high, middle, low)


def window_kernel(order, windows, window_rows, square_rows, window_lanes, band_lanes, spectra, scale):
    group = spectra.shape[0]
    base = pl.program_id(0) * group
    for first in range(0, group, 2):
        image = jnp.concatenate([windows[order[base + first]], windows[order[base + first + 1]]], axis=1)
        rows = dot(window_rows[...], image)
        spec_rows = rows[:WIN] + rows[WIN:2 * WIN]
        sums = rows[2 * WIN:]
        wide = image.astype(f32)
        square_high, square_low = halves(wide * wide)
        squares = dot(square_rows[...], jnp.concatenate([square_high, square_low], axis=0))
        for part in range(2):
            lanes = slice(part * WIN, (part + 1) * WIN)
            high, low = halves(spec_rows[:, lanes])
            both = dot(jnp.concatenate([high, low], axis=1), window_lanes[...])
            spectra[first + part] = both[:, :WIN] + both[:, WIN:]
            pieces = []
            for source in (sums, squares):
                own = source[:, lanes]
                packed = jnp.concatenate([own[:ROWS], own[ROWS:]], axis=1)
                pieces.extend(thirds(packed))
            boxed = dot(jnp.concatenate(pieces, axis=0), band_lanes[...])
            boxes = [boxed[i * ROWS:(i + 1) * ROWS] for i in range(6)]
            mean = (boxes[0] + boxes[1] + boxes[2]) * (1.0 / (CHIP * CHIP))
            second = (boxes[3] + boxes[4] + boxes[5]) * (1.0 / (CHIP * CHIP))
            variance = second - mean * mean
            scale[first + part] = lax.rsqrt(variance + epsilon)


def score_kernel(capacity, subs, opening, closing, *refs):
    (choice, spots, target, ranks, slots, position, limits,
     spectra, scale, chip_lanes, chip_rows, inverse_rows, inverse_lanes, *rest) = refs
    *sources, out, marks, lefts, lines, packs, pairs, products, backs = rest
    step = pl.program_id(0)
    kept = () if opening else sources[-2:]
    sources = sources if opening else sources[:-2]

    @pl.when(step == 0)
    def _():
        out[...] = jnp.zeros_like(out) if opening else kept[0][...]
        marks[...] = jnp.zeros_like(marks) if opening else kept[1][...]

    @pl.when((step >= limits[0]) & (step < limits[1]))
    def _():
        score_group(
            capacity, subs, step, choice, spots, target, ranks, slots, position, spectra, scale,
            chip_lanes, chip_rows, inverse_rows, inverse_lanes, sources,
            out, marks, lefts, lines, packs, pairs, products, backs,
        )

    if closing:
        @pl.when(step == pl.num_programs(0) - 1)
        def _():
            for to in range(out.shape[0]):
                notes = marks[to]
                notes = jnp.concatenate([notes, jnp.zeros_like(notes)], axis=0)
                out[to, capacity * ROWS:, :] = notes.astype(jnp.int32).astype(jnp.int16)


def score_group(
    capacity, subs, step, choice, spots, target, ranks, slots, position, spectra, scale,
    chip_lanes, chip_rows, inverse_rows, inverse_lanes, sources,
    out, marks, lefts, lines, packs, pairs, products, backs,
):
    group = lefts.shape[0] // ROWS
    base = step * group
    lane = lax.broadcasted_iota(jnp.int32, (8, WIN), 1)
    line = lax.broadcasted_iota(jnp.int32, (8, WIN), 0)
    raws = []
    for part in range(group):
        window = base + part
        raw = sources[0][spots[0, window]]
        for index in range(1, len(sources)):
            raw = jnp.where(choice[window] == index, sources[index][spots[index // subs, window]], raw)
        raws.append(raw.astype(f32))
    total = jnp.concatenate([jnp.sum(raw, axis=0, keepdims=True) for raw in raws], axis=0)
    mean = jnp.sum(total, axis=1, keepdims=True) * (1.0 / (CHIP * CHIP))
    raws = [raws[part] - mean[part:part + 1] for part in range(group)]
    total = jnp.concatenate([jnp.sum(raw * raw, axis=0, keepdims=True) for raw in raws], axis=0)
    power = jnp.sum(total, axis=1, keepdims=True) * (1.0 / (CHIP * CHIP))
    gain = lax.rsqrt(power + epsilon) * (1.0 / CHIP)
    for part in range(group):
        own = slice(part * ROWS, (part + 1) * ROWS)
        high, low = halves(raws[part])
        lefts[own, :WIN] = high
        lefts[own, WIN:2 * WIN] = low
        lefts[own, 2 * WIN:] = high
    lines[...] = dot(lefts[...], chip_lanes[...])

    def chip_spectrum(part):
        high, low = halves(lines[part * ROWS:(part + 1) * ROWS, :])
        pieces = [high[:, :2 * WIN], high[:, 2 * WIN:], low[:, :2 * WIN], low[:, 2 * WIN:]]
        pairs[part] = dot(chip_rows[...], jnp.concatenate(pieces + pieces[:2], axis=0))

    def multiply(part):
        lanes = slice(part % 2 * WIN, (part % 2 + 1) * WIN)
        for row in range(0, HALF, 32):
            upper, lower = slice(row, row + 32), slice(HALF + row, HALF + row + 32)
            own_c, own_s = spectra[part, upper], spectra[part, lower]
            turned_c, turned_s = pltpu.roll(own_c, HALF, 1), pltpu.roll(own_s, HALF, 1)
            same_c, same_s = pairs[part, upper, :WIN], pairs[part, lower, :WIN]
            cross_c, cross_s = pairs[part, upper, WIN:], pairs[part, lower, WIN:]
            out_c = same_c * own_c + cross_c * turned_c + same_s * own_s + cross_s * turned_s
            out_s = same_c * own_s + cross_c * turned_s - same_s * own_c - cross_s * turned_c
            for value, place_to in ((out_c, row), (out_s, HALF + row)):
                high, low = halves(value)
                products[part // 2, place_to:place_to + 32, lanes] = high
                products[part // 2, WIN + place_to:WIN + place_to + 32, lanes] = low

    def invert(pair):
        back = dot(inverse_rows[...], products[pair])
        backs[pair] = back[:OFF] + back[OFF:]

    def pack(pair):
        for part in (2 * pair, 2 * pair + 1):
            lanes = slice(part % 2 * WIN, (part % 2 + 1) * WIN)
            own = slice(part * ROWS, (part + 1) * ROWS)
            high, low = halves(backs[pair, :, lanes])
            packs[own, :WIN] = high[:ROWS]
            packs[own, WIN:2 * WIN] = high[ROWS:]
            packs[own, 2 * WIN:3 * WIN] = low[:ROWS]
            packs[own, 3 * WIN:] = low[ROWS:]

    for part in range(group + 4):
        if part < group:
            chip_spectrum(part)
        if 2 <= part < group + 2:
            multiply(part - 2)
            if part % 2 == 1:
                invert((part - 2) // 2)
        if part >= 4 and part % 2 == 1:
            pack((part - 4) // 2)
    both = dot(packs[...], inverse_lanes[...])
    scores = []
    for part in range(group):
        own = slice(part * ROWS, (part + 1) * ROWS)
        numerator = both[own, :WIN] + both[own, WIN:]
        scores.append(numerator * (scale[part] * gain[part:part + 1]))
    largest = jnp.concatenate([jnp.max(jnp.abs(score), axis=0, keepdims=True) for score in scores], axis=0)
    largest = jnp.max(largest, axis=1, keepdims=True)
    power = jnp.ceil(jnp.log2(jnp.maximum(largest, 1e-30)))
    shrink = jnp.exp2(-power).astype(bf16).astype(f32)
    for part in range(group):
        window = base + part
        score = scores[part]
        size = jnp.maximum(jnp.abs(score) * shrink[part:part + 1], 1e-30)
        root = size * lax.rsqrt(size) * CODE
        root = jnp.minimum(root, CODE)
        code = jnp.round(jnp.where(score < 0, -root, root)).astype(jnp.int32).astype(jnp.int16)
        to = target[window]
        out[to, pl.ds(pl.multiple_of(ranks[window] * ROWS, ROWS), ROWS), :] = code
        here = lane == position[0] * capacity + ranks[window]
        named = (slots[window] + 1).astype(f32)
        mark = jnp.where(line == 0, named, jnp.where(line == 1, power[part:part + 1], 0.0))
        marks[to] = jnp.where(here & (line < 2), mark, marks[to])


def average_kernel(capacity, chip_amount, codes, smooth, first, last, values):
    devices = codes.shape[0]
    body = capacity * ROWS
    slots = devices * capacity
    notes = codes[0, body:, :].astype(jnp.int32).astype(f32)
    for source in range(1, devices):
        notes = notes + codes[source, body:, :].astype(jnp.int32).astype(f32)
    for source in range(devices):
        wide = codes[source, :body, :].astype(jnp.int32).astype(f32)
        turned = jnp.swapaxes((wide * jnp.abs(wide)).reshape(capacity, ROWS, WIN), 0, 1)
        values[:, source * capacity:(source + 1) * capacity, :] = turned
    chip = lax.broadcasted_iota(jnp.int32, (chip_amount, WIN), 0)
    hit = (notes[0:1] - 1.0).astype(jnp.int32) == chip
    looks = jnp.sum(hit.astype(f32), axis=1, keepdims=True)
    weight = jnp.where(hit, jnp.exp2(notes[1:2]), 0.0).astype(bf16)[:, :slots]
    weight = jnp.concatenate([weight, weight], axis=1)
    factor = 1.0 / (jnp.maximum(looks, 1.0) * (CODE * CODE))
    factor = jnp.broadcast_to(factor, (chip_amount, WIN))
    column = chip % GC
    zero = jnp.zeros((GC, WIN), f32)
    for row in range(ROWS):
        high, low = halves(values[row])
        average = dot(weight, jnp.concatenate([high, low], axis=0)) * factor
        lanes = slice(row * WIN, (row + 1) * WIN)
        first[:, lanes] = average[:GC]
        last[:, lanes] = average[chip_amount - GC:]
        below = jnp.concatenate([average[GC:], zero], axis=0)
        above = jnp.concatenate([zero, average[:-GC]], axis=0)
        left = jnp.where(column == 0, 0.0, pltpu.roll(average, 1, 0))
        right = jnp.where(column == GC - 1, 0.0, pltpu.roll(average, chip_amount - 1, 0))
        smooth[:, lanes] = (4.0 * average + above + below + left + right) * 0.125


def resident():
    return pl.BlockSpec(memory_space=pltpu.VMEM)


def away(array):
    return pltpu.with_memory_space_constraint(array, pltpu.HBM)


def near(array):
    return pltpu.with_memory_space_constraint(array, pltpu.VMEM)


def spread_kernel(chips, *parts):
    for first in range(0, chips.shape[0], 8):
        for row in range(0, ROWS, 8):
            lanes = [chips[first:first + 8, (row + i) * WIN:(row + i + 1) * WIN].astype(f32) for i in range(8)]
            turned = jnp.swapaxes(jnp.stack(lanes, axis=0), 0, 1).astype(bf16)
            own = first - parts[0].shape[1]
            if own >= 0:
                parts[1][own:own + 8, row:row + 8, :] = turned
            else:
                for to in range(parts[0].shape[0]):
                    parts[0][to, first:first + 8, row:row + 8, :] = turned


def spread(chips, tiles, cut):
    shapes = [(tiles, cut, ROWS, WIN), (chips.shape[0] - cut, ROWS, WIN)]
    return pl.pallas_call(
        spread_kernel,
        in_specs=[resident()],
        out_specs=[resident(), resident()],
        out_shape=[pltpu.VMEM(shape, bf16) for shape in shapes],
        compiler_params=pltpu.CompilerParams(vmem_limit_bytes=VMEM_GRANT),
        name="spread",
    )(chips)


def prepare_windows(images, order, table):
    amount = images.shape[0]
    group = min(GROUP, amount)
    constants = [jnp.asarray(table[k]) for k in ("window_rows", "square_rows", "window_lanes", "band_lanes")]
    return pl.pallas_call(
        window_kernel,
        grid_spec=pltpu.PrefetchScalarGridSpec(
            num_scalar_prefetch=1,
            grid=(amount // group,),
            in_specs=[resident()] + [resident() for _ in constants],
            out_specs=[
                pl.BlockSpec((group, WIN, WIN), lambda i, _: (i, 0, 0)),
                pl.BlockSpec((group, ROWS, WIN), lambda i, _: (i, 0, 0)),
            ],
        ),
        out_shape=[
            pltpu.HBM((amount, WIN, WIN), f32),
            pltpu.HBM((amount, ROWS, WIN), f32),
        ],
        cost_estimate=pl.CostEstimate(
            flops=amount * 2 * 900 * 65536, transcendentals=amount * ROWS * WIN, bytes_accessed=amount * 120000
        ),
        compiler_params=pltpu.CompilerParams(vmem_limit_bytes=VMEM_GRANT),
        name="window_spectra",
    )(order, near(images), *constants)


def score_windows(spectra, scale, sources, scalars, table, devices, capacity, subs, earlier, closing):
    amount = spectra.shape[0]
    group = min(SCORE_GROUP, amount)
    constants = [jnp.asarray(table[k]) for k in ("chip_lanes", "chip_rows", "inverse_rows", "inverse_lanes")]
    shapes = [(devices, capacity * ROWS + 16, WIN), (devices, 8, WIN)]
    count = len(scalars)
    kept = [] if earlier is None else [near(e) for e in earlier]
    steps = amount // group

    def block(i, *prefetched):
        limits = prefetched[-1]
        return (jnp.clip(i, jnp.minimum(limits[0], steps - 1), jnp.maximum(limits[1] - 1, 0)), 0, 0)

    return pl.pallas_call(
        functools.partial(score_kernel, capacity, subs, earlier is None, closing),
        grid_spec=pltpu.PrefetchScalarGridSpec(
            num_scalar_prefetch=count,
            grid=(steps,),
            in_specs=[pl.BlockSpec((group, WIN, WIN), block), pl.BlockSpec((group, ROWS, WIN), block)]
            + [resident() for _ in constants] + [resident() for _ in sources] + [resident() for _ in kept],
            out_specs=[resident(), resident()],
            scratch_shapes=[
                pltpu.VMEM((group * ROWS, 3 * WIN), bf16),
                pltpu.VMEM((group * ROWS, 4 * WIN), f32),
                pltpu.VMEM((group * ROWS, 4 * WIN), bf16),
                pltpu.VMEM((group, WIN, 2 * WIN), f32),
                pltpu.VMEM((group // 2, 2 * WIN, 2 * WIN), bf16),
                pltpu.VMEM((group // 2, OFF, 2 * WIN), f32),
            ],
        ),
        out_shape=[pltpu.VMEM(shapes[0], jnp.int16), pltpu.VMEM(shapes[1], f32)],
        cost_estimate=pl.CostEstimate(
            flops=amount * 800 * 65536, transcendentals=amount * ROWS * WIN, bytes_accessed=amount * 60000
        ),
        compiler_params=pltpu.CompilerParams(vmem_limit_bytes=VMEM_GRANT),
        name="scores",
    )(*scalars, away(spectra), away(scale), *[near(c) for c in constants], *[near(p) for p in sources], *kept)


def average_scores(codes, capacity, chip_amount):
    devices = codes.shape[0]
    return pl.pallas_call(
        functools.partial(average_kernel, capacity, chip_amount),
        in_specs=[resident()],
        out_specs=[resident(), resident(), resident()],
        out_shape=[
            pltpu.VMEM((chip_amount, OFF * OFF), f32),
            pltpu.VMEM((GC, OFF * OFF), f32),
            pltpu.VMEM((GC, OFF * OFF), f32),
        ],
        scratch_shapes=[pltpu.VMEM((ROWS, devices * capacity, WIN), f32)],
        compiler_params=pltpu.CompilerParams(vmem_limit_bytes=VMEM_GRANT),
        name="average",
    )(near(codes))


def finish_kernel(turn, smooth, inner, outer, result):
    edge = smooth.shape[0] - GC
    result[...] = smooth[...]
    for row in range(ROWS):
        lanes = slice(row * WIN, (row + 1) * WIN)
        near, far = inner[:, lanes], outer[:, lanes]
        swap = turn[0] == 1
        result[:GC, lanes] = smooth[:GC, lanes] + jnp.where(swap, near, far) * 0.125
        result[edge:, lanes] = smooth[edge:, lanes] + jnp.where(swap, far, near) * 0.125


def finish(smooth, inner, outer, turn):
    return pl.pallas_call(
        finish_kernel,
        in_specs=[pl.BlockSpec(memory_space=pltpu.SMEM), resident(), resident(), resident()],
        out_shape=jax.ShapeDtypeStruct(smooth.shape, f32),
        compiler_params=pltpu.CompilerParams(vmem_limit_bytes=VMEM_GRANT),
        name="finish",
    )(jnp.full((1,), turn, jnp.int32), smooth, near(inner), near(outer))


def on_device(ref_chips, search_windows, dest_block, dest_slot):
    table = tables()
    chips = ref_chips[0]
    windows = search_windows[0]
    targets = dest_block[0, :, 0]
    slots = dest_slot[0]
    window_amount = windows.shape[0]
    chip_amount = chips.shape[0]
    tiles = lax.axis_size("tile")
    subs = lax.axis_size("sub")
    devices = tiles * subs
    capacity = max(2, 2 * window_amount // devices)

    images = windows.reshape(window_amount, WIN, WIN)
    sub = lax.axis_index("sub")
    cut = chip_amount * 3 // 4 // 8 * 8
    first_part, rest_part = spread(chips, tiles, cut)
    got = lax.all_to_all(first_part.reshape(tiles, cut * ROWS, WIN), "tile", split_axis=0, concat_axis=0, tiled=True)
    rests = [rest_part]
    for hop in range(1, tiles):
        rests.append(lax.ppermute(rest_part, "tile", [(i, (i + hop) % tiles) for i in range(tiles)]))
    gathered = [got.reshape(tiles * cut, ROWS, WIN), jnp.concatenate(rests, axis=0)]
    sources = []
    for index, part in enumerate(gathered):
        sources.append([part])
        for shift in range(1, subs):
            ring = [(i, (i - shift) % subs) for i in range(subs)]
            sources[index].append(lax.ppermute(part, "sub", ring))

    order = jnp.arange(window_amount, dtype=jnp.int32)
    late = (slots >= cut).astype(jnp.int32)
    before = order[:, None] > order[None, :]
    matches = targets[:, None] == targets[None, :]
    ranks = jnp.sum((matches & before).astype(jnp.int32), axis=1)
    ahead = (late[None, :] < late[:, None]) | ((late[None, :] == late[:, None]) & before)
    rows_at = jnp.sum(ahead.astype(jnp.int32), axis=1)
    chosen = rows_at[None, :] == order[:, None]

    def sort(values):
        return jnp.sum(jnp.where(chosen, values[None, :], 0), axis=1)

    group = min(SCORE_GROUP, window_amount)
    split = lax.div(window_amount - jnp.sum(late), group)
    place = (targets // subs) * cut + jnp.minimum(slots, cut - 1)
    turn = (lax.axis_index("tile") - targets // subs) % tiles
    place_late = turn * (chip_amount - cut) + jnp.maximum(slots - cut, 0)
    choice = (targets % subs - sub) % subs + late * subs
    position = jnp.full((1,), lax.axis_index(("tile", "sub")), jnp.int32)
    listing = sort(order)
    spectra, scale = prepare_windows(images, listing, table)
    spots = jnp.stack([sort(place), sort(place_late)])
    scalars = (sort(choice), spots, sort(targets), sort(ranks), sort(slots), position)
    settings = (table, devices, capacity, subs)
    zero = jnp.zeros_like(split)
    limits = jnp.stack([zero, split])
    partial = score_windows(spectra, scale, sources[0], (*scalars, limits), *settings, None, False)
    limits = jnp.stack([split, zero + window_amount // group])
    codes, _ = score_windows(
        spectra, scale, sources[0] + sources[1], (*scalars, limits), *settings, partial, True
    )

    received = lax.all_to_all(codes, ("tile", "sub"), split_axis=0, concat_axis=0, tiled=True)
    smooth, first, last = average_scores(received, capacity, chip_amount)
    if subs == 2:
        inner = lax.ppermute(jnp.where(sub == 0, last, first), "sub", [(0, 1), (1, 0)])
        ups = [(2 * i + 1, 2 * i + 2) for i in range(tiles - 1)]
        downs = [(2 * i + 2, 2 * i + 1) for i in range(tiles - 1)]
        outer = lax.ppermute(jnp.where(sub == 0, first, last), ("tile", "sub"), ups + downs)
        turn = sub
    else:
        inner = lax.ppermute(first, ("tile", "sub"), [(i + 1, i) for i in range(devices - 1)])
        outer = lax.ppermute(last, ("tile", "sub"), [(i, i + 1) for i in range(devices - 1)])
        turn = 0
    return finish(smooth, inner, outer, turn)[None]


def solution(mesh):
    return jax.shard_map(
        on_device,
        mesh=mesh,
        in_specs=(
            P(("groups", "pair"), ("tile", "sub"), None),
            P(("groups", "pair"), ("tile", "sub"), None),
            P(("groups", "pair"), ("tile", "sub"), None),
            P(("groups", "pair"), ("tile", "sub")),
        ),
        out_specs=P(("groups", "pair"), ("tile", "sub"), None),
        check_vma=False,
    )
```

```python
import functools

import jax
import jax.numpy as jnp
import ml_dtypes
import numpy as np
from jax import lax
from jax.experimental import pallas as pl
from jax.experimental.pallas import tpu as pltpu
from jax.sharding import PartitionSpec as P

CHIP = 64
WIN = 128
GC = 8
OFF = WIN - CHIP
PERIOD = WIN - 1
HALF = WIN // 2
ROWS = OFF * OFF // WIN
GROUP = 8
SCORE_GROUP = 16
VMEM_GRANT = 24 * 1024 * 1024
CODE = 32767.0
epsilon = 1e-06
f32 = jnp.float32
bf16 = jnp.bfloat16


def split_table(table):
    high = table.astype(ml_dtypes.bfloat16)
    low = (table - high.astype(np.float64)).astype(ml_dtypes.bfloat16)
    return (high, low)


def basis():
    freqs = np.arange(HALF)[:, None]
    places = np.arange(WIN)[None, :]
    angle = (freqs * places % PERIOD) * (2.0 * np.pi / PERIOD)
    used = (places < PERIOD).astype(np.float64)
    return (np.cos(angle) * used, np.sin(angle) * used)


def interleaved(table):
    return np.concatenate([table[0::2], table[1::2]], axis=0)


def twice(block):
    zero = np.zeros_like(block)
    return np.block([[block, zero], [zero, block]])


def tables():
    cosine, sine = basis()
    forward = np.concatenate([cosine, sine], axis=0)
    high, low = split_table(forward)
    starts = np.arange(OFF)[:, None]
    places = np.arange(WIN)[None, :]
    band = ((places >= starts) & (places < starts + CHIP)).astype(ml_dtypes.bfloat16)
    rows_band = interleaved(band)
    window_rows = np.concatenate([high, low, rows_band], axis=0)
    square_rows = np.concatenate([rows_band, rows_band], axis=1)
    window_lanes = np.concatenate([high.T, low.T], axis=1)
    window_lanes = np.concatenate([window_lanes, window_lanes], axis=0)
    band_lanes = twice(band.T)

    def pair_of(part):
        return np.concatenate([part[:, 0:CHIP:2], part[:, 1:CHIP:2]], axis=1)

    chip_rows = np.concatenate([pair_of(high), pair_of(high), pair_of(low)], axis=1)
    same = np.concatenate([cosine, cosine], axis=0)[:, :CHIP].T
    cross = np.concatenate([sine, -sine], axis=0)[:, :CHIP].T
    lane_high, lane_low = split_table(twice(np.concatenate([same, cross], axis=1)))
    chip_lanes = np.concatenate([lane_high, lane_high, lane_low], axis=0)
    weight = np.full((2 * HALF, 1), 2.0 / PERIOD)
    weight[0] = 1.0 / PERIOD
    inverse = (forward * weight)[:, :OFF].T
    inv_high, inv_low = split_table(inverse)
    rows_high, rows_low = interleaved(inv_high), interleaved(inv_low)
    inverse_rows = np.block([[rows_high, rows_high], [rows_low, rows_low]])
    inverse_lanes = np.concatenate([twice(inv_high.T), twice(inv_low.T)], axis=1)
    inverse_lanes = np.concatenate([inverse_lanes, inverse_lanes], axis=0)
    return dict(
        window_rows=window_rows, square_rows=square_rows, window_lanes=window_lanes,
        band_lanes=band_lanes, chip_rows=chip_rows, chip_lanes=chip_lanes,
        inverse_rows=inverse_rows, inverse_lanes=inverse_lanes,
    )


def dot(left, right):
    return jnp.dot(left, right, preferred_element_type=f32)


def halves(value):
    high = value.astype(bf16)
    low = (value - high.astype(f32)).astype(bf16)
    return (high, low)


def thirds(value):
    high = value.astype(bf16)
    rest = value - high.astype(f32)
    middle = rest.astype(bf16)
    low = (rest - middle.astype(f32)).astype(bf16)
    return (high, middle, low)


def window_kernel(windows, window_rows, square_rows, window_lanes, band_lanes, spectra, scale):
    group = windows.shape[0]
    for first in range(0, group, 2):
        image = jnp.concatenate([windows[first], windows[first + 1]], axis=1)
        rows = dot(window_rows[...], image)
        spec_rows = rows[:WIN] + rows[WIN:2 * WIN]
        sums = rows[2 * WIN:]
        wide = image.astype(f32)
        square_high, square_low = halves(wide * wide)
        squares = dot(square_rows[...], jnp.concatenate([square_high, square_low], axis=0))
        for part in range(2):
            lanes = slice(part * WIN, (part + 1) * WIN)
            high, low = halves(spec_rows[:, lanes])
            both = dot(jnp.concatenate([high, low], axis=1), window_lanes[...])
            spectra[first + part] = both[:, :WIN] + both[:, WIN:]
            pieces = []
            for source in (sums, squares):
                own = source[:, lanes]
                packed = jnp.concatenate([own[:ROWS], own[ROWS:]], axis=1)
                pieces.extend(thirds(packed))
            boxed = dot(jnp.concatenate(pieces, axis=0), band_lanes[...])
            boxes = [boxed[i * ROWS:(i + 1) * ROWS] for i in range(6)]
            mean = (boxes[0] + boxes[1] + boxes[2]) * (1.0 / (CHIP * CHIP))
            second = (boxes[3] + boxes[4] + boxes[5]) * (1.0 / (CHIP * CHIP))
            variance = second - mean * mean
            scale[first + part] = lax.rsqrt(variance + epsilon)


def score_kernel(
    capacity, choice, place, target, ranks, slots, position,
    spectra, scale, chip_lanes, chip_rows, inverse_rows, inverse_lanes, *rest,
):
    *sources, out, marks, lefts, lines, packs, pairs, products, backs = rest
    step = pl.program_id(0)
    group = lefts.shape[0] // ROWS
    base = step * group
    body = capacity * ROWS
    lane = lax.broadcasted_iota(jnp.int32, (8, WIN), 1)
    line = lax.broadcasted_iota(jnp.int32, (8, WIN), 0)

    @pl.when(step == 0)
    def _():
        marks[...] = jnp.zeros_like(marks)

    raws = []
    for part in range(group):
        window = base + part
        raw = sources[0][place[window]]
        for index in range(1, len(sources)):
            raw = jnp.where(choice[window] == index, sources[index][place[window]], raw)
        raws.append(raw.astype(f32))
    total = jnp.concatenate([jnp.sum(raw, axis=0, keepdims=True) for raw in raws], axis=0)
    mean = jnp.sum(total, axis=1, keepdims=True) * (1.0 / (CHIP * CHIP))
    raws = [raws[part] - mean[part:part + 1] for part in range(group)]
    total = jnp.concatenate([jnp.sum(raw * raw, axis=0, keepdims=True) for raw in raws], axis=0)
    power = jnp.sum(total, axis=1, keepdims=True) * (1.0 / (CHIP * CHIP))
    gain = lax.rsqrt(power + epsilon) * (1.0 / CHIP)
    for part in range(group):
        own = slice(part * ROWS, (part + 1) * ROWS)
        high, low = halves(raws[part])
        lefts[own, :WIN] = high
        lefts[own, WIN:2 * WIN] = low
        lefts[own, 2 * WIN:] = high
    lines[...] = dot(lefts[...], chip_lanes[...])

    def chip_spectrum(part):
        high, low = halves(lines[part * ROWS:(part + 1) * ROWS, :])
        pieces = [high[:, :2 * WIN], high[:, 2 * WIN:], low[:, :2 * WIN], low[:, 2 * WIN:]]
        pairs[part] = dot(chip_rows[...], jnp.concatenate(pieces + pieces[:2], axis=0))

    def multiply(part):
        lanes = slice(part % 2 * WIN, (part % 2 + 1) * WIN)
        for row in range(0, HALF, 32):
            upper, lower = slice(row, row + 32), slice(HALF + row, HALF + row + 32)
            own_c, own_s = spectra[part, upper], spectra[part, lower]
            turned_c, turned_s = pltpu.roll(own_c, HALF, 1), pltpu.roll(own_s, HALF, 1)
            same_c, same_s = pairs[part, upper, :WIN], pairs[part, lower, :WIN]
            cross_c, cross_s = pairs[part, upper, WIN:], pairs[part, lower, WIN:]
            out_c = same_c * own_c + cross_c * turned_c + same_s * own_s + cross_s * turned_s
            out_s = same_c * own_s + cross_c * turned_s - same_s * own_c - cross_s * turned_c
            for value, place_to in ((out_c, row), (out_s, HALF + row)):
                high, low = halves(value)
                products[part // 2, place_to:place_to + 32, lanes] = high
                products[part // 2, WIN + place_to:WIN + place_to + 32, lanes] = low

    def invert(pair):
        back = dot(inverse_rows[...], products[pair])
        backs[pair] = back[:OFF] + back[OFF:]

    def pack(pair):
        for part in (2 * pair, 2 * pair + 1):
            lanes = slice(part % 2 * WIN, (part % 2 + 1) * WIN)
            own = slice(part * ROWS, (part + 1) * ROWS)
            high, low = halves(backs[pair, :, lanes])
            packs[own, :WIN] = high[:ROWS]
            packs[own, WIN:2 * WIN] = high[ROWS:]
            packs[own, 2 * WIN:3 * WIN] = low[:ROWS]
            packs[own, 3 * WIN:] = low[ROWS:]

    for part in range(group + 4):
        if part < group:
            chip_spectrum(part)
        if 2 <= part < group + 2:
            multiply(part - 2)
            if part % 2 == 1:
                invert((part - 2) // 2)
        if part >= 4 and part % 2 == 1:
            pack((part - 4) // 2)
    both = dot(packs[...], inverse_lanes[...])
    scores = []
    for part in range(group):
        own = slice(part * ROWS, (part + 1) * ROWS)
        numerator = both[own, :WIN] + both[own, WIN:]
        scores.append(numerator * (scale[part] * gain[part:part + 1]))
    largest = jnp.concatenate([jnp.max(jnp.abs(score), axis=0, keepdims=True) for score in scores], axis=0)
    largest = jnp.max(largest, axis=1, keepdims=True)
    power = jnp.ceil(jnp.log2(jnp.maximum(largest, 1e-30)))
    shrink = jnp.exp2(-power).astype(bf16).astype(f32)
    for part in range(group):
        window = base + part
        score = scores[part]
        size = jnp.maximum(jnp.abs(score) * shrink[part:part + 1], 1e-30)
        root = size * lax.rsqrt(size) * CODE
        root = jnp.minimum(root, CODE)
        code = jnp.round(jnp.where(score < 0, -root, root)).astype(jnp.int32).astype(jnp.int16)
        to = target[window]
        out[to, pl.ds(pl.multiple_of(ranks[window] * ROWS, ROWS), ROWS), :] = code
        here = lane == position[0] * capacity + ranks[window]
        named = (slots[window] + 1).astype(f32)
        mark = jnp.where(line == 0, named, jnp.where(line == 1, power[part:part + 1], 0.0))
        marks[to] = marks[to] + jnp.where(here, mark, 0.0)

    @pl.when(step == pl.num_programs(0) - 1)
    def _():
        for to in range(out.shape[0]):
            out[to, body:, :] = marks[to].astype(jnp.int32).astype(jnp.int16)


def average_kernel(capacity, chip_amount, codes, smooth, first, last, values):
    devices = codes.shape[0]
    body = capacity * ROWS
    slots = devices * capacity
    notes = codes[0, body:, :].astype(jnp.int32).astype(f32)
    for source in range(1, devices):
        notes = notes + codes[source, body:, :].astype(jnp.int32).astype(f32)
    for source in range(devices):
        wide = codes[source, :body, :].astype(jnp.int32).astype(f32)
        turned = jnp.swapaxes((wide * jnp.abs(wide)).reshape(capacity, ROWS, WIN), 0, 1)
        values[:, source * capacity:(source + 1) * capacity, :] = turned
    chip = lax.broadcasted_iota(jnp.int32, (chip_amount, WIN), 0)
    hit = (notes[0:1] - 1.0).astype(jnp.int32) == chip
    looks = jnp.sum(hit.astype(f32), axis=1, keepdims=True)
    weight = jnp.where(hit, jnp.exp2(notes[1:2]), 0.0).astype(bf16)[:, :slots]
    weight = jnp.concatenate([weight, weight], axis=1)
    factor = 1.0 / (jnp.maximum(looks, 1.0) * (CODE * CODE))
    factor = jnp.broadcast_to(factor, (chip_amount, WIN))
    column = chip % GC
    zero = jnp.zeros((GC, WIN), f32)
    for row in range(ROWS):
        high, low = halves(values[row])
        average = dot(weight, jnp.concatenate([high, low], axis=0)) * factor
        lanes = slice(row * WIN, (row + 1) * WIN)
        first[:, lanes] = average[:GC]
        last[:, lanes] = average[chip_amount - GC:]
        below = jnp.concatenate([average[GC:], zero], axis=0)
        above = jnp.concatenate([zero, average[:-GC]], axis=0)
        left = jnp.where(column == 0, 0.0, pltpu.roll(average, 1, 0))
        right = jnp.where(column == GC - 1, 0.0, pltpu.roll(average, chip_amount - 1, 0))
        smooth[:, lanes] = (4.0 * average + above + below + left + right) * 0.125


def resident():
    return pl.BlockSpec(memory_space=pltpu.VMEM)


def away(array):
    return pltpu.with_memory_space_constraint(array, pltpu.HBM)


def near(array):
    return pltpu.with_memory_space_constraint(array, pltpu.VMEM)


def spread_kernel(chips, sent):
    base = pl.program_id(0) * 8
    for row in range(0, ROWS, 8):
        lanes = [chips[:, (row + i) * WIN:(row + i + 1) * WIN].astype(f32) for i in range(8)]
        turned = jnp.swapaxes(jnp.stack(lanes, axis=0), 0, 1).astype(bf16)
        for to in range(sent.shape[0]):
            sent[to, pl.ds(base, 8), row:row + 8, :] = turned


def spread(chips, tiles):
    return pl.pallas_call(
        spread_kernel,
        grid=(chips.shape[0] // 8,),
        in_specs=[pl.BlockSpec((8, chips.shape[1]), lambda i: (i, 0))],
        out_specs=resident(),
        out_shape=pltpu.VMEM((tiles, chips.shape[0], ROWS, WIN), bf16),
        compiler_params=pltpu.CompilerParams(vmem_limit_bytes=VMEM_GRANT),
        name="spread",
    )(away(chips))


def prepare_windows(images, table):
    amount = images.shape[0]
    group = min(GROUP, amount)
    constants = [jnp.asarray(table[k]) for k in ("window_rows", "square_rows", "window_lanes", "band_lanes")]
    return pl.pallas_call(
        window_kernel,
        grid=(amount // group,),
        in_specs=[pl.BlockSpec((group, WIN, WIN), lambda i: (i, 0, 0))] + [resident() for _ in constants],
        out_specs=[
            pl.BlockSpec((group, WIN, WIN), lambda i: (i, 0, 0)),
            pl.BlockSpec((group, ROWS, WIN), lambda i: (i, 0, 0)),
        ],
        out_shape=[
            pltpu.HBM((amount, WIN, WIN), f32),
            pltpu.HBM((amount, ROWS, WIN), f32),
        ],
        cost_estimate=pl.CostEstimate(
            flops=amount * 2 * 900 * 65536, transcendentals=amount * ROWS * WIN, bytes_accessed=amount * 120000
        ),
        compiler_params=pltpu.CompilerParams(vmem_limit_bytes=VMEM_GRANT),
        name="window_spectra",
    )(images, *constants)


def score_windows(spectra, scale, sources, scalars, table, devices, capacity):
    amount = spectra.shape[0]
    group = min(SCORE_GROUP, amount)
    constants = [jnp.asarray(table[k]) for k in ("chip_lanes", "chip_rows", "inverse_rows", "inverse_lanes")]
    shape = (devices, capacity * ROWS + 8, WIN)
    return pl.pallas_call(
        functools.partial(score_kernel, capacity),
        grid_spec=pltpu.PrefetchScalarGridSpec(
            num_scalar_prefetch=len(scalars),
            grid=(amount // group,),
            in_specs=[
                pl.BlockSpec((group, WIN, WIN), lambda i, *_: (i, 0, 0)),
                pl.BlockSpec((group, ROWS, WIN), lambda i, *_: (i, 0, 0)),
            ] + [resident() for _ in constants] + [resident() for _ in sources],
            out_specs=resident(),
            scratch_shapes=[
                pltpu.VMEM((devices, 8, WIN), f32),
                pltpu.VMEM((group * ROWS, 3 * WIN), bf16),
                pltpu.VMEM((group * ROWS, 4 * WIN), f32),
                pltpu.VMEM((group * ROWS, 4 * WIN), bf16),
                pltpu.VMEM((group, WIN, 2 * WIN), f32),
                pltpu.VMEM((group // 2, 2 * WIN, 2 * WIN), bf16),
                pltpu.VMEM((group // 2, OFF, 2 * WIN), f32),
            ],
        ),
        out_shape=pltpu.VMEM(shape, jnp.int16),
        compiler_params=pltpu.CompilerParams(vmem_limit_bytes=VMEM_GRANT),
        name="scores",
    )(*scalars, away(spectra), away(scale), *[near(c) for c in constants], *[near(source) for source in sources])


def average_scores(codes, capacity, chip_amount):
    devices = codes.shape[0]
    return pl.pallas_call(
        functools.partial(average_kernel, capacity, chip_amount),
        in_specs=[resident()],
        out_specs=[resident(), resident(), resident()],
        out_shape=[
            pltpu.VMEM((chip_amount, OFF * OFF), f32),
            pltpu.VMEM((GC, OFF * OFF), f32),
            pltpu.VMEM((GC, OFF * OFF), f32),
        ],
        scratch_shapes=[pltpu.VMEM((ROWS, devices * capacity, WIN), f32)],
        compiler_params=pltpu.CompilerParams(vmem_limit_bytes=VMEM_GRANT),
        name="average",
    )(near(codes))


def finish_kernel(turn, smooth, inner, outer, result):
    edge = smooth.shape[0] - GC
    result[...] = smooth[...]
    for row in range(ROWS):
        lanes = slice(row * WIN, (row + 1) * WIN)
        near, far = inner[:, lanes], outer[:, lanes]
        swap = turn[0] == 1
        result[:GC, lanes] = smooth[:GC, lanes] + jnp.where(swap, near, far) * 0.125
        result[edge:, lanes] = smooth[edge:, lanes] + jnp.where(swap, far, near) * 0.125


def finish(smooth, inner, outer, turn):
    return pl.pallas_call(
        finish_kernel,
        in_specs=[pl.BlockSpec(memory_space=pltpu.SMEM), resident(), resident(), resident()],
        out_shape=jax.ShapeDtypeStruct(smooth.shape, f32),
        compiler_params=pltpu.CompilerParams(vmem_limit_bytes=VMEM_GRANT),
        name="finish",
    )(jnp.full((1,), turn, jnp.int32), smooth, near(inner), near(outer))


def on_device(ref_chips, search_windows, dest_block, dest_slot):
    table = tables()
    chips = ref_chips[0]
    windows = search_windows[0]
    targets = dest_block[0, :, 0]
    slots = dest_slot[0]
    window_amount = windows.shape[0]
    chip_amount = chips.shape[0]
    tiles = lax.axis_size("tile")
    subs = lax.axis_size("sub")
    devices = tiles * subs
    capacity = max(2, 2 * window_amount // devices)

    images = windows.reshape(window_amount, WIN, WIN)
    sub = lax.axis_index("sub")
    sent = spread(chips, tiles).reshape(tiles, chip_amount * ROWS, WIN)
    gathered = lax.all_to_all(sent, "tile", split_axis=0, concat_axis=0, tiled=True)
    gathered = gathered.reshape(tiles * chip_amount, ROWS, WIN)
    spectra, scale = prepare_windows(images, table)
    sources = [gathered]
    for shift in range(1, subs):
        ring = [(i, (i - shift) % subs) for i in range(subs)]
        sources.append(lax.ppermute(gathered, "sub", ring))

    order = jnp.arange(window_amount, dtype=jnp.int32)
    matches = targets[:, None] == targets[None, :]
    earlier = order[:, None] > order[None, :]
    ranks = jnp.sum((matches & earlier).astype(jnp.int32), axis=1)
    choice = (targets % subs - sub) % subs
    place = (targets // subs) * chip_amount + slots
    position = jnp.full((1,), lax.axis_index(("tile", "sub")), jnp.int32)
    scalars = (choice, place, targets, ranks, slots, position)
    codes = score_windows(spectra, scale, sources, scalars, table, devices, capacity)

    received = lax.all_to_all(codes, ("tile", "sub"), split_axis=0, concat_axis=0, tiled=True)
    smooth, first, last = average_scores(received, capacity, chip_amount)
    if subs == 2:
        inner = lax.ppermute(jnp.where(sub == 0, last, first), "sub", [(0, 1), (1, 0)])
        ups = [(2 * i + 1, 2 * i + 2) for i in range(tiles - 1)]
        downs = [(2 * i + 2, 2 * i + 1) for i in range(tiles - 1)]
        outer = lax.ppermute(jnp.where(sub == 0, first, last), ("tile", "sub"), ups + downs)
        turn = sub
    else:
        inner = lax.ppermute(first, ("tile", "sub"), [(i + 1, i) for i in range(devices - 1)])
        outer = lax.ppermute(last, ("tile", "sub"), [(i, i + 1) for i in range(devices - 1)])
        turn = 0
    return finish(smooth, inner, outer, turn)[None]


def solution(mesh):
    return jax.shard_map(
        on_device,
        mesh=mesh,
        in_specs=(
            P(("groups", "pair"), ("tile", "sub"), None),
            P(("groups", "pair"), ("tile", "sub"), None),
            P(("groups", "pair"), ("tile", "sub"), None),
            P(("groups", "pair"), ("tile", "sub")),
        ),
        out_specs=P(("groups", "pair"), ("tile", "sub"), None),
        check_vma=False,
    )
```

```python
import functools

import jax
import jax.numpy as jnp
import ml_dtypes
import numpy as np
from jax import lax
from jax.experimental import pallas as pl
from jax.experimental.pallas import tpu as pltpu
from jax.sharding import PartitionSpec as P

CHIP = 64
WIN = 128
GC = 8
OFF = WIN - CHIP
PERIOD = WIN - 1
HALF = WIN // 2
ROWS = OFF * OFF // WIN
GROUP = 8
SCORE_GROUP = 16
VMEM_GRANT = 24 * 1024 * 1024
CODE = 32767.0
epsilon = 1e-06
f32 = jnp.float32
bf16 = jnp.bfloat16


def split_table(table):
    high = table.astype(ml_dtypes.bfloat16)
    low = (table - high.astype(np.float64)).astype(ml_dtypes.bfloat16)
    return (high, low)


def basis():
    freqs = np.arange(HALF)[:, None]
    places = np.arange(WIN)[None, :]
    angle = (freqs * places % PERIOD) * (2.0 * np.pi / PERIOD)
    used = (places < PERIOD).astype(np.float64)
    return (np.cos(angle) * used, np.sin(angle) * used)


def interleaved(table):
    return np.concatenate([table[0::2], table[1::2]], axis=0)


def twice(block):
    zero = np.zeros_like(block)
    return np.block([[block, zero], [zero, block]])


def tables():
    cosine, sine = basis()
    forward = np.concatenate([cosine, sine], axis=0)
    high, low = split_table(forward)
    starts = np.arange(OFF)[:, None]
    places = np.arange(WIN)[None, :]
    band = ((places >= starts) & (places < starts + CHIP)).astype(ml_dtypes.bfloat16)
    rows_band = interleaved(band)
    window_rows = np.concatenate([high, low, rows_band], axis=0)
    square_rows = np.concatenate([rows_band, rows_band], axis=1)
    window_lanes = np.concatenate([high.T, low.T], axis=1)
    window_lanes = np.concatenate([window_lanes, window_lanes], axis=0)
    band_lanes = twice(band.T)

    def pair_of(part):
        return np.concatenate([part[:, 0:CHIP:2], part[:, 1:CHIP:2]], axis=1)

    chip_rows = np.concatenate([pair_of(high), pair_of(high), pair_of(low)], axis=1)
    same = np.concatenate([cosine, cosine], axis=0)[:, :CHIP].T
    cross = np.concatenate([sine, -sine], axis=0)[:, :CHIP].T
    lane_high, lane_low = split_table(twice(np.concatenate([same, cross], axis=1)))
    chip_lanes = np.concatenate([lane_high, lane_high, lane_low], axis=0)
    weight = np.full((2 * HALF, 1), 2.0 / PERIOD)
    weight[0] = 1.0 / PERIOD
    inverse = (forward * weight)[:, :OFF].T
    inv_high, inv_low = split_table(inverse)
    rows_high, rows_low = interleaved(inv_high), interleaved(inv_low)
    inverse_rows = np.block([[rows_high, rows_high], [rows_low, rows_low]])
    inverse_lanes = np.concatenate([twice(inv_high.T), twice(inv_low.T)], axis=1)
    inverse_lanes = np.concatenate([inverse_lanes, inverse_lanes], axis=0)
    return dict(
        window_rows=window_rows, square_rows=square_rows, window_lanes=window_lanes,
        band_lanes=band_lanes, chip_rows=chip_rows, chip_lanes=chip_lanes,
        inverse_rows=inverse_rows, inverse_lanes=inverse_lanes,
    )


def dot(left, right):
    return jnp.dot(left, right, preferred_element_type=f32)


def halves(value):
    high = value.astype(bf16)
    low = (value - high.astype(f32)).astype(bf16)
    return (high, low)


def thirds(value):
    high = value.astype(bf16)
    rest = value - high.astype(f32)
    middle = rest.astype(bf16)
    low = (rest - middle.astype(f32)).astype(bf16)
    return (high, middle, low)


def window_kernel(order, windows, window_rows, square_rows, window_lanes, band_lanes, spectra, scale):
    group = spectra.shape[0]
    base = pl.program_id(0) * group
    for first in range(0, group, 2):
        image = jnp.concatenate([windows[order[base + first]], windows[order[base + first + 1]]], axis=1)
        rows = dot(window_rows[...], image)
        spec_rows = rows[:WIN] + rows[WIN:2 * WIN]
        sums = rows[2 * WIN:]
        wide = image.astype(f32)
        square_high, square_low = halves(wide * wide)
        squares = dot(square_rows[...], jnp.concatenate([square_high, square_low], axis=0))
        for part in range(2):
            lanes = slice(part * WIN, (part + 1) * WIN)
            high, low = halves(spec_rows[:, lanes])
            both = dot(jnp.concatenate([high, low], axis=1), window_lanes[...])
            spectra[first + part] = both[:, :WIN] + both[:, WIN:]
            pieces = []
            for source in (sums, squares):
                own = source[:, lanes]
                packed = jnp.concatenate([own[:ROWS], own[ROWS:]], axis=1)
                pieces.extend(thirds(packed))
            boxed = dot(jnp.concatenate(pieces, axis=0), band_lanes[...])
            boxes = [boxed[i * ROWS:(i + 1) * ROWS] for i in range(6)]
            mean = (boxes[0] + boxes[1] + boxes[2]) * (1.0 / (CHIP * CHIP))
            second = (boxes[3] + boxes[4] + boxes[5]) * (1.0 / (CHIP * CHIP))
            variance = second - mean * mean
            scale[first + part] = lax.rsqrt(variance + epsilon)


def score_kernel(capacity, quick, opening, *refs):
    (choice, place, target, ranks, slots, position,
     spectra, scale, chip_lanes, chip_rows, inverse_rows, inverse_lanes, *rest) = refs
    *rest, lefts, lines, packs, pairs, products, backs, marks, stage, note_stage, sems, note_sem = rest
    if opening:
        *sources, early_codes, late_codes, marks_out = rest
    else:
        *sources, _, marks_in, late_codes = rest
    step = pl.program_id(0)
    steps = pl.num_programs(0)
    group = lefts.shape[0] // ROWS
    devices = late_codes.shape[0]
    first_step = 0 if opening else position[1]
    base = (step + first_step) * group
    lane = lax.broadcasted_iota(jnp.int32, (8, WIN), 1)
    line = lax.broadcasted_iota(jnp.int32, (8, WIN), 0)

    @pl.when(step == 0)
    def _():
        marks[...] = jnp.zeros_like(marks)
        if not opening:
            marks[devices:] = marks_in[...]

    raws = []
    for part in range(group):
        window = base + part
        raw = sources[0][place[window]]
        for index in range(1, len(sources)):
            raw = jnp.where(choice[window] == index, sources[index][place[window]], raw)
        raws.append(raw.astype(f32))
    total = jnp.concatenate([jnp.sum(raw, axis=0, keepdims=True) for raw in raws], axis=0)
    mean = jnp.sum(total, axis=1, keepdims=True) * (1.0 / (CHIP * CHIP))
    raws = [raws[part] - mean[part:part + 1] for part in range(group)]
    total = jnp.concatenate([jnp.sum(raw * raw, axis=0, keepdims=True) for raw in raws], axis=0)
    power = jnp.sum(total, axis=1, keepdims=True) * (1.0 / (CHIP * CHIP))
    gain = lax.rsqrt(power + epsilon) * (1.0 / CHIP)
    for part in range(group):
        own = slice(part * ROWS, (part + 1) * ROWS)
        high, low = halves(raws[part])
        lefts[own, :WIN] = high
        lefts[own, WIN:2 * WIN] = low
        lefts[own, 2 * WIN:] = high
    lines[...] = dot(lefts[...], chip_lanes[...])

    def chip_spectrum(part):
        high, low = halves(lines[part * ROWS:(part + 1) * ROWS, :])
        pieces = [high[:, :2 * WIN], high[:, 2 * WIN:], low[:, :2 * WIN], low[:, 2 * WIN:]]
        pairs[part] = dot(chip_rows[...], jnp.concatenate(pieces + pieces[:2], axis=0))

    def multiply(part):
        lanes = slice(part % 2 * WIN, (part % 2 + 1) * WIN)
        for row in range(0, HALF, 32):
            upper, lower = slice(row, row + 32), slice(HALF + row, HALF + row + 32)
            own_c, own_s = spectra[part, upper], spectra[part, lower]
            turned_c, turned_s = pltpu.roll(own_c, HALF, 1), pltpu.roll(own_s, HALF, 1)
            same_c, same_s = pairs[part, upper, :WIN], pairs[part, lower, :WIN]
            cross_c, cross_s = pairs[part, upper, WIN:], pairs[part, lower, WIN:]
            out_c = same_c * own_c + cross_c * turned_c + same_s * own_s + cross_s * turned_s
            out_s = same_c * own_s + cross_c * turned_s - same_s * own_c - cross_s * turned_c
            for value, place_to in ((out_c, row), (out_s, HALF + row)):
                high, low = halves(value)
                products[part // 2, place_to:place_to + 32, lanes] = high
                products[part // 2, WIN + place_to:WIN + place_to + 32, lanes] = low

    def invert(pair):
        back = dot(inverse_rows[...], products[pair])
        backs[pair] = back[:OFF] + back[OFF:]

    def pack(pair):
        for part in (2 * pair, 2 * pair + 1):
            lanes = slice(part % 2 * WIN, (part % 2 + 1) * WIN)
            own = slice(part * ROWS, (part + 1) * ROWS)
            high, low = halves(backs[pair, :, lanes])
            packs[own, :WIN] = high[:ROWS]
            packs[own, WIN:2 * WIN] = high[ROWS:]
            packs[own, 2 * WIN:3 * WIN] = low[:ROWS]
            packs[own, 3 * WIN:] = low[ROWS:]

    for part in range(group + 4):
        if part < group:
            chip_spectrum(part)
        if 2 <= part < group + 2:
            multiply(part - 2)
            if part % 2 == 1:
                invert((part - 2) // 2)
        if part >= 4 and part % 2 == 1:
            pack((part - 4) // 2)
    both = dot(packs[...], inverse_lanes[...])
    scores = []
    for part in range(group):
        own = slice(part * ROWS, (part + 1) * ROWS)
        numerator = both[own, :WIN] + both[own, WIN:]
        scores.append(numerator * (scale[part] * gain[part:part + 1]))
    largest = jnp.concatenate([jnp.max(jnp.abs(score), axis=0, keepdims=True) for score in scores], axis=0)
    largest = jnp.max(largest, axis=1, keepdims=True)
    power = jnp.ceil(jnp.log2(jnp.maximum(largest, 1e-30)))
    shrink = jnp.exp2(-power).astype(bf16).astype(f32)
    for part in range(group):
        window = base + part
        score = scores[part]
        size = jnp.maximum(jnp.abs(score) * shrink[part:part + 1], 1e-30)
        root = size * lax.rsqrt(size) * CODE
        root = jnp.minimum(root, CODE)
        code = jnp.round(jnp.where(score < 0, -root, root)).astype(jnp.int32).astype(jnp.int16)
        stage[step * group + part] = code
        to = target[window] + jnp.where(ranks[window] < quick, 0, devices)
        here = (lane == position[0] * capacity + ranks[window]) & (line < 2)
        named = (slots[window] + 1).astype(f32)
        mark = jnp.where(line == 0, named, power[part:part + 1])
        marks[to] = jnp.where(here, mark, marks[to])

    def copy_out(part, codes, rank):
        rows = pl.ds(pl.multiple_of(rank * ROWS, ROWS), ROWS)
        index = step * group + part
        return pltpu.make_async_copy(stage.at[index], codes.at[target[base + part], rows, :], sems.at[index])

    for part in range(group):
        rank = ranks[base + part]
        if opening:
            @pl.when(rank < quick)
            def _():
                copy_out(part, early_codes, rank).start()

            @pl.when(rank >= quick)
            def _():
                copy_out(part, late_codes, rank - quick).start()
        else:
            copy_out(part, late_codes, rank - quick).start()

    @pl.when(step == steps - 1)
    def _():
        codes = early_codes if opening else late_codes
        own = marks[:devices] if opening else marks[devices:]
        note_stage[...] = own.astype(jnp.int32).astype(jnp.int16)
        if opening:
            marks_out[...] = marks[devices:]
        count = codes.shape[1] - 8
        notes = pltpu.make_async_copy(note_stage, codes.at[:, count:, :], note_sem)
        notes.start()
        for index in range(stage.shape[0]):
            pltpu.make_async_copy(stage.at[index], late_codes.at[0, :ROWS, :], sems.at[index]).wait()
        notes.wait()


def average_kernel(capacity, quick, chip_amount, early_codes, late_codes, smooth, first, last, values):
    devices = early_codes.shape[0]
    slots = devices * capacity
    notes = jnp.zeros((8, WIN), f32)
    for codes, start, count in ((early_codes, 0, quick), (late_codes, quick, capacity - quick)):
        for source in range(devices):
            notes = notes + codes[source, count * ROWS:, :].astype(jnp.int32).astype(f32)
            wide = codes[source, :count * ROWS, :].astype(jnp.int32).astype(f32)
            turned = jnp.swapaxes((wide * jnp.abs(wide)).reshape(count, ROWS, WIN), 0, 1)
            values[:, source * capacity + start:source * capacity + start + count, :] = turned
    chip = lax.broadcasted_iota(jnp.int32, (chip_amount, WIN), 0)
    hit = (notes[0:1] - 1.0).astype(jnp.int32) == chip
    looks = jnp.sum(hit.astype(f32), axis=1, keepdims=True)
    weight = jnp.where(hit, jnp.exp2(notes[1:2]), 0.0).astype(bf16)[:, :slots]
    weight = jnp.concatenate([weight, weight], axis=1)
    factor = 1.0 / (jnp.maximum(looks, 1.0) * (CODE * CODE))
    factor = jnp.broadcast_to(factor, (chip_amount, WIN))
    column = chip % GC
    zero = jnp.zeros((GC, WIN), f32)
    for row in range(ROWS):
        high, low = halves(values[row])
        average = dot(weight, jnp.concatenate([high, low], axis=0)) * factor
        lanes = slice(row * WIN, (row + 1) * WIN)
        first[:, lanes] = average[:GC]
        last[:, lanes] = average[chip_amount - GC:]
        below = jnp.concatenate([average[GC:], zero], axis=0)
        above = jnp.concatenate([zero, average[:-GC]], axis=0)
        left = jnp.where(column == 0, 0.0, pltpu.roll(average, 1, 0))
        right = jnp.where(column == GC - 1, 0.0, pltpu.roll(average, chip_amount - 1, 0))
        smooth[:, lanes] = (4.0 * average + above + below + left + right) * 0.125


def resident():
    return pl.BlockSpec(memory_space=pltpu.VMEM)


def away(array):
    return pltpu.with_memory_space_constraint(array, pltpu.HBM)


def near(array):
    return pltpu.with_memory_space_constraint(array, pltpu.VMEM)


def spread_kernel(chips, sent):
    chip_amount = chips.shape[0]
    for first in range(0, chip_amount, 8):
        for row in range(0, ROWS, 8):
            lanes = [chips[first:first + 8, (row + i) * WIN:(row + i + 1) * WIN].astype(f32) for i in range(8)]
            turned = jnp.swapaxes(jnp.stack(lanes, axis=0), 0, 1).astype(bf16)
            for to in range(sent.shape[0]):
                sent[to, first:first + 8, row:row + 8, :] = turned


def spread(chips, tiles):
    return pl.pallas_call(
        spread_kernel,
        in_specs=[resident()],
        out_specs=resident(),
        out_shape=pltpu.VMEM((tiles, chips.shape[0], ROWS, WIN), bf16),
        compiler_params=pltpu.CompilerParams(vmem_limit_bytes=VMEM_GRANT),
        name="spread",
    )(chips)


def prepare_windows(images, order, table):
    amount = images.shape[0]
    group = min(GROUP, amount)
    constants = [jnp.asarray(table[k]) for k in ("window_rows", "square_rows", "window_lanes", "band_lanes")]
    return pl.pallas_call(
        window_kernel,
        grid_spec=pltpu.PrefetchScalarGridSpec(
            num_scalar_prefetch=1,
            grid=(amount // group,),
            in_specs=[resident()] + [resident() for _ in constants],
            out_specs=[
                pl.BlockSpec((group, WIN, WIN), lambda i, _: (i, 0, 0)),
                pl.BlockSpec((group, ROWS, WIN), lambda i, _: (i, 0, 0)),
            ],
        ),
        out_shape=[
            pltpu.HBM((amount, WIN, WIN), f32),
            pltpu.HBM((amount, ROWS, WIN), f32),
        ],
        cost_estimate=pl.CostEstimate(
            flops=amount * 2 * 900 * 65536, transcendentals=amount * ROWS * WIN, bytes_accessed=amount * 120000
        ),
        compiler_params=pltpu.CompilerParams(vmem_limit_bytes=VMEM_GRANT),
        name="window_spectra",
    )(order, near(images), *constants)


def score_windows(spectra, scale, sources, scalars, table, devices, capacity, quick, half, earlier):
    amount = spectra.shape[0]
    group = min(SCORE_GROUP, half)
    opening = earlier is None
    steps = (half if opening else amount - half) // group
    start = 0 if opening else half // group
    constants = [jnp.asarray(table[k]) for k in ("chip_lanes", "chip_rows", "inverse_rows", "inverse_lanes")]
    count = len(scalars)
    anywhere = pl.BlockSpec(memory_space=pl.ANY)
    late = jax.ShapeDtypeStruct((devices, (capacity - quick) * ROWS + 8, WIN), jnp.int16)
    if opening:
        kept, kept_specs = [], []
        out_specs = [anywhere, anywhere, resident()]
        out_shape = [
            jax.ShapeDtypeStruct((devices, quick * ROWS + 8, WIN), jnp.int16),
            late,
            jax.ShapeDtypeStruct((devices, 8, WIN), f32),
        ]
        aliases = {}
    else:
        kept, kept_specs = list(earlier), [anywhere, resident()]
        out_specs, out_shape = [anywhere], [late]
        aliases = {count + 6 + len(sources): 0}

    def block(i, *_):
        return (i + start, 0, 0)

    return pl.pallas_call(
        functools.partial(score_kernel, capacity, quick, opening),
        grid_spec=pltpu.PrefetchScalarGridSpec(
            num_scalar_prefetch=count,
            grid=(steps,),
            in_specs=[pl.BlockSpec((group, WIN, WIN), block), pl.BlockSpec((group, ROWS, WIN), block)]
            + [resident() for _ in constants] + [resident() for _ in sources] + kept_specs,
            out_specs=out_specs,
            scratch_shapes=[
                pltpu.VMEM((group * ROWS, 3 * WIN), bf16),
                pltpu.VMEM((group * ROWS, 4 * WIN), f32),
                pltpu.VMEM((group * ROWS, 4 * WIN), bf16),
                pltpu.VMEM((group, WIN, 2 * WIN), f32),
                pltpu.VMEM((group // 2, 2 * WIN, 2 * WIN), bf16),
                pltpu.VMEM((group // 2, OFF, 2 * WIN), f32),
                pltpu.VMEM((2 * devices, 8, WIN), f32),
                pltpu.VMEM((steps * group, ROWS, WIN), jnp.int16),
                pltpu.VMEM((devices, 8, WIN), jnp.int16),
                pltpu.SemaphoreType.DMA((steps * group,)),
                pltpu.SemaphoreType.DMA,
            ],
        ),
        out_shape=out_shape,
        input_output_aliases=aliases,
        cost_estimate=pl.CostEstimate(
            flops=steps * group * 1600 * 65536, transcendentals=0, bytes_accessed=steps * group * 90000
        ),
        compiler_params=pltpu.CompilerParams(vmem_limit_bytes=VMEM_GRANT),
        name="scores",
    )(*scalars, away(spectra), away(scale), *[near(c) for c in constants], *[near(p) for p in sources], *kept)


def average_scores(early_codes, late_codes, capacity, quick, chip_amount):
    devices = early_codes.shape[0]
    return pl.pallas_call(
        functools.partial(average_kernel, capacity, quick, chip_amount),
        in_specs=[resident(), resident()],
        out_specs=[resident(), resident(), resident()],
        out_shape=[
            pltpu.VMEM((chip_amount, OFF * OFF), f32),
            pltpu.VMEM((GC, OFF * OFF), f32),
            pltpu.VMEM((GC, OFF * OFF), f32),
        ],
        scratch_shapes=[pltpu.VMEM((ROWS, devices * capacity, WIN), f32)],
        compiler_params=pltpu.CompilerParams(vmem_limit_bytes=VMEM_GRANT),
        name="average",
    )(near(early_codes), near(late_codes))


def finish_kernel(turn, smooth, inner, outer, result):
    edge = smooth.shape[0] - GC
    result[...] = smooth[...]
    for row in range(ROWS):
        lanes = slice(row * WIN, (row + 1) * WIN)
        near, far = inner[:, lanes], outer[:, lanes]
        swap = turn[0] == 1
        result[:GC, lanes] = smooth[:GC, lanes] + jnp.where(swap, near, far) * 0.125
        result[edge:, lanes] = smooth[edge:, lanes] + jnp.where(swap, far, near) * 0.125


def finish(smooth, inner, outer, turn):
    return pl.pallas_call(
        finish_kernel,
        in_specs=[pl.BlockSpec(memory_space=pltpu.SMEM), resident(), resident(), resident()],
        out_shape=jax.ShapeDtypeStruct(smooth.shape, f32),
        compiler_params=pltpu.CompilerParams(vmem_limit_bytes=VMEM_GRANT),
        name="finish",
    )(jnp.full((1,), turn, jnp.int32), smooth, near(inner), near(outer))


def on_device(ref_chips, search_windows, dest_block, dest_slot):
    table = tables()
    chips = ref_chips[0]
    windows = search_windows[0]
    targets = dest_block[0, :, 0]
    slots = dest_slot[0]
    window_amount = windows.shape[0]
    chip_amount = chips.shape[0]
    tiles = lax.axis_size("tile")
    subs = lax.axis_size("sub")
    devices = tiles * subs
    capacity = max(2, 2 * window_amount // devices)

    images = windows.reshape(window_amount, WIN, WIN)
    sub = lax.axis_index("sub")
    sent = spread(chips, tiles).reshape(tiles, chip_amount * ROWS, WIN)
    gathered = lax.all_to_all(sent, "tile", split_axis=0, concat_axis=0, tiled=True)
    gathered = gathered.reshape(tiles * chip_amount, ROWS, WIN)
    sources = [gathered]
    for shift in range(1, subs):
        ring = [(i, (i - shift) % subs) for i in range(subs)]
        sources.append(lax.ppermute(gathered, "sub", ring))

    group = min(SCORE_GROUP, window_amount // 2)
    half = window_amount // group // 2 * group
    quick = max(1, min(capacity - 1, half // devices))
    order = jnp.arange(window_amount, dtype=jnp.int32)
    before = order[:, None] > order[None, :]
    matches = targets[:, None] == targets[None, :]
    ranks = jnp.sum((matches & before).astype(jnp.int32), axis=1)
    late = (ranks >= quick).astype(jnp.int32)
    ahead = (late[None, :] < late[:, None]) | ((late[None, :] == late[:, None]) & before)
    chosen = jnp.sum(ahead.astype(jnp.int32), axis=1)[None, :] == order[:, None]

    def sort(values):
        return jnp.sum(jnp.where(chosen, values[None, :], 0), axis=1)

    place = sort((targets // subs) * chip_amount + slots)
    choice = sort((targets % subs - sub) % subs)
    listing = sort(order)
    spectra, scale = prepare_windows(images, listing, table)
    own = lax.axis_index(("tile", "sub")).astype(jnp.int32)
    position = jnp.stack([own, jnp.full_like(own, half // group)])
    scalars = (choice, place, sort(targets), sort(ranks), sort(slots), position)
    settings = (table, devices, capacity, quick, half)
    early_codes, partial, marks = score_windows(spectra, scale, sources, scalars, *settings, None)
    early_codes = lax.all_to_all(early_codes, ("tile", "sub"), split_axis=0, concat_axis=0, tiled=True)
    (late_codes,) = score_windows(spectra, scale, sources, scalars, *settings, (partial, marks))
    late_codes = lax.all_to_all(late_codes, ("tile", "sub"), split_axis=0, concat_axis=0, tiled=True)
    smooth, first, last = average_scores(early_codes, late_codes, capacity, quick, chip_amount)
    if subs == 2:
        inner = lax.ppermute(jnp.where(sub == 0, last, first), "sub", [(0, 1), (1, 0)])
        ups = [(2 * i + 1, 2 * i + 2) for i in range(tiles - 1)]
        downs = [(2 * i + 2, 2 * i + 1) for i in range(tiles - 1)]
        outer = lax.ppermute(jnp.where(sub == 0, first, last), ("tile", "sub"), ups + downs)
        turn = sub
    else:
        inner = lax.ppermute(first, ("tile", "sub"), [(i + 1, i) for i in range(devices - 1)])
        outer = lax.ppermute(last, ("tile", "sub"), [(i, i + 1) for i in range(devices - 1)])
        turn = 0
    return finish(smooth, inner, outer, turn)[None]


def solution(mesh):
    return jax.shard_map(
        on_device,
        mesh=mesh,
        in_specs=(
            P(("groups", "pair"), ("tile", "sub"), None),
            P(("groups", "pair"), ("tile", "sub"), None),
            P(("groups", "pair"), ("tile", "sub"), None),
            P(("groups", "pair"), ("tile", "sub")),
        ),
        out_specs=P(("groups", "pair"), ("tile", "sub"), None),
        check_vma=False,
    )
```

```python
import functools

import jax
import jax.numpy as jnp
import ml_dtypes
import numpy as np
from jax import lax
from jax.experimental import pallas as pl
from jax.experimental.pallas import tpu as pltpu
from jax.sharding import PartitionSpec as P

CHIP = 64
WIN = 128
GC = 8
OFF = WIN - CHIP
PERIOD = WIN - 1
HALF = WIN // 2
ROWS = OFF * OFF // WIN
GROUP = 8
SCORE_GROUP = 16
VMEM_GRANT = 24 * 1024 * 1024
CODE = 32767.0
epsilon = 1e-06
f32 = jnp.float32
bf16 = jnp.bfloat16


def split_table(table):
    high = table.astype(ml_dtypes.bfloat16)
    low = (table - high.astype(np.float64)).astype(ml_dtypes.bfloat16)
    return (high, low)


def basis():
    freqs = np.arange(HALF)[:, None]
    places = np.arange(WIN)[None, :]
    angle = (freqs * places % PERIOD) * (2.0 * np.pi / PERIOD)
    used = (places < PERIOD).astype(np.float64)
    return (np.cos(angle) * used, np.sin(angle) * used)


def interleaved(table):
    return np.concatenate([table[0::2], table[1::2]], axis=0)


def twice(block):
    zero = np.zeros_like(block)
    return np.block([[block, zero], [zero, block]])


def tables():
    cosine, sine = basis()
    forward = np.concatenate([cosine, sine], axis=0)
    high, low = split_table(forward)
    starts = np.arange(OFF)[:, None]
    places = np.arange(WIN)[None, :]
    band = ((places >= starts) & (places < starts + CHIP)).astype(ml_dtypes.bfloat16)
    rows_band = interleaved(band)
    window_rows = np.concatenate([high, low, rows_band], axis=0)
    square_rows = np.concatenate([rows_band, rows_band], axis=1)
    window_lanes = np.concatenate([high.T, low.T], axis=1)
    window_lanes = np.concatenate([window_lanes, window_lanes], axis=0)
    band_lanes = twice(band.T)

    def pair_of(part):
        return np.concatenate([part[:, 0:CHIP:2], part[:, 1:CHIP:2]], axis=1)

    chip_rows = np.concatenate([pair_of(high), pair_of(high), pair_of(low)], axis=1)
    same = np.concatenate([cosine, cosine], axis=0)[:, :CHIP].T
    cross = np.concatenate([sine, -sine], axis=0)[:, :CHIP].T
    lane_high, lane_low = split_table(twice(np.concatenate([same, cross], axis=1)))
    chip_lanes = np.concatenate([lane_high, lane_high, lane_low], axis=0)
    weight = np.full((2 * HALF, 1), 2.0 / PERIOD)
    weight[0] = 1.0 / PERIOD
    inverse = (forward * weight)[:, :OFF].T
    inv_high, inv_low = split_table(inverse)
    rows_high, rows_low = interleaved(inv_high), interleaved(inv_low)
    inverse_rows = np.block([[rows_high, rows_high], [rows_low, rows_low]])
    inverse_lanes = np.concatenate([twice(inv_high.T), twice(inv_low.T)], axis=1)
    inverse_lanes = np.concatenate([inverse_lanes, inverse_lanes], axis=0)
    return dict(
        window_rows=window_rows, square_rows=square_rows, window_lanes=window_lanes,
        band_lanes=band_lanes, chip_rows=chip_rows, chip_lanes=chip_lanes,
        inverse_rows=inverse_rows, inverse_lanes=inverse_lanes,
    )


def dot(left, right):
    return jnp.dot(left, right, preferred_element_type=f32)


def halves(value):
    high = value.astype(bf16)
    low = (value - high.astype(f32)).astype(bf16)
    return (high, low)


def thirds(value):
    high = value.astype(bf16)
    rest = value - high.astype(f32)
    middle = rest.astype(bf16)
    low = (rest - middle.astype(f32)).astype(bf16)
    return (high, middle, low)


def window_kernel(windows, window_rows, square_rows, window_lanes, band_lanes, spectra, scale):
    group = windows.shape[0]
    for first in range(0, group, 2):
        image = jnp.concatenate([windows[first], windows[first + 1]], axis=1)
        rows = dot(window_rows[...], image)
        spec_rows = rows[:WIN] + rows[WIN:2 * WIN]
        sums = rows[2 * WIN:]
        wide = image.astype(f32)
        square_high, square_low = halves(wide * wide)
        squares = dot(square_rows[...], jnp.concatenate([square_high, square_low], axis=0))
        for part in range(2):
            lanes = slice(part * WIN, (part + 1) * WIN)
            high, low = halves(spec_rows[:, lanes])
            both = dot(jnp.concatenate([high, low], axis=1), window_lanes[...])
            spectra[first + part] = both[:, :WIN] + both[:, WIN:]
            pieces = []
            for source in (sums, squares):
                own = source[:, lanes]
                packed = jnp.concatenate([own[:ROWS], own[ROWS:]], axis=1)
                pieces.extend(thirds(packed))
            boxed = dot(jnp.concatenate(pieces, axis=0), band_lanes[...])
            boxes = [boxed[i * ROWS:(i + 1) * ROWS] for i in range(6)]
            mean = (boxes[0] + boxes[1] + boxes[2]) * (1.0 / (CHIP * CHIP))
            second = (boxes[3] + boxes[4] + boxes[5]) * (1.0 / (CHIP * CHIP))
            variance = second - mean * mean
            scale[first + part] = lax.rsqrt(variance + epsilon)


def score_kernel(
    capacity, choice, place, target, ranks, slots, position,
    spectra, scale, chip_lanes, chip_rows, inverse_rows, inverse_lanes, *rest,
):
    (*sources, out, marks, lefts, lines, packs, pairs, products, backs,
     images, levels, stage, note_stage, in_sems, out_sems, note_sem) = rest
    step = pl.program_id(0)
    steps = pl.num_programs(0)
    group = lefts.shape[0] // ROWS
    base = step * group
    slot = step % 2
    body = capacity * ROWS
    lane = lax.broadcasted_iota(jnp.int32, (8, WIN), 1)
    line = lax.broadcasted_iota(jnp.int32, (8, WIN), 0)

    def incoming(index, to):
        rows = pl.ds(pl.multiple_of(index * group, group), group)
        return (
            pltpu.make_async_copy(spectra.at[rows], images.at[to], in_sems.at[to, 0]),
            pltpu.make_async_copy(scale.at[rows], levels.at[to], in_sems.at[to, 1]),
        )

    @pl.when(step == 0)
    def _():
        for copy in incoming(0, 0):
            copy.start()
        marks[...] = jnp.zeros_like(marks)

    @pl.when(step < steps - 1)
    def _():
        for copy in incoming(step + 1, 1 - slot):
            copy.start()

    raws = []
    for part in range(group):
        window = base + part
        raw = sources[0][place[window]]
        for index in range(1, len(sources)):
            raw = jnp.where(choice[window] == index, sources[index][place[window]], raw)
        raws.append(raw.astype(f32))
    total = jnp.concatenate([jnp.sum(raw, axis=0, keepdims=True) for raw in raws], axis=0)
    mean = jnp.sum(total, axis=1, keepdims=True) * (1.0 / (CHIP * CHIP))
    raws = [raws[part] - mean[part:part + 1] for part in range(group)]
    total = jnp.concatenate([jnp.sum(raw * raw, axis=0, keepdims=True) for raw in raws], axis=0)
    power = jnp.sum(total, axis=1, keepdims=True) * (1.0 / (CHIP * CHIP))
    gain = lax.rsqrt(power + epsilon) * (1.0 / CHIP)
    for part in range(group):
        own = slice(part * ROWS, (part + 1) * ROWS)
        high, low = halves(raws[part])
        lefts[own, :WIN] = high
        lefts[own, WIN:2 * WIN] = low
        lefts[own, 2 * WIN:] = high
    lines[...] = dot(lefts[...], chip_lanes[...])

    def chip_spectrum(part):
        high, low = halves(lines[part * ROWS:(part + 1) * ROWS, :])
        pieces = [high[:, :2 * WIN], high[:, 2 * WIN:], low[:, :2 * WIN], low[:, 2 * WIN:]]
        pairs[part] = dot(chip_rows[...], jnp.concatenate(pieces + pieces[:2], axis=0))

    def multiply(part):
        lanes = slice(part % 2 * WIN, (part % 2 + 1) * WIN)
        for row in range(0, HALF, 32):
            upper, lower = slice(row, row + 32), slice(HALF + row, HALF + row + 32)
            own_c, own_s = images[slot, part, upper], images[slot, part, lower]
            turned_c, turned_s = pltpu.roll(own_c, HALF, 1), pltpu.roll(own_s, HALF, 1)
            same_c, same_s = pairs[part, upper, :WIN], pairs[part, lower, :WIN]
            cross_c, cross_s = pairs[part, upper, WIN:], pairs[part, lower, WIN:]
            out_c = same_c * own_c + cross_c * turned_c + same_s * own_s + cross_s * turned_s
            out_s = same_c * own_s + cross_c * turned_s - same_s * own_c - cross_s * turned_c
            for value, place_to in ((out_c, row), (out_s, HALF + row)):
                high, low = halves(value)
                products[part // 2, place_to:place_to + 32, lanes] = high
                products[part // 2, WIN + place_to:WIN + place_to + 32, lanes] = low

    def invert(pair):
        back = dot(inverse_rows[...], products[pair])
        backs[pair] = back[:OFF] + back[OFF:]

    def pack(pair):
        for part in (2 * pair, 2 * pair + 1):
            lanes = slice(part % 2 * WIN, (part % 2 + 1) * WIN)
            own = slice(part * ROWS, (part + 1) * ROWS)
            high, low = halves(backs[pair, :, lanes])
            packs[own, :WIN] = high[:ROWS]
            packs[own, WIN:2 * WIN] = high[ROWS:]
            packs[own, 2 * WIN:3 * WIN] = low[:ROWS]
            packs[own, 3 * WIN:] = low[ROWS:]

    for copy in incoming(step, slot):
        copy.wait()
    for part in range(group + 4):
        if part < group:
            chip_spectrum(part)
        if 2 <= part < group + 2:
            multiply(part - 2)
            if part % 2 == 1:
                invert((part - 2) // 2)
        if part >= 4 and part % 2 == 1:
            pack((part - 4) // 2)
    both = dot(packs[...], inverse_lanes[...])
    scores = []
    for part in range(group):
        own = slice(part * ROWS, (part + 1) * ROWS)
        numerator = both[own, :WIN] + both[own, WIN:]
        scores.append(numerator * (levels[slot, part] * gain[part:part + 1]))
    largest = jnp.concatenate([jnp.max(jnp.abs(score), axis=0, keepdims=True) for score in scores], axis=0)
    largest = jnp.max(largest, axis=1, keepdims=True)
    power = jnp.ceil(jnp.log2(jnp.maximum(largest, 1e-30)))
    shrink = jnp.exp2(-power).astype(bf16).astype(f32)
    for part in range(group):
        window = base + part
        score = scores[part]
        size = jnp.maximum(jnp.abs(score) * shrink[part:part + 1], 1e-30)
        root = size * lax.rsqrt(size) * CODE
        root = jnp.minimum(root, CODE)
        code = jnp.round(jnp.where(score < 0, -root, root)).astype(jnp.int32).astype(jnp.int16)
        to = target[window]
        stage[window] = code
        here = lane == position[0] * capacity + ranks[window]
        named = (slots[window] + 1).astype(f32)
        mark = jnp.where(line == 0, named, jnp.where(line == 1, power[part:part + 1], 0.0))
        marks[to] = marks[to] + jnp.where(here, mark, 0.0)
    for part in range(group):
        window = base + part
        rows = pl.ds(pl.multiple_of(ranks[window] * ROWS, ROWS), ROWS)
        pltpu.make_async_copy(stage.at[window], out.at[target[window], rows, :], out_sems.at[window]).start()

    @pl.when(step == steps - 1)
    def _():
        note_stage[...] = marks[...].astype(jnp.int32).astype(jnp.int16)
        notes = pltpu.make_async_copy(note_stage, out.at[:, body:, :], note_sem)
        notes.start()
        for window in range(stage.shape[0]):
            pltpu.make_async_copy(stage.at[window], out.at[0, :ROWS, :], out_sems.at[window]).wait()
        notes.wait()


def average_kernel(capacity, chip_amount, codes, smooth, first, last, values):
    devices = codes.shape[0]
    body = capacity * ROWS
    slots = devices * capacity
    notes = codes[0, body:, :].astype(jnp.int32).astype(f32)
    for source in range(1, devices):
        notes = notes + codes[source, body:, :].astype(jnp.int32).astype(f32)
    for source in range(devices):
        wide = codes[source, :body, :].astype(jnp.int32).astype(f32)
        turned = jnp.swapaxes((wide * jnp.abs(wide)).reshape(capacity, ROWS, WIN), 0, 1)
        values[:, source * capacity:(source + 1) * capacity, :] = turned
    chip = lax.broadcasted_iota(jnp.int32, (chip_amount, WIN), 0)
    hit = (notes[0:1] - 1.0).astype(jnp.int32) == chip
    looks = jnp.sum(hit.astype(f32), axis=1, keepdims=True)
    weight = jnp.where(hit, jnp.exp2(notes[1:2]), 0.0).astype(bf16)[:, :slots]
    weight = jnp.concatenate([weight, weight], axis=1)
    factor = 1.0 / (jnp.maximum(looks, 1.0) * (CODE * CODE))
    factor = jnp.broadcast_to(factor, (chip_amount, WIN))
    column = chip % GC
    zero = jnp.zeros((GC, WIN), f32)
    for row in range(ROWS):
        high, low = halves(values[row])
        average = dot(weight, jnp.concatenate([high, low], axis=0)) * factor
        lanes = slice(row * WIN, (row + 1) * WIN)
        first[:, lanes] = average[:GC]
        last[:, lanes] = average[chip_amount - GC:]
        below = jnp.concatenate([average[GC:], zero], axis=0)
        above = jnp.concatenate([zero, average[:-GC]], axis=0)
        left = jnp.where(column == 0, 0.0, pltpu.roll(average, 1, 0))
        right = jnp.where(column == GC - 1, 0.0, pltpu.roll(average, chip_amount - 1, 0))
        smooth[:, lanes] = (4.0 * average + above + below + left + right) * 0.125


def resident():
    return pl.BlockSpec(memory_space=pltpu.VMEM)


def away(array):
    return pltpu.with_memory_space_constraint(array, pltpu.HBM)


def near(array):
    return pltpu.with_memory_space_constraint(array, pltpu.VMEM)


def spread_kernel(chips, sent):
    chip_amount = chips.shape[0]
    for first in range(0, chip_amount, 8):
        for row in range(0, ROWS, 8):
            lanes = [chips[first:first + 8, (row + i) * WIN:(row + i + 1) * WIN].astype(f32) for i in range(8)]
            turned = jnp.swapaxes(jnp.stack(lanes, axis=0), 0, 1).astype(bf16)
            for to in range(sent.shape[0]):
                sent[to, first:first + 8, row:row + 8, :] = turned


def spread(chips, tiles):
    return pl.pallas_call(
        spread_kernel,
        in_specs=[resident()],
        out_specs=resident(),
        out_shape=pltpu.VMEM((tiles, chips.shape[0], ROWS, WIN), bf16),
        compiler_params=pltpu.CompilerParams(vmem_limit_bytes=VMEM_GRANT),
        name="spread",
    )(chips)


def prepare_windows(images, table):
    amount = images.shape[0]
    group = min(GROUP, amount)
    constants = [jnp.asarray(table[k]) for k in ("window_rows", "square_rows", "window_lanes", "band_lanes")]
    return pl.pallas_call(
        window_kernel,
        grid=(amount // group,),
        in_specs=[pl.BlockSpec((group, WIN, WIN), lambda i: (i, 0, 0))] + [resident() for _ in constants],
        out_specs=[
            pl.BlockSpec((group, WIN, WIN), lambda i: (i, 0, 0)),
            pl.BlockSpec((group, ROWS, WIN), lambda i: (i, 0, 0)),
        ],
        out_shape=[
            pltpu.HBM((amount, WIN, WIN), f32),
            pltpu.HBM((amount, ROWS, WIN), f32),
        ],
        cost_estimate=pl.CostEstimate(
            flops=amount * 2 * 900 * 65536, transcendentals=amount * ROWS * WIN, bytes_accessed=amount * 120000
        ),
        compiler_params=pltpu.CompilerParams(vmem_limit_bytes=VMEM_GRANT),
        name="window_spectra",
    )(images, *constants)


def score_windows(spectra, scale, sources, scalars, table, devices, capacity):
    amount = spectra.shape[0]
    group = min(SCORE_GROUP, amount)
    constants = [jnp.asarray(table[k]) for k in ("chip_lanes", "chip_rows", "inverse_rows", "inverse_lanes")]
    shape = (devices, capacity * ROWS + 8, WIN)
    return pl.pallas_call(
        functools.partial(score_kernel, capacity),
        grid_spec=pltpu.PrefetchScalarGridSpec(
            num_scalar_prefetch=len(scalars),
            grid=(amount // group,),
            in_specs=[
                pl.BlockSpec(memory_space=pl.ANY), pl.BlockSpec(memory_space=pl.ANY),
            ] + [resident() for _ in constants] + [resident() for _ in sources],
            out_specs=pl.BlockSpec(memory_space=pl.ANY),
            scratch_shapes=[
                pltpu.VMEM((devices, 8, WIN), f32),
                pltpu.VMEM((group * ROWS, 3 * WIN), bf16),
                pltpu.VMEM((group * ROWS, 4 * WIN), f32),
                pltpu.VMEM((group * ROWS, 4 * WIN), bf16),
                pltpu.VMEM((group, WIN, 2 * WIN), f32),
                pltpu.VMEM((group // 2, 2 * WIN, 2 * WIN), bf16),
                pltpu.VMEM((group // 2, OFF, 2 * WIN), f32),
                pltpu.VMEM((2, group, WIN, WIN), f32),
                pltpu.VMEM((2, group, ROWS, WIN), f32),
                pltpu.VMEM((amount, ROWS, WIN), jnp.int16),
                pltpu.VMEM((devices, 8, WIN), jnp.int16),
                pltpu.SemaphoreType.DMA((2, 2)),
                pltpu.SemaphoreType.DMA((amount,)),
                pltpu.SemaphoreType.DMA,
            ],
        ),
        out_shape=jax.ShapeDtypeStruct(shape, jnp.int16),
        compiler_params=pltpu.CompilerParams(vmem_limit_bytes=VMEM_GRANT),
        name="scores",
    )(*scalars, away(spectra), away(scale), *[near(c) for c in constants], *[near(source) for source in sources])


def average_scores(codes, capacity, chip_amount):
    devices = codes.shape[0]
    return pl.pallas_call(
        functools.partial(average_kernel, capacity, chip_amount),
        in_specs=[resident()],
        out_specs=[resident(), resident(), resident()],
        out_shape=[
            pltpu.VMEM((chip_amount, OFF * OFF), f32),
            pltpu.VMEM((GC, OFF * OFF), f32),
            pltpu.VMEM((GC, OFF * OFF), f32),
        ],
        scratch_shapes=[pltpu.VMEM((ROWS, devices * capacity, WIN), f32)],
        compiler_params=pltpu.CompilerParams(vmem_limit_bytes=VMEM_GRANT),
        name="average",
    )(near(codes))


def finish_kernel(turn, smooth, inner, outer, result):
    edge = smooth.shape[0] - GC
    result[...] = smooth[...]
    for row in range(ROWS):
        lanes = slice(row * WIN, (row + 1) * WIN)
        near, far = inner[:, lanes], outer[:, lanes]
        swap = turn[0] == 1
        result[:GC, lanes] = smooth[:GC, lanes] + jnp.where(swap, near, far) * 0.125
        result[edge:, lanes] = smooth[edge:, lanes] + jnp.where(swap, far, near) * 0.125


def finish(smooth, inner, outer, turn):
    return pl.pallas_call(
        finish_kernel,
        in_specs=[pl.BlockSpec(memory_space=pltpu.SMEM), resident(), resident(), resident()],
        out_shape=jax.ShapeDtypeStruct(smooth.shape, f32),
        compiler_params=pltpu.CompilerParams(vmem_limit_bytes=VMEM_GRANT),
        name="finish",
    )(jnp.full((1,), turn, jnp.int32), smooth, near(inner), near(outer))


def on_device(ref_chips, search_windows, dest_block, dest_slot):
    table = tables()
    chips = ref_chips[0]
    windows = search_windows[0]
    targets = dest_block[0, :, 0]
    slots = dest_slot[0]
    window_amount = windows.shape[0]
    chip_amount = chips.shape[0]
    tiles = lax.axis_size("tile")
    subs = lax.axis_size("sub")
    devices = tiles * subs
    capacity = max(2, 2 * window_amount // devices)

    images = windows.reshape(window_amount, WIN, WIN)
    sub = lax.axis_index("sub")
    sent = spread(chips, tiles).reshape(tiles, chip_amount * ROWS, WIN)
    gathered = lax.all_to_all(sent, "tile", split_axis=0, concat_axis=0, tiled=True)
    gathered = gathered.reshape(tiles * chip_amount, ROWS, WIN)
    spectra, scale = prepare_windows(images, table)
    sources = [gathered]
    for shift in range(1, subs):
        ring = [(i, (i - shift) % subs) for i in range(subs)]
        sources.append(lax.ppermute(gathered, "sub", ring))

    order = jnp.arange(window_amount, dtype=jnp.int32)
    matches = targets[:, None] == targets[None, :]
    earlier = order[:, None] > order[None, :]
    ranks = jnp.sum((matches & earlier).astype(jnp.int32), axis=1)
    choice = (targets % subs - sub) % subs
    place = (targets // subs) * chip_amount + slots
    position = jnp.full((1,), lax.axis_index(("tile", "sub")), jnp.int32)
    scalars = (choice, place, targets, ranks, slots, position)
    codes = score_windows(spectra, scale, sources, scalars, table, devices, capacity)

    received = lax.all_to_all(codes, ("tile", "sub"), split_axis=0, concat_axis=0, tiled=True)
    smooth, first, last = average_scores(received, capacity, chip_amount)
    if subs == 2:
        inner = lax.ppermute(jnp.where(sub == 0, last, first), "sub", [(0, 1), (1, 0)])
        ups = [(2 * i + 1, 2 * i + 2) for i in range(tiles - 1)]
        downs = [(2 * i + 2, 2 * i + 1) for i in range(tiles - 1)]
        outer = lax.ppermute(jnp.where(sub == 0, first, last), ("tile", "sub"), ups + downs)
        turn = sub
    else:
        inner = lax.ppermute(first, ("tile", "sub"), [(i + 1, i) for i in range(devices - 1)])
        outer = lax.ppermute(last, ("tile", "sub"), [(i, i + 1) for i in range(devices - 1)])
        turn = 0
    return finish(smooth, inner, outer, turn)[None]


def solution(mesh):
    return jax.shard_map(
        on_device,
        mesh=mesh,
        in_specs=(
            P(("groups", "pair"), ("tile", "sub"), None),
            P(("groups", "pair"), ("tile", "sub"), None),
            P(("groups", "pair"), ("tile", "sub"), None),
            P(("groups", "pair"), ("tile", "sub")),
        ),
        out_specs=P(("groups", "pair"), ("tile", "sub"), None),
        check_vma=False,
    )
```

```python
import functools

import jax
import jax.numpy as jnp
import ml_dtypes
import numpy as np
from jax import lax
from jax.experimental import pallas as pl
from jax.experimental.pallas import tpu as pltpu
from jax.sharding import PartitionSpec as P

CHIP = 64
WIN = 128
GC = 8
OFF = WIN - CHIP
PERIOD = WIN - 1
HALF = WIN // 2
ROWS = OFF * OFF // WIN
GROUP = 8
SCORE_GROUP = 16
VMEM_GRANT = 24 * 1024 * 1024
CODE = 32767.0
epsilon = 1e-06
f32 = jnp.float32
bf16 = jnp.bfloat16


def split_table(table):
    high = table.astype(ml_dtypes.bfloat16)
    low = (table - high.astype(np.float64)).astype(ml_dtypes.bfloat16)
    return (high, low)


def basis():
    freqs = np.arange(HALF)[:, None]
    places = np.arange(WIN)[None, :]
    angle = (freqs * places % PERIOD) * (2.0 * np.pi / PERIOD)
    used = (places < PERIOD).astype(np.float64)
    return (np.cos(angle) * used, np.sin(angle) * used)


def interleaved(table):
    return np.concatenate([table[0::2], table[1::2]], axis=0)


def twice(block):
    zero = np.zeros_like(block)
    return np.block([[block, zero], [zero, block]])


def tables():
    cosine, sine = basis()
    forward = np.concatenate([cosine, sine], axis=0)
    high, low = split_table(forward)
    starts = np.arange(OFF)[:, None]
    places = np.arange(WIN)[None, :]
    band = ((places >= starts) & (places < starts + CHIP)).astype(ml_dtypes.bfloat16)
    rows_band = interleaved(band)
    window_rows = np.concatenate([high, low, rows_band], axis=0)
    square_rows = np.concatenate([rows_band, rows_band], axis=1)
    window_lanes = np.concatenate([high.T, low.T], axis=1)
    window_lanes = np.concatenate([window_lanes, window_lanes], axis=0)
    band_lanes = twice(band.T)

    def pair_of(part):
        return np.concatenate([part[:, 0:CHIP:2], part[:, 1:CHIP:2]], axis=1)

    chip_rows = np.concatenate([pair_of(high), pair_of(high), pair_of(low)], axis=1)
    same = np.concatenate([cosine, cosine], axis=0)[:, :CHIP].T
    cross = np.concatenate([sine, -sine], axis=0)[:, :CHIP].T
    lane_high, lane_low = split_table(np.concatenate([same, cross], axis=1))
    none = np.zeros_like(lane_low)
    even_lanes = np.concatenate([lane_high, lane_high, lane_low, none], axis=0)
    odd_lanes = np.concatenate([none, lane_low, lane_high, lane_high], axis=0)
    chip_lanes = np.concatenate([even_lanes, odd_lanes], axis=1)
    weight = np.full((2 * HALF, 1), 2.0 / PERIOD)
    weight[0] = 1.0 / PERIOD
    inverse = (forward * weight)[:, :OFF].T
    inv_high, inv_low = split_table(inverse)
    rows_high, rows_low = interleaved(inv_high), interleaved(inv_low)
    inverse_rows = np.block([[rows_high, rows_high], [rows_low, rows_low]])
    inverse_lanes = np.concatenate([twice(inv_high.T), twice(inv_low.T)], axis=1)
    inverse_lanes = np.concatenate([inverse_lanes, inverse_lanes], axis=0)
    return dict(
        window_rows=window_rows, square_rows=square_rows, window_lanes=window_lanes,
        band_lanes=band_lanes, chip_rows=chip_rows, chip_lanes=chip_lanes,
        inverse_rows=inverse_rows, inverse_lanes=inverse_lanes,
    )


def dot(left, right):
    return jnp.dot(left, right, preferred_element_type=f32)


def halves(value):
    high = value.astype(bf16)
    low = (value - high.astype(f32)).astype(bf16)
    return (high, low)


def thirds(value):
    high = value.astype(bf16)
    rest = value - high.astype(f32)
    middle = rest.astype(bf16)
    low = (rest - middle.astype(f32)).astype(bf16)
    return (high, middle, low)


def window_kernel(windows, window_rows, square_rows, window_lanes, band_lanes, spectra, scale):
    group = windows.shape[0]
    for first in range(0, group, 2):
        image = jnp.concatenate([windows[first], windows[first + 1]], axis=1)
        rows = dot(window_rows[...], image)
        spec_rows = rows[:WIN] + rows[WIN:2 * WIN]
        sums = rows[2 * WIN:]
        wide = image.astype(f32)
        square_high, square_low = halves(wide * wide)
        squares = dot(square_rows[...], jnp.concatenate([square_high, square_low], axis=0))
        for part in range(2):
            lanes = slice(part * WIN, (part + 1) * WIN)
            high, low = halves(spec_rows[:, lanes])
            both = dot(jnp.concatenate([high, low], axis=1), window_lanes[...])
            spectra[first + part] = both[:, :WIN] + both[:, WIN:]
            pieces = []
            for source in (sums, squares):
                own = source[:, lanes]
                packed = jnp.concatenate([own[:ROWS], own[ROWS:]], axis=1)
                pieces.extend(thirds(packed))
            boxed = dot(jnp.concatenate(pieces, axis=0), band_lanes[...])
            boxes = [boxed[i * ROWS:(i + 1) * ROWS] for i in range(6)]
            mean = (boxes[0] + boxes[1] + boxes[2]) * (1.0 / (CHIP * CHIP))
            second = (boxes[3] + boxes[4] + boxes[5]) * (1.0 / (CHIP * CHIP))
            variance = second - mean * mean
            scale[first + part] = lax.rsqrt(variance + epsilon)


def score_kernel(
    capacity, choice, place, target, ranks, slots, position,
    spectra, scale, chip_lanes, chip_rows, inverse_rows, inverse_lanes, *rest,
):
    *sources, out, marks, lefts, lines, packs, pairs, products, backs = rest
    step = pl.program_id(0)
    group = lefts.shape[0] // ROWS
    base = step * group
    body = capacity * ROWS
    lane = lax.broadcasted_iota(jnp.int32, (8, WIN), 1)
    line = lax.broadcasted_iota(jnp.int32, (8, WIN), 0)

    @pl.when(step == 0)
    def _():
        marks[...] = jnp.zeros_like(marks)

    even = lax.broadcasted_iota(jnp.int32, (ROWS, WIN), 1) < CHIP
    raws = []
    for part in range(group):
        window = base + part
        raw = sources[0][place[window]]
        for index in range(1, len(sources)):
            raw = jnp.where(choice[window] == index, sources[index][place[window]], raw)
        raws.append(raw.astype(f32))
    total = jnp.concatenate([jnp.sum(raw, axis=0, keepdims=True) for raw in raws], axis=0)
    mean = jnp.sum(total, axis=1, keepdims=True) * (1.0 / (CHIP * CHIP))
    raws = [raws[part] - mean[part:part + 1] for part in range(group)]
    total = jnp.concatenate([jnp.sum(raw * raw, axis=0, keepdims=True) for raw in raws], axis=0)
    power = jnp.sum(total, axis=1, keepdims=True) * (1.0 / (CHIP * CHIP))
    gain = lax.rsqrt(power + epsilon) * (1.0 / CHIP)
    for part in range(group):
        own = slice(part * ROWS, (part + 1) * ROWS)
        high = raws[part].astype(bf16).astype(f32)
        low = raws[part] - high
        lefts[own, :WIN] = jnp.where(even, high, pltpu.roll(low, CHIP, 1)).astype(bf16)
        lefts[own, WIN:2 * WIN] = high.astype(bf16)
        lefts[own, 2 * WIN:] = jnp.where(even, pltpu.roll(high, CHIP, 1), low).astype(bf16)
    lines[:, :2 * WIN] = dot(lefts[:, :2 * WIN], chip_lanes[:, :2 * WIN])
    lines[:, 2 * WIN:] = dot(lefts[:, WIN:], chip_lanes[:, 2 * WIN:])

    def chip_spectrum(part):
        high, low = halves(lines[part * ROWS:(part + 1) * ROWS, :])
        pieces = [high[:, :2 * WIN], high[:, 2 * WIN:], low[:, :2 * WIN], low[:, 2 * WIN:]]
        pairs[part] = dot(chip_rows[...], jnp.concatenate(pieces + pieces[:2], axis=0))

    def multiply(part):
        lanes = slice(part % 2 * WIN, (part % 2 + 1) * WIN)
        for row in range(0, HALF, 32):
            upper, lower = slice(row, row + 32), slice(HALF + row, HALF + row + 32)
            own_c, own_s = spectra[part, upper], spectra[part, lower]
            turned_c, turned_s = pltpu.roll(own_c, HALF, 1), pltpu.roll(own_s, HALF, 1)
            same_c, same_s = pairs[part, upper, :WIN], pairs[part, lower, :WIN]
            cross_c, cross_s = pairs[part, upper, WIN:], pairs[part, lower, WIN:]
            out_c = same_c * own_c + cross_c * turned_c + same_s * own_s + cross_s * turned_s
            out_s = same_c * own_s + cross_c * turned_s - same_s * own_c - cross_s * turned_c
            for value, place_to in ((out_c, row), (out_s, HALF + row)):
                high, low = halves(value)
                products[part // 2, place_to:place_to + 32, lanes] = high
                products[part // 2, WIN + place_to:WIN + place_to + 32, lanes] = low

    def invert(pair):
        back = dot(inverse_rows[...], products[pair])
        backs[pair] = back[:OFF] + back[OFF:]

    def pack(pair):
        for part in (2 * pair, 2 * pair + 1):
            lanes = slice(part % 2 * WIN, (part % 2 + 1) * WIN)
            own = slice(part * ROWS, (part + 1) * ROWS)
            high, low = halves(backs[pair, :, lanes])
            packs[own, :WIN] = high[:ROWS]
            packs[own, WIN:2 * WIN] = high[ROWS:]
            packs[own, 2 * WIN:3 * WIN] = low[:ROWS]
            packs[own, 3 * WIN:] = low[ROWS:]

    for part in range(group + 4):
        if part < group:
            chip_spectrum(part)
        if 2 <= part < group + 2:
            multiply(part - 2)
            if part % 2 == 1:
                invert((part - 2) // 2)
        if part >= 4 and part % 2 == 1:
            pack((part - 4) // 2)
    both = dot(packs[...], inverse_lanes[...])
    scores = []
    for part in range(group):
        own = slice(part * ROWS, (part + 1) * ROWS)
        numerator = both[own, :WIN] + both[own, WIN:]
        scores.append(numerator * (scale[part] * gain[part:part + 1]))
    largest = jnp.concatenate([jnp.max(jnp.abs(score), axis=0, keepdims=True) for score in scores], axis=0)
    largest = jnp.max(largest, axis=1, keepdims=True)
    power = jnp.ceil(jnp.log2(jnp.maximum(largest, 1e-30)))
    shrink = jnp.exp2(-power).astype(bf16).astype(f32)
    for part in range(group):
        window = base + part
        score = scores[part]
        size = jnp.maximum(jnp.abs(score) * shrink[part:part + 1], 1e-30)
        root = size * lax.rsqrt(size) * CODE
        root = jnp.minimum(root, CODE)
        code = jnp.round(jnp.where(score < 0, -root, root)).astype(jnp.int32).astype(jnp.int16)
        to = target[window]
        out[to, pl.ds(pl.multiple_of(ranks[window] * ROWS, ROWS), ROWS), :] = code
        here = lane == position[0] * capacity + ranks[window]
        named = (slots[window] + 1).astype(f32)
        mark = jnp.where(line == 0, named, jnp.where(line == 1, power[part:part + 1], 0.0))
        marks[to] = marks[to] + jnp.where(here, mark, 0.0)

    @pl.when(step == pl.num_programs(0) - 1)
    def _():
        for to in range(out.shape[0]):
            out[to, body:, :] = marks[to].astype(jnp.int32).astype(jnp.int16)


def average_kernel(capacity, chip_amount, codes, smooth, first, last, values):
    devices = codes.shape[0]
    body = capacity * ROWS
    slots = devices * capacity
    notes = codes[0, body:, :].astype(jnp.int32).astype(f32)
    for source in range(1, devices):
        notes = notes + codes[source, body:, :].astype(jnp.int32).astype(f32)
    for source in range(devices):
        wide = codes[source, :body, :].astype(jnp.int32).astype(f32)
        turned = jnp.swapaxes((wide * jnp.abs(wide)).reshape(capacity, ROWS, WIN), 0, 1)
        values[:, source * capacity:(source + 1) * capacity, :] = turned
    chip = lax.broadcasted_iota(jnp.int32, (chip_amount, WIN), 0)
    hit = (notes[0:1] - 1.0).astype(jnp.int32) == chip
    looks = jnp.sum(hit.astype(f32), axis=1, keepdims=True)
    weight = jnp.where(hit, jnp.exp2(notes[1:2]), 0.0).astype(bf16)[:, :slots]
    weight = jnp.concatenate([weight, weight], axis=1)
    factor = 1.0 / (jnp.maximum(looks, 1.0) * (CODE * CODE))
    factor = jnp.broadcast_to(factor, (chip_amount, WIN))
    column = chip % GC
    zero = jnp.zeros((GC, WIN), f32)
    for row in range(ROWS):
        high, low = halves(values[row])
        average = dot(weight, jnp.concatenate([high, low], axis=0)) * factor
        lanes = slice(row * WIN, (row + 1) * WIN)
        first[:, lanes] = average[:GC]
        last[:, lanes] = average[chip_amount - GC:]
        below = jnp.concatenate([average[GC:], zero], axis=0)
        above = jnp.concatenate([zero, average[:-GC]], axis=0)
        left = jnp.where(column == 0, 0.0, pltpu.roll(average, 1, 0))
        right = jnp.where(column == GC - 1, 0.0, pltpu.roll(average, chip_amount - 1, 0))
        smooth[:, lanes] = (4.0 * average + above + below + left + right) * 0.125


def resident():
    return pl.BlockSpec(memory_space=pltpu.VMEM)


def away(array):
    return pltpu.with_memory_space_constraint(array, pltpu.HBM)


def near(array):
    return pltpu.with_memory_space_constraint(array, pltpu.VMEM)


def spread_kernel(chips, sent):
    chip_amount = chips.shape[0]
    for first in range(0, chip_amount, 8):
        for row in range(0, ROWS, 8):
            lanes = [chips[first:first + 8, (row + i) * WIN:(row + i + 1) * WIN].astype(f32) for i in range(8)]
            turned = jnp.swapaxes(jnp.stack(lanes, axis=0), 0, 1).astype(bf16)
            for to in range(sent.shape[0]):
                sent[to, first:first + 8, row:row + 8, :] = turned


def spread(chips, tiles):
    return pl.pallas_call(
        spread_kernel,
        in_specs=[resident()],
        out_specs=resident(),
        out_shape=pltpu.VMEM((tiles, chips.shape[0], ROWS, WIN), bf16),
        compiler_params=pltpu.CompilerParams(vmem_limit_bytes=VMEM_GRANT),
        name="spread",
    )(chips)


def prepare_windows(images, table):
    amount = images.shape[0]
    group = min(GROUP, amount)
    constants = [jnp.asarray(table[k]) for k in ("window_rows", "square_rows", "window_lanes", "band_lanes")]
    return pl.pallas_call(
        window_kernel,
        grid=(amount // group,),
        in_specs=[pl.BlockSpec((group, WIN, WIN), lambda i: (i, 0, 0))] + [resident() for _ in constants],
        out_specs=[
            pl.BlockSpec((group, WIN, WIN), lambda i: (i, 0, 0)),
            pl.BlockSpec((group, ROWS, WIN), lambda i: (i, 0, 0)),
        ],
        out_shape=[
            pltpu.HBM((amount, WIN, WIN), f32),
            pltpu.HBM((amount, ROWS, WIN), f32),
        ],
        cost_estimate=pl.CostEstimate(
            flops=amount * 2 * 900 * 65536, transcendentals=amount * ROWS * WIN, bytes_accessed=amount * 120000
        ),
        compiler_params=pltpu.CompilerParams(vmem_limit_bytes=VMEM_GRANT),
        name="window_spectra",
    )(images, *constants)


def score_windows(spectra, scale, sources, scalars, table, devices, capacity):
    amount = spectra.shape[0]
    group = min(SCORE_GROUP, amount)
    constants = [jnp.asarray(table[k]) for k in ("chip_lanes", "chip_rows", "inverse_rows", "inverse_lanes")]
    shape = (devices, capacity * ROWS + 8, WIN)
    return pl.pallas_call(
        functools.partial(score_kernel, capacity),
        grid_spec=pltpu.PrefetchScalarGridSpec(
            num_scalar_prefetch=len(scalars),
            grid=(amount // group,),
            in_specs=[
                pl.BlockSpec((group, WIN, WIN), lambda i, *_: (i, 0, 0)),
                pl.BlockSpec((group, ROWS, WIN), lambda i, *_: (i, 0, 0)),
            ] + [resident() for _ in constants] + [resident() for _ in sources],
            out_specs=resident(),
            scratch_shapes=[
                pltpu.VMEM((devices, 8, WIN), f32),
                pltpu.VMEM((group * ROWS, 3 * WIN), bf16),
                pltpu.VMEM((group * ROWS, 4 * WIN), f32),
                pltpu.VMEM((group * ROWS, 4 * WIN), bf16),
                pltpu.VMEM((group, WIN, 2 * WIN), f32),
                pltpu.VMEM((group // 2, 2 * WIN, 2 * WIN), bf16),
                pltpu.VMEM((group // 2, OFF, 2 * WIN), f32),
            ],
        ),
        out_shape=pltpu.VMEM(shape, jnp.int16),
        compiler_params=pltpu.CompilerParams(vmem_limit_bytes=VMEM_GRANT),
        name="scores",
    )(*scalars, away(spectra), away(scale), *[near(c) for c in constants], *[near(source) for source in sources])


def average_scores(codes, capacity, chip_amount):
    devices = codes.shape[0]
    return pl.pallas_call(
        functools.partial(average_kernel, capacity, chip_amount),
        in_specs=[resident()],
        out_specs=[resident(), resident(), resident()],
        out_shape=[
            pltpu.VMEM((chip_amount, OFF * OFF), f32),
            pltpu.VMEM((GC, OFF * OFF), f32),
            pltpu.VMEM((GC, OFF * OFF), f32),
        ],
        scratch_shapes=[pltpu.VMEM((ROWS, devices * capacity, WIN), f32)],
        compiler_params=pltpu.CompilerParams(vmem_limit_bytes=VMEM_GRANT),
        name="average",
    )(near(codes))


def finish_kernel(turn, smooth, inner, outer, result):
    edge = smooth.shape[0] - GC
    result[...] = smooth[...]
    for row in range(ROWS):
        lanes = slice(row * WIN, (row + 1) * WIN)
        near, far = inner[:, lanes], outer[:, lanes]
        swap = turn[0] == 1
        result[:GC, lanes] = smooth[:GC, lanes] + jnp.where(swap, near, far) * 0.125
        result[edge:, lanes] = smooth[edge:, lanes] + jnp.where(swap, far, near) * 0.125


def finish(smooth, inner, outer, turn):
    return pl.pallas_call(
        finish_kernel,
        in_specs=[pl.BlockSpec(memory_space=pltpu.SMEM), resident(), resident(), resident()],
        out_shape=jax.ShapeDtypeStruct(smooth.shape, f32),
        compiler_params=pltpu.CompilerParams(vmem_limit_bytes=VMEM_GRANT),
        name="finish",
    )(jnp.full((1,), turn, jnp.int32), smooth, near(inner), near(outer))


def on_device(ref_chips, search_windows, dest_block, dest_slot):
    table = tables()
    chips = ref_chips[0]
    windows = search_windows[0]
    targets = dest_block[0, :, 0]
    slots = dest_slot[0]
    window_amount = windows.shape[0]
    chip_amount = chips.shape[0]
    tiles = lax.axis_size("tile")
    subs = lax.axis_size("sub")
    devices = tiles * subs
    capacity = max(2, 2 * window_amount // devices)

    images = windows.reshape(window_amount, WIN, WIN)
    sub = lax.axis_index("sub")
    sent = spread(chips, tiles).reshape(tiles, chip_amount * ROWS, WIN)
    gathered = lax.all_to_all(sent, "tile", split_axis=0, concat_axis=0, tiled=True)
    gathered = gathered.reshape(tiles * chip_amount, ROWS, WIN)
    spectra, scale = prepare_windows(images, table)
    sources = [gathered]
    for shift in range(1, subs):
        ring = [(i, (i - shift) % subs) for i in range(subs)]
        sources.append(lax.ppermute(gathered, "sub", ring))

    order = jnp.arange(window_amount, dtype=jnp.int32)
    matches = targets[:, None] == targets[None, :]
    earlier = order[:, None] > order[None, :]
    ranks = jnp.sum((matches & earlier).astype(jnp.int32), axis=1)
    choice = (targets % subs - sub) % subs
    place = (targets // subs) * chip_amount + slots
    position = jnp.full((1,), lax.axis_index(("tile", "sub")), jnp.int32)
    scalars = (choice, place, targets, ranks, slots, position)
    codes = score_windows(spectra, scale, sources, scalars, table, devices, capacity)

    received = lax.all_to_all(codes, ("tile", "sub"), split_axis=0, concat_axis=0, tiled=True)
    smooth, first, last = average_scores(received, capacity, chip_amount)
    if subs == 2:
        inner = lax.ppermute(jnp.where(sub == 0, last, first), "sub", [(0, 1), (1, 0)])
        ups = [(2 * i + 1, 2 * i + 2) for i in range(tiles - 1)]
        downs = [(2 * i + 2, 2 * i + 1) for i in range(tiles - 1)]
        outer = lax.ppermute(jnp.where(sub == 0, first, last), ("tile", "sub"), ups + downs)
        turn = sub
    else:
        inner = lax.ppermute(first, ("tile", "sub"), [(i + 1, i) for i in range(devices - 1)])
        outer = lax.ppermute(last, ("tile", "sub"), [(i, i + 1) for i in range(devices - 1)])
        turn = 0
    return finish(smooth, inner, outer, turn)[None]


def solution(mesh):
    return jax.shard_map(
        on_device,
        mesh=mesh,
        in_specs=(
            P(("groups", "pair"), ("tile", "sub"), None),
            P(("groups", "pair"), ("tile", "sub"), None),
            P(("groups", "pair"), ("tile", "sub"), None),
            P(("groups", "pair"), ("tile", "sub")),
        ),
        out_specs=P(("groups", "pair"), ("tile", "sub"), None),
        check_vma=False,
    )
```

```python
import functools

import jax
import jax.numpy as jnp
import ml_dtypes
import numpy as np
from jax import lax
from jax.experimental import pallas as pl
from jax.experimental.pallas import tpu as pltpu
from jax.sharding import PartitionSpec as P

CHIP = 64
WIN = 128
GC = 8
OFF = WIN - CHIP
PERIOD = WIN - 1
HALF = WIN // 2
ROWS = OFF * OFF // WIN
GROUP = 8
SCORE_GROUP = 16
VMEM_GRANT = 24 * 1024 * 1024
CODE = 32767.0
epsilon = 1e-06
f32 = jnp.float32
bf16 = jnp.bfloat16


def split_table(table):
    high = table.astype(ml_dtypes.bfloat16)
    low = (table - high.astype(np.float64)).astype(ml_dtypes.bfloat16)
    return (high, low)


def basis():
    freqs = np.arange(HALF)[:, None]
    places = np.arange(WIN)[None, :]
    angle = (freqs * places % PERIOD) * (2.0 * np.pi / PERIOD)
    used = (places < PERIOD).astype(np.float64)
    return (np.cos(angle) * used, np.sin(angle) * used)


def interleaved(table):
    return np.concatenate([table[0::2], table[1::2]], axis=0)


def twice(block):
    zero = np.zeros_like(block)
    return np.block([[block, zero], [zero, block]])


def tables():
    cosine, sine = basis()
    forward = np.concatenate([cosine, sine], axis=0)
    high, low = split_table(forward)
    starts = np.arange(OFF)[:, None]
    places = np.arange(WIN)[None, :]
    band = ((places >= starts) & (places < starts + CHIP)).astype(ml_dtypes.bfloat16)
    rows_band = interleaved(band)
    window_rows = np.concatenate([high, low, rows_band], axis=0)
    square_rows = np.concatenate([rows_band, rows_band], axis=1)
    window_lanes = np.concatenate([high.T, low.T], axis=1)
    window_lanes = np.concatenate([window_lanes, window_lanes], axis=0)
    band_lanes = twice(band.T)

    def pair_of(part):
        return np.concatenate([part[:, 0:CHIP:2], part[:, 1:CHIP:2]], axis=1)

    chip_rows = np.concatenate([pair_of(high), pair_of(high), pair_of(low)], axis=1)
    same = np.concatenate([cosine, cosine], axis=0)[:, :CHIP].T
    cross = np.concatenate([sine, -sine], axis=0)[:, :CHIP].T
    lane_high, lane_low = split_table(np.concatenate([same, cross], axis=1))
    none = np.zeros_like(lane_low)
    even_lanes = np.concatenate([lane_high, lane_high, lane_low, none], axis=0)
    odd_lanes = np.concatenate([none, lane_low, lane_high, lane_high], axis=0)
    chip_lanes = np.concatenate([even_lanes, odd_lanes], axis=1)
    weight = np.full((2 * HALF, 1), 2.0 / PERIOD)
    weight[0] = 1.0 / PERIOD
    inverse = (forward * weight)[:, :OFF].T
    inv_high, inv_low = split_table(inverse)
    rows_high, rows_low = interleaved(inv_high), interleaved(inv_low)
    inverse_rows = np.block([[rows_high, rows_high], [rows_low, rows_low]])
    inverse_lanes = np.concatenate([twice(inv_high.T), twice(inv_low.T)], axis=1)
    inverse_lanes = np.concatenate([inverse_lanes, inverse_lanes], axis=0)
    return dict(
        window_rows=window_rows, square_rows=square_rows, window_lanes=window_lanes,
        band_lanes=band_lanes, chip_rows=chip_rows, chip_lanes=chip_lanes,
        inverse_rows=inverse_rows, inverse_lanes=inverse_lanes,
    )


def dot(left, right):
    return jnp.dot(left, right, preferred_element_type=f32)


def halves(value):
    high = value.astype(bf16)
    low = (value - high.astype(f32)).astype(bf16)
    return (high, low)


def thirds(value):
    high = value.astype(bf16)
    rest = value - high.astype(f32)
    middle = rest.astype(bf16)
    low = (rest - middle.astype(f32)).astype(bf16)
    return (high, middle, low)


def window_kernel(windows, window_rows, square_rows, window_lanes, band_lanes, spectra, scale):
    group = windows.shape[0]
    for first in range(0, group, 2):
        image = jnp.concatenate([windows[first], windows[first + 1]], axis=1)
        rows = dot(window_rows[...], image)
        spec_rows = rows[:WIN] + rows[WIN:2 * WIN]
        sums = rows[2 * WIN:]
        wide = image.astype(f32)
        square_high, square_low = halves(wide * wide)
        squares = dot(square_rows[...], jnp.concatenate([square_high, square_low], axis=0))
        for part in range(2):
            lanes = slice(part * WIN, (part + 1) * WIN)
            high, low = halves(spec_rows[:, lanes])
            both = dot(jnp.concatenate([high, low], axis=1), window_lanes[...])
            spectra[first + part] = both[:, :WIN] + both[:, WIN:]
            pieces = []
            for source in (sums, squares):
                own = source[:, lanes]
                packed = jnp.concatenate([own[:ROWS], own[ROWS:]], axis=1)
                pieces.extend(thirds(packed))
            boxed = dot(jnp.concatenate(pieces, axis=0), band_lanes[...])
            boxes = [boxed[i * ROWS:(i + 1) * ROWS] for i in range(6)]
            mean = (boxes[0] + boxes[1] + boxes[2]) * (1.0 / (CHIP * CHIP))
            second = (boxes[3] + boxes[4] + boxes[5]) * (1.0 / (CHIP * CHIP))
            variance = second - mean * mean
            scale[first + part] = lax.rsqrt(variance + epsilon)


def score_kernel(
    capacity, choice, place, target, ranks, slots, position,
    spectra, scale, chip_lanes, chip_rows, inverse_rows, inverse_lanes, *rest,
):
    *sources, out, marks, lefts, lines, packs, pairs, products, backs = rest
    step = pl.program_id(0)
    group = lefts.shape[0] // ROWS
    base = step * group
    body = capacity * ROWS
    lane = lax.broadcasted_iota(jnp.int32, (8, WIN), 1)
    line = lax.broadcasted_iota(jnp.int32, (8, WIN), 0)

    @pl.when(step == 0)
    def _():
        marks[...] = jnp.zeros_like(marks)

    even = lax.broadcasted_iota(jnp.int32, (ROWS, WIN), 1) < CHIP
    raws = []
    for part in range(group):
        window = base + part
        raw = sources[0][place[window]]
        for index in range(1, len(sources)):
            raw = jnp.where(choice[window] == index, sources[index][place[window]], raw)
        raws.append(raw.astype(f32))
    total = jnp.concatenate([jnp.sum(raw, axis=0, keepdims=True) for raw in raws], axis=0)
    mean = jnp.sum(total, axis=1, keepdims=True) * (1.0 / (CHIP * CHIP))
    raws = [raws[part] - mean[part:part + 1] for part in range(group)]
    total = jnp.concatenate([jnp.sum(raw * raw, axis=0, keepdims=True) for raw in raws], axis=0)
    power = jnp.sum(total, axis=1, keepdims=True) * (1.0 / (CHIP * CHIP))
    gain = lax.rsqrt(power + epsilon) * (1.0 / CHIP)
    for part in range(group):
        own = slice(part * ROWS, (part + 1) * ROWS)
        high = raws[part].astype(bf16).astype(f32)
        low = raws[part] - high
        lefts[own, :WIN] = jnp.where(even, high, pltpu.roll(low, CHIP, 1)).astype(bf16)
        lefts[own, WIN:2 * WIN] = high.astype(bf16)
        lefts[own, 2 * WIN:] = jnp.where(even, pltpu.roll(high, CHIP, 1), low).astype(bf16)
    lines[:, :2 * WIN] = dot(lefts[:, :2 * WIN], chip_lanes[:, :2 * WIN])
    lines[:, 2 * WIN:] = dot(lefts[:, WIN:], chip_lanes[:, 2 * WIN:])

    def chip_spectrum(part):
        high, low = halves(lines[part * ROWS:(part + 1) * ROWS, :])
        pieces = [high[:, :2 * WIN], high[:, 2 * WIN:], low[:, :2 * WIN], low[:, 2 * WIN:]]
        pairs[part] = dot(chip_rows[...], jnp.concatenate(pieces + pieces[:2], axis=0))

    def multiply(part):
        lanes = slice(part % 2 * WIN, (part % 2 + 1) * WIN)
        for row in range(0, HALF, 32):
            upper, lower = slice(row, row + 32), slice(HALF + row, HALF + row + 32)
            own_c, own_s = spectra[part, upper], spectra[part, lower]
            turned_c, turned_s = pltpu.roll(own_c, HALF, 1), pltpu.roll(own_s, HALF, 1)
            same_c, same_s = pairs[part, upper, :WIN], pairs[part, lower, :WIN]
            cross_c, cross_s = pairs[part, upper, WIN:], pairs[part, lower, WIN:]
            out_c = same_c * own_c + cross_c * turned_c + same_s * own_s + cross_s * turned_s
            out_s = same_c * own_s + cross_c * turned_s - same_s * own_c - cross_s * turned_c
            for value, place_to in ((out_c, row), (out_s, HALF + row)):
                high, low = halves(value)
                products[part // 2, place_to:place_to + 32, lanes] = high
                products[part // 2, WIN + place_to:WIN + place_to + 32, lanes] = low

    def invert(pair):
        back = dot(inverse_rows[...], products[pair])
        backs[pair] = back[:OFF] + back[OFF:]

    def pack(pair):
        for part in (2 * pair, 2 * pair + 1):
            lanes = slice(part % 2 * WIN, (part % 2 + 1) * WIN)
            own = slice(part * ROWS, (part + 1) * ROWS)
            high, low = halves(backs[pair, :, lanes])
            packs[own, :WIN] = high[:ROWS]
            packs[own, WIN:2 * WIN] = high[ROWS:]
            packs[own, 2 * WIN:3 * WIN] = low[:ROWS]
            packs[own, 3 * WIN:] = low[ROWS:]

    def conclude(first):
        both = dot(packs[first * ROWS:(first + piece) * ROWS, :], inverse_lanes[...])
        scores = []
        for part in range(piece):
            own = slice(part * ROWS, (part + 1) * ROWS)
            numerator = both[own, :WIN] + both[own, WIN:]
            scores.append(numerator * (scale[first + part] * gain[first + part:first + part + 1]))
        largest = [jnp.max(jnp.abs(score), axis=0, keepdims=True) for score in scores]
        largest = jnp.max(jnp.concatenate(largest, axis=0), axis=1, keepdims=True)
        power = jnp.ceil(jnp.log2(jnp.maximum(largest, 1e-30)))
        shrink = jnp.exp2(-power).astype(bf16).astype(f32)
        for part in range(piece):
            window = base + first + part
            score = scores[part]
            size = jnp.maximum(jnp.abs(score) * shrink[part:part + 1], 1e-30)
            root = size * lax.rsqrt(size) * CODE
            root = jnp.minimum(root, CODE)
            code = jnp.round(jnp.where(score < 0, -root, root)).astype(jnp.int32).astype(jnp.int16)
            to = target[window]
            out[to, pl.ds(pl.multiple_of(ranks[window] * ROWS, ROWS), ROWS), :] = code
            here = lane == position[0] * capacity + ranks[window]
            named = (slots[window] + 1).astype(f32)
            mark = jnp.where(line == 0, named, jnp.where(line == 1, power[part:part + 1], 0.0))
            marks[to] = marks[to] + jnp.where(here, mark, 0.0)

    lag, piece = 6, min(4, group)
    for part in range(group + 2 * lag):
        if part < group:
            chip_spectrum(part)
        if lag <= part < group + lag:
            multiply(part - lag)
            if (part - lag) % 2 == 1:
                invert((part - lag) // 2)
        done = part - 2 * lag
        if done >= 0 and done % 2 == 1:
            pack(done // 2)
            if (done + 1) % piece == 0:
                conclude(done + 1 - piece)

    @pl.when(step == pl.num_programs(0) - 1)
    def _():
        for to in range(out.shape[0]):
            out[to, body:, :] = marks[to].astype(jnp.int32).astype(jnp.int16)


def average_kernel(capacity, chip_amount, codes, smooth, first, last, values):
    devices = codes.shape[0]
    body = capacity * ROWS
    slots = devices * capacity
    notes = codes[0, body:, :].astype(jnp.int32).astype(f32)
    for source in range(1, devices):
        notes = notes + codes[source, body:, :].astype(jnp.int32).astype(f32)
    for source in range(devices):
        wide = codes[source, :body, :].astype(jnp.int32).astype(f32)
        turned = jnp.swapaxes((wide * jnp.abs(wide)).reshape(capacity, ROWS, WIN), 0, 1)
        values[:, source * capacity:(source + 1) * capacity, :] = turned
    chip = lax.broadcasted_iota(jnp.int32, (chip_amount, WIN), 0)
    hit = (notes[0:1] - 1.0).astype(jnp.int32) == chip
    looks = jnp.sum(hit.astype(f32), axis=1, keepdims=True)
    weight = jnp.where(hit, jnp.exp2(notes[1:2]), 0.0).astype(bf16)[:, :slots]
    weight = jnp.concatenate([weight, weight], axis=1)
    factor = 1.0 / (jnp.maximum(looks, 1.0) * (CODE * CODE))
    factor = jnp.broadcast_to(factor, (chip_amount, WIN))
    column = chip % GC
    zero = jnp.zeros((GC, WIN), f32)
    for row in range(ROWS):
        high, low = halves(values[row])
        average = dot(weight, jnp.concatenate([high, low], axis=0)) * factor
        lanes = slice(row * WIN, (row + 1) * WIN)
        first[:, lanes] = average[:GC]
        last[:, lanes] = average[chip_amount - GC:]
        below = jnp.concatenate([average[GC:], zero], axis=0)
        above = jnp.concatenate([zero, average[:-GC]], axis=0)
        left = jnp.where(column == 0, 0.0, pltpu.roll(average, 1, 0))
        right = jnp.where(column == GC - 1, 0.0, pltpu.roll(average, chip_amount - 1, 0))
        smooth[:, lanes] = (4.0 * average + above + below + left + right) * 0.125


def resident():
    return pl.BlockSpec(memory_space=pltpu.VMEM)


def away(array):
    return pltpu.with_memory_space_constraint(array, pltpu.HBM)


def near(array):
    return pltpu.with_memory_space_constraint(array, pltpu.VMEM)


def spread_kernel(chips, sent):
    chip_amount = chips.shape[0]
    for first in range(0, chip_amount, 8):
        for row in range(0, ROWS, 8):
            lanes = [chips[first:first + 8, (row + i) * WIN:(row + i + 1) * WIN].astype(f32) for i in range(8)]
            turned = jnp.swapaxes(jnp.stack(lanes, axis=0), 0, 1).astype(bf16)
            for to in range(sent.shape[0]):
                sent[to, first:first + 8, row:row + 8, :] = turned


def spread(chips, tiles):
    return pl.pallas_call(
        spread_kernel,
        in_specs=[resident()],
        out_specs=resident(),
        out_shape=pltpu.VMEM((tiles, chips.shape[0], ROWS, WIN), bf16),
        compiler_params=pltpu.CompilerParams(vmem_limit_bytes=VMEM_GRANT),
        name="spread",
    )(chips)


def prepare_windows(images, table):
    amount = images.shape[0]
    group = min(GROUP, amount)
    constants = [jnp.asarray(table[k]) for k in ("window_rows", "square_rows", "window_lanes", "band_lanes")]
    return pl.pallas_call(
        window_kernel,
        grid=(amount // group,),
        in_specs=[pl.BlockSpec((group, WIN, WIN), lambda i: (i, 0, 0))] + [resident() for _ in constants],
        out_specs=[
            pl.BlockSpec((group, WIN, WIN), lambda i: (i, 0, 0)),
            pl.BlockSpec((group, ROWS, WIN), lambda i: (i, 0, 0)),
        ],
        out_shape=[
            pltpu.HBM((amount, WIN, WIN), f32),
            pltpu.HBM((amount, ROWS, WIN), f32),
        ],
        cost_estimate=pl.CostEstimate(
            flops=amount * 2 * 900 * 65536, transcendentals=amount * ROWS * WIN, bytes_accessed=amount * 120000
        ),
        compiler_params=pltpu.CompilerParams(vmem_limit_bytes=VMEM_GRANT),
        name="window_spectra",
    )(images, *constants)


def score_windows(spectra, scale, sources, scalars, table, devices, capacity):
    amount = spectra.shape[0]
    group = min(SCORE_GROUP, amount)
    constants = [jnp.asarray(table[k]) for k in ("chip_lanes", "chip_rows", "inverse_rows", "inverse_lanes")]
    shape = (devices, capacity * ROWS + 8, WIN)
    return pl.pallas_call(
        functools.partial(score_kernel, capacity),
        grid_spec=pltpu.PrefetchScalarGridSpec(
            num_scalar_prefetch=len(scalars),
            grid=(amount // group,),
            in_specs=[
                pl.BlockSpec((group, WIN, WIN), lambda i, *_: (i, 0, 0)),
                pl.BlockSpec((group, ROWS, WIN), lambda i, *_: (i, 0, 0)),
            ] + [resident() for _ in constants] + [resident() for _ in sources],
            out_specs=resident(),
            scratch_shapes=[
                pltpu.VMEM((devices, 8, WIN), f32),
                pltpu.VMEM((group * ROWS, 3 * WIN), bf16),
                pltpu.VMEM((group * ROWS, 4 * WIN), f32),
                pltpu.VMEM((group * ROWS, 4 * WIN), bf16),
                pltpu.VMEM((group, WIN, 2 * WIN), f32),
                pltpu.VMEM((group // 2, 2 * WIN, 2 * WIN), bf16),
                pltpu.VMEM((group // 2, OFF, 2 * WIN), f32),
            ],
        ),
        out_shape=pltpu.VMEM(shape, jnp.int16),
        compiler_params=pltpu.CompilerParams(vmem_limit_bytes=VMEM_GRANT),
        name="scores",
    )(*scalars, away(spectra), away(scale), *[near(c) for c in constants], *[near(source) for source in sources])


def average_scores(codes, capacity, chip_amount):
    devices = codes.shape[0]
    return pl.pallas_call(
        functools.partial(average_kernel, capacity, chip_amount),
        in_specs=[resident()],
        out_specs=[resident(), resident(), resident()],
        out_shape=[
            pltpu.VMEM((chip_amount, OFF * OFF), f32),
            pltpu.VMEM((GC, OFF * OFF), f32),
            pltpu.VMEM((GC, OFF * OFF), f32),
        ],
        scratch_shapes=[pltpu.VMEM((ROWS, devices * capacity, WIN), f32)],
        compiler_params=pltpu.CompilerParams(vmem_limit_bytes=VMEM_GRANT),
        name="average",
    )(near(codes))


def finish_kernel(turn, smooth, inner, outer, result):
    edge = smooth.shape[0] - GC
    result[...] = smooth[...]
    for row in range(ROWS):
        lanes = slice(row * WIN, (row + 1) * WIN)
        near, far = inner[:, lanes], outer[:, lanes]
        swap = turn[0] == 1
        result[:GC, lanes] = smooth[:GC, lanes] + jnp.where(swap, near, far) * 0.125
        result[edge:, lanes] = smooth[edge:, lanes] + jnp.where(swap, far, near) * 0.125


def finish(smooth, inner, outer, turn):
    return pl.pallas_call(
        finish_kernel,
        in_specs=[pl.BlockSpec(memory_space=pltpu.SMEM), resident(), resident(), resident()],
        out_shape=jax.ShapeDtypeStruct(smooth.shape, f32),
        compiler_params=pltpu.CompilerParams(vmem_limit_bytes=VMEM_GRANT),
        name="finish",
    )(jnp.full((1,), turn, jnp.int32), smooth, near(inner), near(outer))


def on_device(ref_chips, search_windows, dest_block, dest_slot):
    table = tables()
    chips = ref_chips[0]
    windows = search_windows[0]
    targets = dest_block[0, :, 0]
    slots = dest_slot[0]
    window_amount = windows.shape[0]
    chip_amount = chips.shape[0]
    tiles = lax.axis_size("tile")
    subs = lax.axis_size("sub")
    devices = tiles * subs
    capacity = max(2, 2 * window_amount // devices)

    images = windows.reshape(window_amount, WIN, WIN)
    sub = lax.axis_index("sub")
    sent = spread(chips, tiles).reshape(tiles, chip_amount * ROWS, WIN)
    gathered = lax.all_to_all(sent, "tile", split_axis=0, concat_axis=0, tiled=True)
    gathered = gathered.reshape(tiles * chip_amount, ROWS, WIN)
    spectra, scale = prepare_windows(images, table)
    sources = [gathered]
    for shift in range(1, subs):
        ring = [(i, (i - shift) % subs) for i in range(subs)]
        sources.append(lax.ppermute(gathered, "sub", ring))

    order = jnp.arange(window_amount, dtype=jnp.int32)
    matches = targets[:, None] == targets[None, :]
    earlier = order[:, None] > order[None, :]
    ranks = jnp.sum((matches & earlier).astype(jnp.int32), axis=1)
    choice = (targets % subs - sub) % subs
    place = (targets // subs) * chip_amount + slots
    position = jnp.full((1,), lax.axis_index(("tile", "sub")), jnp.int32)
    scalars = (choice, place, targets, ranks, slots, position)
    codes = score_windows(spectra, scale, sources, scalars, table, devices, capacity)

    received = lax.all_to_all(codes, ("tile", "sub"), split_axis=0, concat_axis=0, tiled=True)
    smooth, first, last = average_scores(received, capacity, chip_amount)
    if subs == 2:
        inner = lax.ppermute(jnp.where(sub == 0, last, first), "sub", [(0, 1), (1, 0)])
        ups = [(2 * i + 1, 2 * i + 2) for i in range(tiles - 1)]
        downs = [(2 * i + 2, 2 * i + 1) for i in range(tiles - 1)]
        outer = lax.ppermute(jnp.where(sub == 0, first, last), ("tile", "sub"), ups + downs)
        turn = sub
    else:
        inner = lax.ppermute(first, ("tile", "sub"), [(i + 1, i) for i in range(devices - 1)])
        outer = lax.ppermute(last, ("tile", "sub"), [(i, i + 1) for i in range(devices - 1)])
        turn = 0
    return finish(smooth, inner, outer, turn)[None]


def solution(mesh):
    return jax.shard_map(
        on_device,
        mesh=mesh,
        in_specs=(
            P(("groups", "pair"), ("tile", "sub"), None),
            P(("groups", "pair"), ("tile", "sub"), None),
            P(("groups", "pair"), ("tile", "sub"), None),
            P(("groups", "pair"), ("tile", "sub")),
        ),
        out_specs=P(("groups", "pair"), ("tile", "sub"), None),
        check_vma=False,
    )
```
